32 devices in a mesh: dp: 8 (over z, x), mp: 4 (over y, core).
Axes of the slice: x: 2, y: 2, z: 4, core: 2. Of those that a mesh axis runs over, the one named last changes fastest.
Arguments:
- inputs: float32 [8, 1024, 768], P('dp', None, 'mp'), may hold values from -6 to 6
- lengths: int32 [8], P('dp'), may hold values from 64 to 1024, as said below
- ln1_gain: float32 [768], P('mp'), may hold values from 0.5 to 1.5
- ln1_bias: float32 [768], P('mp'), may hold values from -3 to 3
- w_query: float32 [768, 768], P(None, 'mp'), may hold values from -0.21875 to 0.21875
- w_key: float32 [768, 768], P(None, 'mp'), may hold values from -0.21875 to 0.21875
- w_value: float32 [768, 768], P(None, 'mp'), may hold values from -0.21875 to 0.21875
- query_bias: float32 [768], P('mp'), may hold values from -3 to 3
- value_bias: float32 [768], P('mp'), may hold values from -3 to 3
- pair_bias: float32 [1024, 256], replicated, may hold values from -3 to 3
- w_out: float32 [768, 768], P('mp'), may hold values from -0.875 to 0.875
- out_bias: float32 [768], P('mp'), may hold values from -3 to 3
- ln2_gain: float32 [768], P('mp'), may hold values from 0.5 to 1.5
- ln2_bias: float32 [768], P('mp'), may hold values from -3 to 3
- w_up: float32 [768, 3072], P(None, 'mp'), may hold values from -0.21875 to 0.21875
- up_bias: float32 [3072], P('mp'), may hold values from -3 to 3
- w_down: float32 [3072, 768], P('mp'), may hold values from -0.109375 to 0.109375
- down_bias: float32 [768], P('mp'), may hold values from -3 to 3
- cotangent: float32 [8, 1024, 768], P('dp', None, 'mp'), may hold values from -6 to 6
Outputs:
- result: float32 [8, 1024, 768], P('dp', None, 'mp')
- d_inputs: float32 [8, 1024, 768], P('dp', None, 'mp')
- d_ln1_gain: float32 [768], P('mp')
- d_ln1_bias: float32 [768], P('mp')
- d_w_query: float32 [768, 768], P(None, 'mp')
- d_w_key: float32 [768, 768], P(None, 'mp')
- d_w_value: float32 [768, 768], P(None, 'mp')
- d_query_bias: float32 [768], P('mp')
- d_value_bias: float32 [768], P('mp')
- d_pair_bias: float32 [1024, 256], replicated
- d_w_out: float32 [768, 768], P('mp')
- d_out_bias: float32 [768], P('mp')
- d_ln2_gain: float32 [768], P('mp')
- d_ln2_bias: float32 [768], P('mp')
- d_w_up: float32 [768, 3072], P(None, 'mp')
- d_up_bias: float32 [3072], P('mp')
- d_w_down: float32 [3072, 768], P('mp')
- d_down_bias: float32 [768], P('mp')
The draws below stay inside these ranges and needn't reach their ends.
Inputs may be any that keep to these rules, and one draw needn't show every extreme that they name: `lengths`: some row of every draw has exactly 1024 live positions.
All inputs are finite; a program needn't handle non-finite values.
Results may differ from the reference program's by a relative error of at most 0.0003.
Values sent between devices are 32-bit elements; how exact they have to be, the bound alone decides.
No kernel may reach another device: no remote copies, remote signals or barrier semaphores. Data moves between devices by JAX's collectives and lax.ppermute only.
A program may use at most 192 MiB of HBM per device.

```python
import math
import jax
import jax.numpy as jnp
from jax import lax

D = 768
FF = 3072
WIN = 256
LPAD = 1024
LMIN = 64
SEQS = 8


def draw_lengths(key, part):
    base_lengths = jax.random.randint(key, (SEQS,), LMIN, LPAD + 1)
    full_row = jax.random.randint(jax.random.fold_in(key, 7), (), 0, SEQS)
    positions = jnp.arange(SEQS, dtype=jnp.int32)
    return jnp.where(positions == full_row, LPAD, base_lengths).astype(jnp.int32)


def steps_of(stream_key, dims, shards, low, top_value):
    level, own = 1.0, jax.random.fold_in(stream_key, 6)
    for axis_at, shards_of in shards:
        draws = jnp.exp(jax.random.uniform(jax.random.fold_in(own, axis_at), (shards_of,), jnp.float32, low / len(shards), top_value / len(shards)))
        level = level * jnp.repeat(draws, dims[axis_at] // shards_of).reshape([-1 if axis == axis_at else 1 for axis in range(len(dims))])
    return level


def scatter_about(own_key, shape, deviation, most, split=(), kind=jnp.bfloat16):
    level = steps_of(own_key, shape, split, -0.22, 0.18) if split else 1.0
    result = jax.random.normal(own_key, shape, jnp.float32) * deviation * level
    return jnp.minimum(jnp.maximum(result, -most), most).astype(kind)


def setup_inputs(seed: int = 0) -> dict:
    key_of = jax.random.split(jax.random.key(seed), 20)
    return {
        "inputs": scatter_about(key_of[0], (SEQS, LPAD, D), 1.0, 6.0, ((0, 8), (2, 4)), jnp.float32),
        "lengths": draw_lengths(jax.random.fold_in(key_of[19], 71), 0),
        "ln1_gain": jnp.clip(1.0 + 0.1 * jax.random.normal(key_of[2], (D,), jnp.float32), 0.5, 1.5),
        "ln1_bias": scatter_about(key_of[3], (D,), 0.3, 3.0, ((0, 4),), jnp.float32),
        "w_query": scatter_about(key_of[4], (D, D), D ** -0.5, 0.21875, ((1, 4),), jnp.float32),
        "w_key": scatter_about(key_of[5], (D, D), D ** -0.5, 0.21875, ((1, 4),), jnp.float32),
        "w_value": scatter_about(key_of[6], (D, D), D ** -0.5, 0.21875, ((1, 4),), jnp.float32),
        "query_bias": scatter_about(key_of[7], (D,), 0.5, 3.0, ((0, 4),), jnp.float32),
        "value_bias": scatter_about(key_of[8], (D,), 0.5, 3.0, ((0, 4),), jnp.float32),
        "pair_bias": scatter_about(key_of[9], (LPAD, WIN), 1.0, 3.0, (), jnp.float32),
        "w_out": scatter_about(key_of[10], (D, D), (D // 16) ** -0.5, 0.875, ((0, 4),), jnp.float32),
        "out_bias": scatter_about(key_of[11], (D,), 0.3, 3.0, ((0, 4),), jnp.float32),
        "ln2_gain": jnp.clip(1.0 + 0.1 * jax.random.normal(key_of[12], (D,), jnp.float32), 0.5, 1.5),
        "ln2_bias": scatter_about(key_of[13], (D,), 0.3, 3.0, ((0, 4),), jnp.float32),
        "w_up": scatter_about(key_of[14], (D, FF), D ** -0.5, 0.21875, ((1, 4),), jnp.float32),
        "up_bias": scatter_about(key_of[15], (FF,), 0.3, 3.0, ((0, 4),), jnp.float32),
        "w_down": scatter_about(key_of[16], (FF, D), FF ** -0.5, 0.109375, ((0, 4),), jnp.float32),
        "down_bias": scatter_about(key_of[17], (D,), 0.3, 3.0, ((0, 4),), jnp.float32),
        "cotangent": scatter_about(key_of[18], (SEQS, LPAD, D), 1.0, 6.0, ((0, 8), (2, 4)), jnp.float32),
    }


EXACT_MODE = lax.Precision.HIGHEST
EPSILON = 1e-05

@jax.custom_vjp
def low(v):
    return lax.optimization_barrier(v.astype(jnp.bfloat16)).astype(jnp.float32)

@jax.custom_vjp
def low_back(v):
    return v

def low_keep(v):
    return (low(v), None)

def low_pass(kept, grad):
    return (grad,)

def back_keep(v):
    return (v, None)

def back_low(kept, grad):
    return (low(grad),)
low.defvjp(low_keep, low_pass)
low_back.defvjp(back_keep, back_low)

def layer_norm(values_in, gain_vec, bias_vec):
    row_mean = lax.optimization_barrier(jnp.mean(values_in, axis=-1, keepdims=True))
    row_var = lax.optimization_barrier(jnp.mean(values_in * values_in, axis=-1, keepdims=True)) - row_mean * row_mean
    return (values_in - row_mean) * lax.rsqrt(row_var + EPSILON) * gain_vec + bias_vec

def mixing_weights(pair_bias):
    positions = jnp.arange(LPAD, dtype=jnp.int32)
    offset = positions[:, None] - positions[None, :]
    band_index = jnp.clip(offset, 0, WIN - 1).astype(jnp.int32)
    band_bias = jnp.take_along_axis(pair_bias, band_index, axis=1)
    inside = jnp.where(offset < WIN, jnp.exp(band_bias), jnp.ones_like(band_bias))
    return jnp.where(offset < 0, jnp.zeros_like(band_bias), inside)

def forward(params, x_group, len_group):
    ln1_gain, ln1_bias, w_query, w_key, w_value, query_bias, value_bias, pair_bias, w_out, out_bias, ln2_gain, ln2_bias, w_up, up_bias, w_down, down_bias = params
    live_mask = (jnp.arange(LPAD, dtype=jnp.int32)[None, :] < len_group[:, None]).astype(jnp.float32)[..., None]
    normed1 = layer_norm(x_group, ln1_gain, ln1_bias)
    queries = jnp.einsum('std,de->ste', normed1, w_query, precision=EXACT_MODE) + query_bias
    key_proj = jnp.einsum('std,de->ste', normed1, w_key, precision=EXACT_MODE)
    value_proj = jnp.einsum('std,de->ste', normed1, w_value, precision=EXACT_MODE) + value_bias
    weights = mixing_weights(pair_bias)
    exp_keys = jnp.exp(key_proj)
    numerator = jnp.einsum('tu,suc->stc', weights, exp_keys * value_proj, precision=EXACT_MODE)
    denominator = jnp.einsum('tu,suc->stc', weights, exp_keys, precision=EXACT_MODE)
    mixed = jax.nn.sigmoid(queries) * numerator / denominator
    inner = x_group + live_mask * (jnp.einsum('stc,cd->std', mixed, w_out, precision=EXACT_MODE) + out_bias)
    normed2 = layer_norm(inner, ln2_gain, ln2_bias)
    hidden_act = jax.nn.gelu(jnp.einsum('std,df->stf', normed2, w_up, precision=EXACT_MODE) + up_bias, approximate=True)
    return inner + live_mask * (jnp.einsum('stf,fd->std', hidden_act, w_down, precision=EXACT_MODE) + down_bias)

def reference(inputs, lengths, ln1_gain, ln1_bias, w_query, w_key, w_value, query_bias, value_bias, pair_bias, w_out, out_bias, ln2_gain, ln2_bias, w_up, up_bias, w_down, down_bias, cotangent):
    params = (ln1_gain, ln1_bias, w_query, w_key, w_value, query_bias, value_bias, pair_bias, w_out, out_bias, ln2_gain, ln2_bias, w_up, up_bias, w_down, down_bias)
    params = tuple((item.astype(jnp.float32) for item in params))
    group_size = math.gcd(SEQS, 4)
    group_count = SEQS // group_size

    def group_step(grad_total, pieces):
        x_group, len_group, cot_group = pieces

        def apply_block(param_set, x_values):
            return forward(param_set, x_values, len_group)
        outputs, pullback = jax.vjp(apply_block, params, x_group)
        grad_params, grad_inputs = pullback(cot_group)
        return (jax.tree.map(jnp.add, grad_total, grad_params), (outputs, grad_inputs))
    zero_grads = jax.tree.map(jnp.zeros_like, params)
    grad_total, (results, input_grads) = lax.scan(group_step, zero_grads, (inputs.astype(jnp.float32).reshape(group_count, group_size, LPAD, D), lengths.reshape(group_count, group_size).astype(jnp.int32), cotangent.astype(jnp.float32).reshape(group_count, group_size, LPAD, D)))
    return (results.reshape(SEQS, LPAD, D), input_grads.reshape(SEQS, LPAD, D), grad_total[0], grad_total[1], grad_total[2], grad_total[3], grad_total[4], grad_total[5], grad_total[6], grad_total[7], grad_total[8], grad_total[9], grad_total[10], grad_total[11], grad_total[12], grad_total[13], grad_total[14], grad_total[15])
```

```python
import jax
import jax.numpy as jnp
from jax import lax
from jax.sharding import PartitionSpec as P

MODE = lax.Precision.HIGH
EPSILON = 1e-05


def dot_nn(left_arr, right_arr):
    return lax.dot_general(
        left_arr, right_arr, (((1,), (0,)), ((), ())), precision=MODE, preferred_element_type=jnp.float32
    )


def dot_nt(left_arr, right_arr):
    return lax.dot_general(
        left_arr, right_arr, (((1,), (1,)), ((), ())), precision=MODE, preferred_element_type=jnp.float32
    )


def dot_tn(left_arr, right_arr):
    return lax.dot_general(
        left_arr, right_arr, (((0,), (0,)), ((), ())), precision=MODE, preferred_element_type=jnp.float32
    )


def swap(block, bit):
    return lax.ppermute(block, "mp", [(i, i ^ bit) for i in range(4)])


def gather_rows(own):
    rows, width = own.shape
    place = lax.axis_index("mp")
    far = swap(own, 2)
    near = swap(own, 1)
    far_near = swap(far, 1)
    whole = jnp.zeros((4 * rows, width), own.dtype)
    for flip, part in enumerate((own, near, far, far_near)):
        whole = lax.dynamic_update_slice(whole, part, ((place ^ flip) * rows, 0))
    return whole


def halve(grid, axis, bit):
    mine = lax.dynamic_index_in_dim(grid, bit, axis, keepdims=False)
    other = lax.dynamic_index_in_dim(grid, 1 - bit, axis, keepdims=False)
    return mine, other


def reduce_core(terms):
    rows, width = terms.shape[0] // 4, terms.shape[1]
    place = lax.axis_index("mp")
    mine, other = halve(terms.reshape(2, 2, rows, width), 1, place & 1)
    return mine + swap(other, 1)


def scatter_sum(terms):
    place = lax.axis_index("mp")
    mine, other = halve(reduce_core(terms), 0, place >> 1)
    return mine + swap(other, 2)


def whole_sum(terms):
    place = lax.axis_index("mp")
    half = reduce_core(terms)
    half = half + swap(half, 2)
    other = swap(half, 1)
    odd = (place & 1) == 1
    both = jnp.stack([jnp.where(odd, other, half), jnp.where(odd, half, other)], axis=1)
    return both.reshape(terms.shape)


def column_norm(values_in):
    mean = jnp.mean(values_in, axis=0, keepdims=True)
    var = jnp.mean(values_in * values_in, axis=0, keepdims=True) - mean * mean
    scale = lax.rsqrt(var + EPSILON)
    return (values_in - mean) * scale, scale


def band_blocks(pair_exp):
    span, window = pair_exp.shape
    count = span // window
    flipped = pair_exp.reshape(count, window, window)[:, :, ::-1]
    wide = jnp.pad(flipped, ((0, 0), (0, 0), (1, window)))
    skewed = wide.reshape(count, -1)[:, : window * 2 * window].reshape(count, window, 2 * window)
    query = jnp.arange(window, dtype=jnp.int32)[:, None]
    key = jnp.arange(2 * window, dtype=jnp.int32)[None, :]
    return skewed + (key <= query).astype(jnp.float32)[None]


def band_values(grid):
    window, wide = grid.shape
    flat = jnp.pad(grid.reshape(-1), (0, window))
    return flat.reshape(window, wide + 1)[:, 1 : window + 1][:, ::-1]


def body(
    inputs,
    lengths,
    ln1_gain,
    ln1_bias,
    w_query,
    w_key,
    w_value,
    query_bias,
    value_bias,
    pair_bias,
    w_out,
    out_bias,
    ln2_gain,
    ln2_bias,
    w_up,
    up_bias,
    w_down,
    down_bias,
    cotangent,
):
    seq_rows, span, chans = inputs.shape
    assert seq_rows == 1
    window = pair_bias.shape[1]
    count = span // window
    model = 4 * chans
    place = lax.axis_index("mp")
    live = (jnp.arange(span, dtype=jnp.int32) < lengths[0]).astype(jnp.float32)[None, :]

    def own_rows(whole):
        return lax.dynamic_slice_in_dim(whole, place * chans, chans, 0)

    x_own = inputs[0].T
    cot_own = cotangent[0].T
    vectors = jnp.stack([ln1_gain, ln1_bias, out_bias, ln2_gain, ln2_bias], axis=1)
    vectors = jnp.pad(vectors, ((0, 0), (0, 128 - vectors.shape[1])))
    gathered = gather_rows(jnp.concatenate([x_own, vectors], axis=1))
    whole_x = gathered[:, :span]
    gain_one, bias_one, bias_out, gain_two, bias_two = (
        gathered[:, span + i : span + i + 1] for i in range(5)
    )
    pair_exp = jnp.exp(pair_bias)
    bands = band_blocks(pair_exp)

    normal_one, scale_one = column_norm(whole_x)
    normed1 = normal_one * gain_one + bias_one
    w_qkv = jnp.concatenate([w_query.T, w_key.T, w_value.T], axis=0)
    projected = dot_nn(w_qkv, normed1)
    queries = projected[:chans] + query_bias[:, None]
    exp_keys = jnp.exp(projected[chans : 2 * chans])
    values = projected[2 * chans :] + value_bias[:, None]
    pair = jnp.concatenate([exp_keys * values, exp_keys], axis=0)
    sums = []
    far = jnp.zeros((2 * chans, 1), jnp.float32)
    for i in range(count):
        here = slice(i * window, (i + 1) * window)
        if i == 0:
            sums.append(dot_nt(pair[:, here], bands[i, :, window:]))
        else:
            near = pair[:, (i - 1) * window : (i + 1) * window]
            sums.append(dot_nt(near, bands[i]) + far)
            far = far + jnp.sum(pair[:, (i - 1) * window : i * window], axis=1, keepdims=True)
    sums = jnp.concatenate(sums, axis=1)
    denominator = sums[chans:]
    quotient = sums[:chans] / denominator
    gate_open = jax.nn.sigmoid(queries)
    mixed = gate_open * quotient

    w_out_whole = gather_rows(w_out)
    whole_cot = gather_rows(cot_own)
    mixed_whole = gather_rows(mixed)
    inner = whole_x + live * (dot_tn(w_out_whole, mixed_whole) + bias_out)
    normal_two, scale_two = column_norm(inner)
    normed2 = normal_two * gain_two + bias_two
    hidden_pre = dot_tn(w_up, normed2) + up_bias[:, None]
    hidden_act, gate_pull = jax.vjp(lambda v: jax.nn.gelu(v, approximate=True), hidden_pre)
    branch_two = live * whole_cot
    d_w_down = dot_nt(hidden_act, branch_two)
    (d_pre,) = gate_pull(dot_nn(w_down, branch_two))
    d_w_up = dot_nt(normed2, d_pre)
    d_up_bias = jnp.sum(d_pre, axis=1)
    d_down_bias = jnp.sum(live * cot_own, axis=1)
    d_normed2 = whole_sum(dot_nn(w_up, d_pre))
    ffn_grads = lax.psum((d_w_down, d_w_up), "dp")
    down_own = scatter_sum(dot_tn(w_down, hidden_act))
    result = own_rows(inner) + live * (down_own + down_bias[:, None])

    scaled_two = d_normed2 * gain_two
    d_inner = whole_cot + scale_two * (
        scaled_two
        - jnp.mean(scaled_two, axis=0, keepdims=True)
        - normal_two * jnp.mean(scaled_two * normal_two, axis=0, keepdims=True)
    )
    d_gain_two = jnp.sum(own_rows(d_normed2) * own_rows(normal_two), axis=1)
    d_bias_two = jnp.sum(own_rows(d_normed2), axis=1)
    branch_one = live * d_inner
    d_out_bias = jnp.sum(own_rows(branch_one), axis=1)
    d_w_out = dot_nt(mixed, branch_one)
    d_mixed = dot_nn(w_out, branch_one)

    d_queries = d_mixed * quotient * gate_open * (1.0 - gate_open)
    d_numer = d_mixed * gate_open / denominator
    d_pairs = jnp.concatenate([d_numer, -d_numer * quotient], axis=0)
    back = [None] * count
    d_bands = [None] * count
    later = jnp.zeros((2 * chans, 1), jnp.float32)
    for i in reversed(range(count)):
        here = slice(i * window, (i + 1) * window)
        before = slice(max(i - 1, 0) * window, (i + 1) * window)
        band = bands[i] if i else bands[i, :, window:]
        into = dot_nn(d_pairs[:, here], band)
        grid = dot_tn(d_pairs[:, here], pair[:, before])
        if i == 0:
            grid = jnp.pad(grid, ((0, 0), (window, 0)))
        d_bands[i] = band_values(grid)
        own_part = into[:, -window:] + later
        back[i] = own_part if back[i] is None else back[i] + own_part
        if i:
            back[i - 1] = into[:, :window]
            if i + 1 < count:
                ahead = slice((i + 1) * window, (i + 2) * window)
                later = later + jnp.sum(d_pairs[:, ahead], axis=1, keepdims=True)
    back = jnp.concatenate(back, axis=1)
    d_pair_bias = jnp.concatenate(d_bands, axis=0) * pair_exp
    d_values = exp_keys * back[:chans]
    d_keys = exp_keys * (values * back[:chans] + back[chans:])
    d_qkv = jnp.concatenate([d_queries, d_keys, d_values], axis=0)
    d_w_qkv = dot_nt(d_qkv, normed1)
    terms = dot_tn(w_qkv, d_qkv)
    scaled_terms = terms * gain_one
    stats = jnp.concatenate(
        [
            jnp.sum(scaled_terms, axis=0, keepdims=True),
            jnp.sum(scaled_terms * normal_one, axis=0, keepdims=True),
        ],
        axis=0,
    )
    stats = jnp.pad(stats, ((0, 6), (0, 0)))
    stats = stats + swap(stats, 1)
    stats = (stats + swap(stats, 2)) / model
    d_normed1 = scatter_sum(terms)
    normal_own = own_rows(normal_one)
    d_gain_one = jnp.sum(d_normed1 * normal_own, axis=1)
    d_bias_one = jnp.sum(d_normed1, axis=1)
    d_inputs = own_rows(d_inner) + scale_one * (
        d_normed1 * own_rows(gain_one) - stats[0:1] - normal_own * stats[1:2]
    )
    small = jnp.concatenate(
        [
            d_gain_one,
            d_bias_one,
            jnp.sum(d_queries, axis=1),
            jnp.sum(d_values, axis=1),
            d_out_bias,
            d_gain_two,
            d_bias_two,
            d_down_bias,
            d_up_bias,
        ]
    )
    d_w_qkv, d_w_out, small = lax.psum((d_w_qkv, d_w_out, small), "dp")
    d_pair_bias = lax.psum(d_pair_bias, ("dp", "mp"))
    vecs = [small[i * chans : (i + 1) * chans] for i in range(8)]
    return (
        result.T[None],
        d_inputs.T[None],
        vecs[0],
        vecs[1],
        d_w_qkv[:chans].T,
        d_w_qkv[chans : 2 * chans].T,
        d_w_qkv[2 * chans :].T,
        vecs[2],
        vecs[3],
        d_pair_bias,
        d_w_out,
        vecs[4],
        vecs[5],
        vecs[6],
        ffn_grads[1],
        small[8 * chans :],
        ffn_grads[0],
        vecs[7],
    )


def solution(mesh):
    rows = P("dp", None, "mp")
    vec = P("mp")
    out_dim = P(None, "mp")
    in_dim = P("mp", None)
    return jax.shard_map(
        body,
        mesh=mesh,
        in_specs=(
            rows, P("dp"), vec, vec, out_dim, out_dim, out_dim, vec, vec, P(), in_dim, vec, vec, vec,
            out_dim, vec, in_dim, vec, rows,
        ),
        out_specs=(
            rows, rows, vec, vec, out_dim, out_dim, out_dim, vec, vec, P(), in_dim, vec, vec, vec,
            out_dim, vec, in_dim, vec,
        ),
        check_vma=False,
    )
```

```python
import math
from functools import partial

import jax
import jax.numpy as jnp
from jax import lax
from jax.experimental import pallas as pl
from jax.experimental.pallas import tpu as pltpu
from jax.sharding import PartitionSpec as P

EPSILON = 1e-05
TB = 256
WIDE = 512
NN = (((1,), (0,)), ((), ()))
NT = (((1,), (1,)), ((), ()))
F32 = jnp.float32
BF16 = jnp.bfloat16


def split(wide):
    high = wide.astype(BF16)
    return high, (wide - high.astype(F32)).astype(BF16)


def dot3(left, right, dims):
    def one(a, b):
        return lax.dot_general(a, b, dims, preferred_element_type=F32)

    return one(left[0], right[0]) + (one(left[0], right[1]) + one(left[1], right[0]))


def put(high_ref, low_ref, wide):
    high, low = split(wide)
    high_ref[...] = high
    low_ref[...] = low


def get(high_ref, low_ref):
    return high_ref[...], low_ref[...]


def reverse_lanes(wide):
    size = wide.shape[1]
    row = lax.broadcasted_iota(jnp.int32, (size, size), 0)
    col = lax.broadcasted_iota(jnp.int32, (size, size), 1)
    turn = (row + col == size - 1).astype(F32).astype(BF16)
    high, rest = split(wide)
    middle = wide - high.astype(F32)
    low = (middle - rest.astype(F32)).astype(BF16)

    def one(part):
        return lax.dot_general(part, turn, NN, preferred_element_type=F32)

    return one(high) + (one(rest) + one(low))


def live_row(length, start, width):
    return (lax.broadcasted_iota(jnp.int32, (1, width), 1) + start < length).astype(F32)


def whole(shape):
    return pl.BlockSpec(shape, lambda i: (0,) * len(shape))


def across(rows, width=WIDE):
    return pl.BlockSpec((rows, width), lambda i: (0, i))


SCALARS = pl.BlockSpec(memory_space=pltpu.SMEM)


def shaped(shape, dtype=F32):
    return jax.ShapeDtypeStruct(shape, dtype)


def call(kernel, grid, ins, outs, scratch=(), name=None, flops=0):
    held = sum(2 * math.prod(spec.block_shape) * array.dtype.itemsize for array, spec in ins if spec.block_shape)
    held += sum(2 * math.prod(spec.block_shape) * shape.dtype.itemsize for shape, spec in outs)
    held += sum(math.prod(ref.shape) * jnp.dtype(ref.dtype).itemsize for ref in scratch)
    moved = sum(array.size * array.dtype.itemsize for array, _ in ins)
    moved += sum(math.prod(shape.shape) * shape.dtype.itemsize for shape, _ in outs)
    run = pl.pallas_call(
        kernel,
        grid=(grid,),
        in_specs=[spec for _, spec in ins],
        out_specs=[spec for _, spec in outs],
        out_shape=[shape for shape, _ in outs],
        scratch_shapes=list(scratch),
        compiler_params=pltpu.CompilerParams(
            dimension_semantics=("arbitrary",), vmem_limit_bytes=min(held + 16 * 2**20, 58 * 2**20)
        ),
        cost_estimate=pl.CostEstimate(flops=int(flops), transcendentals=0, bytes_accessed=moved),
        name=name,
    )
    return run(*[array for array, _ in ins])


def place_rows(target, place, parts):
    for flip, part in enumerate(parts):
        rows = part.shape[0]
        target[pl.ds(pl.multiple_of((place ^ flip) * rows, rows), rows), :] = part[...]


def take_rows(source, index, rows):
    return source[pl.ds(pl.multiple_of(index * rows, rows), rows), :]


def fold(wide):
    total = wide[:, :128]
    for at in range(128, wide.shape[1], 128):
        total = total + wide[:, at : at + 128]
    return total


def band_kernel(bias, high, low):
    window = bias.shape[1]
    turned = reverse_lanes(jnp.exp(bias[...]))
    wide = jnp.concatenate([turned, jnp.zeros_like(turned)], axis=1)
    skewed = pltpu.roll(wide, 1, 1, stride=1, stride_axis=0)
    row = lax.broadcasted_iota(jnp.int32, wide.shape, 0)
    col = lax.broadcasted_iota(jnp.int32, wide.shape, 1)
    band = skewed + (col <= row).astype(F32)
    first = (pl.program_id(0) == 0) & (col < window)
    put(high, low, jnp.where(first, 0.0, band))


def qkv_weights_kernel(w_q, w_k, w_v, high, low, high_t, low_t):
    stacked = jnp.concatenate([w_q[...], w_k[...], w_v[...]], axis=0)
    put(high, low, stacked)
    put(high_t, low_t, stacked.T)


def weights_kernel(w, high, low, high_t, low_t):
    put(high, low, w[...])
    put(high_t, low_t, w[...].T)


def out_weights_kernel(own, near, far, far_near, high_own, low_own, high_t, low_t):
    put(high_own, low_own, own[...])
    stacked = jnp.concatenate([own[...], near[...], far[...], far_near[...]], axis=0)
    put(high_t, low_t, stacked.T)


def column_stats(values_in):
    mean = jnp.mean(values_in, axis=0, keepdims=True)
    var = jnp.mean(values_in * values_in, axis=0, keepdims=True) - mean * mean
    return mean, lax.rsqrt(var + EPSILON)


def attend_kernel(
    info, x0, x1, x2, x3, cols, w_hi, w_lo, band_hi, band_lo, biases,
    mixed, quotient, f_query, f_numer, pair_hi, pair_lo, n_hi, n_lo, stats,
    x_all, far, last_hi, last_lo,
):
    step = pl.program_id(0)
    chans = x0.shape[0]
    window = TB
    place_rows(x_all, info[0], (x0, x1, x2, x3))
    x = x_all[...]
    mean, scale = column_stats(x)
    stats[0:1, :] = mean
    stats[1:2, :] = scale
    normed = split((x - mean) * scale * cols[:, 0:1] + cols[:, 1:2])
    n_hi[...], n_lo[...] = normed
    projected = dot3(get(w_hi, w_lo), normed, NN)
    exp_keys = jnp.exp(projected[chans : 2 * chans])
    carried = exp_keys * (projected[2 * chans :] + biases[:, 1:2])
    pair = split(jnp.concatenate([carried, exp_keys], axis=0))
    pair_hi[...], pair_lo[...] = pair

    @pl.when(step == 0)
    def _():
        far[...] = jnp.zeros_like(far)
        last_hi[...] = jnp.zeros_like(last_hi)
        last_lo[...] = jnp.zeros_like(last_lo)

    last = get(last_hi, last_lo)
    total = far[:, 0:1]
    gates = jax.nn.sigmoid(projected[:chans] + biases[:, 0:1])
    for at in range(0, x.shape[1], window):
        here = slice(at, at + window)
        near = (band_hi[here, :], band_lo[here, :])
        block = (pair[0][:, here], pair[1][:, here])
        sums = dot3(block, (near[0][:, window:], near[1][:, window:]), NT)
        sums = sums + dot3(last, (near[0][:, :window], near[1][:, :window]), NT)
        sums = sums + total
        total = total + jnp.sum(last[0].astype(F32) + last[1].astype(F32), axis=1, keepdims=True)
        last = block
        inverse = 1.0 / sums[chans:]
        ratio = sums[:chans] * inverse
        gate = gates[:, here]
        quotient[:, here] = ratio
        mixed[:, here] = gate * ratio
        f_query[:, here] = ratio * gate * (1.0 - gate)
        f_numer[:, here] = gate * inverse
    far[...] = jnp.broadcast_to(total, far.shape)
    last_hi[...], last_lo[...] = last


def cotangent_kernel(info, c0, c1, c2, c3, hi, lo, own_sum, c_all):
    step = pl.program_id(0)
    place_rows(c_all, info[0], (c0, c1, c2, c3))
    live = live_row(info[1], step * WIDE, WIDE)
    put(hi, lo, c_all[...] * live)

    @pl.when(step == 0)
    def _():
        own_sum[...] = jnp.zeros_like(own_sum)

    own_sum[...] += fold(c0[...] * live)


def hidden_kernel(
    info, m0, m1, m2, m3, x0, x1, x2, x3, cols, wo_hi, wo_lo, wu_hi, wu_lo, up_bias,
    act_hi, act_lo, slope, normal, n_hi, n_lo, inner_own, stats,
    x_all,
):
    step = pl.program_id(0)
    place_rows(x_all, info[0], (x0, x1, x2, x3))
    live = live_row(info[1], step * WIDE, WIDE)
    parts = jnp.concatenate([m0[...], m1[...], m2[...], m3[...]], axis=0)
    out = dot3(get(wo_hi, wo_lo), split(parts), NN)
    inner = x_all[...] + live * (out + cols[:, 2:3])
    x_all[...] = inner
    inner_own[...] = take_rows(x_all, info[0], x0.shape[0])
    mean, scale = column_stats(inner)
    stats[0:1, :] = scale
    unit = (inner - mean) * scale
    normal[...] = unit
    normed = split(unit * cols[:, 3:4] + cols[:, 4:5])
    n_hi[...], n_lo[...] = normed
    pre = dot3(get(wu_hi, wu_lo), normed, NN) + up_bias[...]
    root = 0.7978845608028654
    cubic = 0.044715
    square = pre * pre
    bent = jnp.tanh(root * pre * (1.0 + cubic * square))
    put(act_hi, act_lo, 0.5 * pre * (1.0 + bent))
    slope[...] = 0.5 * (1.0 + bent) + 0.5 * pre * (1.0 - bent * bent) * (
        root * (1.0 + 3.0 * cubic * square)
    )


def outer_kernel(a_hi, a_lo, b_hi, b_lo, grad):
    grad[...] = dot3(get(a_hi, a_lo), get(b_hi, b_lo), NT)


def part_halves(grid, place, keep, send):
    rows = grid.shape[0] // 4
    core = place & 1
    for far in range(2):
        here = slice(far * rows, (far + 1) * rows)
        keep[here, :] = take_rows(grid, 2 * far + core, rows)
        send[here, :] = take_rows(grid, 2 * far + 1 - core, rows)


def hidden_back_kernel(
    info, c_hi, c_lo, wd_hi, wd_lo, slope, wu_hi, wu_lo, d_hi, d_lo, keep, send, bias_sum, grid
):
    d_pre = dot3(get(wd_hi, wd_lo), get(c_hi, c_lo), NN) * slope[...]

    @pl.when(pl.program_id(0) == 0)
    def _():
        bias_sum[...] = jnp.zeros_like(bias_sum)

    bias_sum[...] += fold(d_pre)
    parts = split(d_pre)
    d_hi[...], d_lo[...] = parts
    grid[...] = dot3(get(wu_hi, wu_lo), parts, NN)
    part_halves(grid, info[0], keep, send)


def down_kernel(info, wd_hi, wd_lo, act_hi, act_lo, keep, send, grid):
    grid[...] = dot3(get(wd_hi, wd_lo), get(act_hi, act_lo), NN)
    part_halves(grid, info[0], keep, send)


def inner_back_kernel(
    info, half, other, normal, stats, cols, c0, c1, c2, c3, wo_hi, wo_lo, f_query, f_numer, quotient,
    b_hi, b_lo, dq_hi, dq_lo, dp_hi, dp_lo, inner_own, sum_gain, sum_bias, sum_out, sum_query,
    c_all, d_all,
):
    step = pl.program_id(0)
    place = info[0]
    core = place & 1
    chans = c0.shape[0]
    place_rows(c_all, place, (c0, c1, c2, c3))
    for far in range(2):
        here = slice(far * chans, (far + 1) * chans)
        d_all[pl.ds(pl.multiple_of((2 * far + core) * chans, chans), chans), :] = half[here, :]
        d_all[pl.ds(pl.multiple_of((2 * far + 1 - core) * chans, chans), chans), :] = other[here, :]
    live = live_row(info[1], step * WIDE, WIDE)
    scaled = d_all[...] * cols[:, 3:4]
    unit = normal[...]
    mean_one = jnp.mean(scaled, axis=0, keepdims=True)
    mean_two = jnp.mean(scaled * unit, axis=0, keepdims=True)
    d_inner = c_all[...] + stats[0:1, :] * (scaled - mean_one - unit * mean_two)
    c_all[...] = d_inner
    own = take_rows(c_all, place, chans)
    inner_own[...] = own
    d_own = take_rows(d_all, place, chans)

    @pl.when(step == 0)
    def _():
        for total in (sum_gain, sum_bias, sum_out, sum_query):
            total[...] = jnp.zeros_like(total)

    sum_gain[...] += fold(d_own * take_rows(normal, place, chans))
    sum_bias[...] += fold(d_own)
    sum_out[...] += fold(own * live)
    branch = split(d_inner * live)
    b_hi[...], b_lo[...] = branch
    d_mixed = dot3(get(wo_hi, wo_lo), branch, NN)
    d_query = d_mixed * f_query[...]
    sum_query[...] += fold(d_query)
    put(dq_hi, dq_lo, d_query)
    d_numer = d_mixed * f_numer[...]
    put(dp_hi, dp_lo, jnp.concatenate([d_numer, -d_numer * quotient[...]], axis=0))


def outer_two_kernel(a, b_hi, b_lo, c_hi, c_lo, d_hi, d_lo, grad):
    rows = a.shape[0]
    grad[:rows, :] = dot3(split(a[...]), get(b_hi, b_lo), NT)
    grad[rows:, :] = dot3(get(c_hi, c_lo), get(d_hi, d_lo), NT)


def mix_back_kernel(
    d_hi, d_lo, before_hi, before_lo, here_hi, here_lo, band_hi, band_lo, bias,
    kv_hi, kv_lo, d_bias, sum_value,
    carry, later, ahead,
):
    step = pl.program_id(0)
    block = pl.num_programs(0) - 1 - step
    window = TB
    chans = d_hi.shape[0] // 2

    @pl.when(step == 0)
    def _():
        for total in (carry, later, ahead, sum_value):
            total[...] = jnp.zeros_like(total)

    d_pair = get(d_hi, d_lo)
    d_wide = d_pair[0].astype(F32) + d_pair[1].astype(F32)
    into = dot3(d_pair, get(band_hi, band_lo), NN)
    back = into[:, window:] + carry[...] + later[:, 0:1]
    carry[...] = into[:, :window]
    later[...] = later[...] + ahead[...]
    ahead[...] = jnp.broadcast_to(jnp.sum(d_wide, axis=1, keepdims=True), ahead.shape)
    turned = split(d_wide.T)
    right = dot3(turned, get(here_hi, here_lo), NN)
    left = dot3(turned, get(before_hi, before_lo), NN)
    left = jnp.where(block == 0, 0.0, left)
    wide = jnp.concatenate([reverse_lanes(right), reverse_lanes(left)], axis=1)
    placed = pltpu.roll(wide, window + 1, 1, stride=1, stride_axis=0)
    d_bias[...] = placed[:, :window] * jnp.exp(bias[...])
    pair = here_hi[...].astype(F32) + here_lo[...].astype(F32)
    d_value = pair[chans:] * back[:chans]
    d_key = pair[:chans] * back[:chans] + pair[chans:] * back[chans:]
    sum_value[...] += fold(d_value)
    put(kv_hi, kv_lo, jnp.concatenate([d_key, d_value], axis=0))


def project_back_kernel(
    info, dq_hi, dq_lo, kv_hi, kv_lo, w_hi, w_lo, x0, x1, x2, x3, stats, cols, keep, send, sums, x_all, grid
):
    place_rows(x_all, info[0], (x0, x1, x2, x3))
    d_all = (
        jnp.concatenate([dq_hi[...], kv_hi[...]], axis=0),
        jnp.concatenate([dq_lo[...], kv_lo[...]], axis=0),
    )
    terms = dot3(get(w_hi, w_lo), d_all, NN)
    grid[...] = terms
    part_halves(grid, info[0], keep, send)
    scaled = terms * cols[:, 0:1]
    unit = (x_all[...] - stats[0:1, :]) * stats[1:2, :]
    sums[...] = jnp.zeros_like(sums)
    sums[0:1, :] = jnp.sum(scaled, axis=0, keepdims=True)
    sums[1:2, :] = jnp.sum(scaled * unit, axis=0, keepdims=True)


def input_back_kernel(model, mine, come, inner_own, x_own, stats, sums, gain, d_in, sum_gain, sum_bias):
    d_normed = mine[...] + come[...]
    unit = (x_own[...] - stats[0:1, :]) * stats[1:2, :]

    @pl.when(pl.program_id(0) == 0)
    def _():
        for total in (sum_gain, sum_bias):
            total[...] = jnp.zeros_like(total)

    sum_gain[...] += fold(d_normed * unit)
    sum_bias[...] += fold(d_normed)
    d_in[...] = inner_own[...] + stats[1:2, :] * (
        d_normed * gain[...] - sums[0:1, :] / model - unit * (sums[1:2, :] / model)
    )


def swap(block, bit):
    return lax.ppermute(block, "mp", [(i, i ^ bit) for i in range(4)])


def gather_parts(own):
    far = swap(own, 2)
    near = swap(own, 1)
    return own, near, far, swap(far, 1)


def in_order(parts, place):
    stacked = jnp.stack(parts)
    return jnp.concatenate(
        [lax.dynamic_index_in_dim(stacked, place ^ i, 0, keepdims=False) for i in range(4)], axis=0
    )


def after(value, *earlier):
    return lax.optimization_barrier((value, earlier))[0]


def cut(grid, bit):
    rows = grid.shape[0] // 2
    mine = lax.dynamic_slice_in_dim(grid, bit * rows, rows, 0)
    other = lax.dynamic_slice_in_dim(grid, (1 - bit) * rows, rows, 0)
    return mine, other


def join(mine, other, bit):
    low = jnp.where(bit == 0, mine, other)
    high = jnp.where(bit == 0, other, mine)
    return jnp.concatenate([low, high], axis=0)


def trade(block, flip):
    size = lax.axis_size("dp")
    return lax.ppermute(block, "dp", [(i, i ^ flip) for i in range(size)])


def dp_bit(flip):
    return (lax.axis_index("dp") // flip) % 2


def dp_chains(grids, orders):
    first = [cut(g, dp_bit(o[0])) for g, o in zip(grids, orders)]
    come = [trade(send, o[0]) for (_, send), o in zip(first, orders)]
    held = [mine + c for (mine, _), c in zip(first, come)]
    second = [cut(h, dp_bit(o[1])) for h, o in zip(held, orders)]
    come = [trade(send, o[1]) for (_, send), o in zip(second, orders)]
    held = [mine + c for (mine, _), c in zip(second, come)]
    come = [trade(h, o[2]) for h, o in zip(held, orders)]
    held = [h + c for h, c in zip(held, come)]
    come = [trade(h, o[1]) for h, o in zip(held, orders)]
    held = [join(h, c, dp_bit(o[1])) for h, c, o in zip(held, come, orders)]
    come = [trade(h, o[0]) for h, o in zip(held, orders)]
    return [join(h, c, dp_bit(o[0])) for h, c, o in zip(held, come, orders)]


def dp_sum(grid):
    if lax.axis_size("dp") != 8:
        return lax.psum(grid, "dp")
    rows = grid.shape[0] // 2
    parts = dp_chains([grid[:rows], grid[rows:]], [(1, 2, 4), (2, 1, 4)])
    return jnp.concatenate(parts, axis=0)


def pair_sum(grid, place):
    core, far = place % 2, place // 2
    mine, send = cut(grid, core)
    mine, send = cut(mine + swap(send, 1), far)
    quarter = dp_sum(mine + swap(send, 2))
    half = join(quarter, swap(quarter, 2), far)
    return join(half, swap(half, 1), core)


def dp_sum_small(grid):
    if lax.axis_size("dp") != 8:
        return lax.psum(grid, "dp")
    for flip in (1, 2, 4):
        grid = grid + trade(grid, flip)
    return grid


def body(
    inputs,
    lengths,
    ln1_gain,
    ln1_bias,
    w_query,
    w_key,
    w_value,
    query_bias,
    value_bias,
    pair_bias,
    w_out,
    out_bias,
    ln2_gain,
    ln2_bias,
    w_up,
    up_bias,
    w_down,
    down_bias,
    cotangent,
):
    seq_rows, span, chans = inputs.shape
    window = pair_bias.shape[1]
    model = 4 * chans
    units = w_up.shape[1]
    steps = span // WIDE
    blocks = span // TB
    assert seq_rows == 1 and window == TB
    place = lax.axis_index("mp")
    info = jnp.stack([place.astype(jnp.int32), lengths[0]])

    unit = 6 * model * model * span

    x_own = inputs[0].T
    x_far = swap(x_own, 2)
    x_near = swap(x_own, 1)
    vectors = jnp.stack([ln1_gain, ln1_bias, out_bias, ln2_gain, ln2_bias])
    vectors = jnp.pad(vectors, ((0, 3), (0, 0)))
    cols = in_order([v.T for v in gather_parts(vectors)], place)

    band = call(
        band_kernel, blocks,
        [(pair_bias, pl.BlockSpec((TB, window), lambda i: (i, 0)))],
        [(shaped((span, 2 * window), BF16), pl.BlockSpec((TB, 2 * window), lambda i: (i, 0)))] * 2,
        name="band",
    )
    wide_qkv = (shaped((3 * chans, model), BF16), whole((3 * chans, model)))
    tall_qkv = (shaped((model, 3 * chans), BF16), whole((model, 3 * chans)))
    wq_hi, wq_lo, wqt_hi, wqt_lo = call(
        qkv_weights_kernel, 1,
        [(w.T, whole((chans, model))) for w in (w_query, w_key, w_value)],
        [wide_qkv, wide_qkv, tall_qkv, tall_qkv],
        name="qkv_weights",
    )
    up_out = (shaped((model, units), BF16), whole((model, units)))
    up_t_out = (shaped((units, model), BF16), whole((units, model)))
    wu_hi, wu_lo, wut_hi, wut_lo = call(
        weights_kernel, 1, [(w_up, whole((model, units)))], [up_out, up_out, up_t_out, up_t_out], name="up_weights"
    )
    wd_hi, wd_lo, wdt_hi, wdt_lo = call(
        weights_kernel, 1, [(w_down, whole((units, model)))], [up_t_out, up_t_out, up_out, up_out], name="down_weights"
    )

    x_far = after(x_far, band, wq_hi, wqt_hi, wu_hi, wut_hi, wd_hi, wdt_hi, cols)
    x_parts = (x_own, x_near, x_far, swap(x_far, 1))
    wo_own = after(w_out, x_far)
    wo_far = swap(wo_own, 2)
    wo_near = swap(w_out, 1)

    thin = (shaped((chans, span)), across(chans))
    tall = (shaped((model, span)), across(model))
    tall_half = (shaped((model, span), BF16), across(model))
    hid_half = (shaped((units, span), BF16), across(units))
    pair_half = (shaped((2 * chans, span), BF16), across(2 * chans))
    thin_half = (shaped((chans, span), BF16), across(chans))
    rows8 = (shaped((8, span)), across(8))
    x_ins = [(x, across(chans)) for x in x_parts]
    scalars = (info, SCALARS)
    cols_in = (cols, whole((model, 8)))

    mixed, quotient, f_query, f_numer, pair_hi, pair_lo, n1_hi, n1_lo, stats_one = call(
        attend_kernel, steps,
        [scalars, *x_ins, cols_in, (wq_hi, whole((3 * chans, model))), (wq_lo, whole((3 * chans, model)))]
        + [(b, pl.BlockSpec((WIDE, 2 * window), lambda i: (i, 0))) for b in band]
        + [(jnp.stack([query_bias, value_bias], axis=1), whole((chans, 2)))],
        [thin, thin, thin, thin, pair_half, pair_half, tall_half, tall_half, rows8],
        [
            pltpu.VMEM((model, WIDE), F32),
            pltpu.VMEM((2 * chans, 128), F32),
            pltpu.VMEM((2 * chans, TB), BF16),
            pltpu.VMEM((2 * chans, TB), BF16),
        ],
        name="attend",
        flops=1.25 * unit,
    )

    mixed_far = swap(mixed, 2)
    mixed_near = swap(mixed, 1)
    wo_parts = (w_out, wo_near, wo_far, swap(wo_far, 1))
    wo_hi, wo_lo, wot_hi, wot_lo = call(
        out_weights_kernel, 1,
        [(w, whole((chans, model))) for w in wo_parts],
        [(shaped((chans, model), BF16), whole((chans, model)))] * 2
        + [(shaped((model, model), BF16), whole((model, model)))] * 2,
        name="out_weights",
    )
    mixed_far = after(mixed_far, wo_hi, wot_hi)
    mixed_parts = (mixed, mixed_near, mixed_far, swap(mixed_far, 1))
    cot_own = cotangent[0].T
    cot_far = swap(after(cot_own, mixed_far), 2)
    cot_near = swap(cot_own, 1)
    lanes_own = (shaped((chans, 128)), whole((chans, 128)))

    act_hi, act_lo, slope, normal_two, n2_hi, n2_lo, inner_own, stats_two = call(
        hidden_kernel, steps,
        [scalars, *[(p, across(chans)) for p in mixed_parts], *x_ins, cols_in]
        + [(wot_hi, whole((model, model))), (wot_lo, whole((model, model)))]
        + [(wut_hi, whole((units, model))), (wut_lo, whole((units, model))), (up_bias[:, None], whole((units, 1)))],
        [hid_half, hid_half, (shaped((units, span)), across(units)), tall, tall_half, tall_half, thin, rows8],
        [pltpu.VMEM((model, WIDE), F32)],
        name="hidden",
        flops=2 * unit,
    )

    cot_far = after(cot_far, act_hi)
    cot_parts = (cot_own, cot_near, cot_far, swap(cot_far, 1))
    cot_ins = [(c, across(chans)) for c in cot_parts]
    c_hi, c_lo, s_down = call(
        cotangent_kernel, steps, [scalars, *cot_ins], [tall_half, tall_half, lanes_own],
        [pltpu.VMEM((model, WIDE), F32)], name="cotangent",
    )

    def outer(a_hi, a_lo, b_hi, b_lo, name):
        rows, inner_len = a_hi.shape
        deep = b_hi.shape[0]
        slab = pl.BlockSpec((rows // 2, inner_len), lambda i: (i, 0))
        return call(
            outer_kernel, 2,
            [(a_hi, slab), (a_lo, slab), (b_hi, whole((deep, inner_len))), (b_lo, whole((deep, inner_len)))],
            [(shaped((rows, deep)), pl.BlockSpec((rows // 2, deep), lambda i: (i, 0)))],
            name=name,
            flops=unit,
        )[0]

    d_w_down = outer(act_hi, act_lo, c_hi, c_lo, "down_grad")
    c_hi, c_lo = after((c_hi, c_lo), d_w_down)
    g_down = dp_sum(d_w_down)
    half_out = (shaped((2 * chans, span)), across(2 * chans))
    dpre_hi, dpre_lo, keep, send, s_up = call(
        hidden_back_kernel, steps,
        [scalars, (c_hi, across(model)), (c_lo, across(model))]
        + [(wd_hi, whole((units, model))), (wd_lo, whole((units, model))), (slope, across(units))]
        + [(wu_hi, whole((model, units))), (wu_lo, whole((model, units)))],
        [hid_half, hid_half, half_out, half_out, (shaped((units, 128)), whole((units, 128)))],
        [pltpu.VMEM((model, WIDE), F32)],
        name="hidden_back",
        flops=2 * unit,
    )
    half = keep + swap(send, 1)
    half_far = swap(half, 2)
    d_w_up = outer(n2_hi, n2_lo, dpre_hi, dpre_lo, "up_grad")
    g_up = dp_sum(d_w_up)
    keep_down, send_down = call(
        down_kernel, steps,
        [scalars, (wdt_hi, whole((model, units))), (wdt_lo, whole((model, units))), (act_hi, across(units)), (act_lo, across(units))],
        [half_out, half_out],
        [pltpu.VMEM((model, WIDE), F32)],
        name="down",
        flops=unit,
    )
    half_far = after(half_far, d_w_up, keep_down)
    half = half + half_far
    other = swap(half, 1)

    far_bit = place // 2
    mine_down, send_down = cut(keep_down + swap(send_down, 1), far_bit)
    come_down = swap(after(send_down, half_far), 2)
    live = (jnp.arange(span, dtype=jnp.int32) < lengths[0]).astype(F32)[None, :]
    result = inner_own + live * (mine_down + come_down + down_bias[:, None])

    b_hi, b_lo, dq_hi, dq_lo, dp_hi, dp_lo, d_inner_own, s_gain2, s_bias2, s_out, s_query = call(
        inner_back_kernel, steps,
        [scalars, (half, across(2 * chans)), (other, across(2 * chans)), (normal_two, across(model)), (stats_two, across(8)), cols_in]
        + cot_ins
        + [(wo_hi, whole((chans, model))), (wo_lo, whole((chans, model)))]
        + [(f_query, across(chans)), (f_numer, across(chans)), (quotient, across(chans))],
        [tall_half, tall_half, thin_half, thin_half, pair_half, pair_half, thin, lanes_own, lanes_own, lanes_own, lanes_own],
        [pltpu.VMEM((model, WIDE), F32), pltpu.VMEM((model, WIDE), F32)],
        name="inner_back",
        flops=0.25 * unit,
    )
    thin_all, tall_all = whole((chans, span)), whole((model, span))
    def back_at(i):
        return blocks - 1 - i

    pair_spec = pl.BlockSpec((2 * chans, TB), lambda i: (0, back_at(i)))
    prev_spec = pl.BlockSpec((2 * chans, TB), lambda i: (0, jnp.maximum(back_at(i) - 1, 0)))
    band_spec = pl.BlockSpec((TB, 2 * window), lambda i: (back_at(i), 0))
    row_spec = pl.BlockSpec((TB, window), lambda i: (back_at(i), 0))
    kv_hi, kv_lo, d_pair, s_value = call(
        mix_back_kernel, blocks,
        [(dp_hi, pair_spec), (dp_lo, pair_spec), (pair_hi, prev_spec), (pair_lo, prev_spec), (pair_hi, pair_spec), (pair_lo, pair_spec)]
        + [(band[0], band_spec), (band[1], band_spec), (pair_bias, row_spec)],
        [(shaped((2 * chans, span), BF16), pair_spec)] * 2 + [(shaped((span, window)), row_spec), lanes_own],
        [pltpu.VMEM((2 * chans, TB), F32), pltpu.VMEM((2 * chans, 128), F32), pltpu.VMEM((2 * chans, 128), F32)],
        name="mix_back",
        flops=0.7 * unit,
    )
    grad_kv = call(
        outer_kernel, 1,
        [(kv_hi, whole((2 * chans, span))), (kv_lo, whole((2 * chans, span))), (n1_hi, tall_all), (n1_lo, tall_all)],
        [(shaped((2 * chans, model)), whole((2 * chans, model)))],
        name="key_value_grad",
        flops=0.5 * unit,
    )[0]
    grad_oq = call(
        outer_two_kernel, 1,
        [(mixed, thin_all), (b_hi, tall_all), (b_lo, tall_all)]
        + [(dq_hi, thin_all), (dq_lo, thin_all), (n1_hi, tall_all), (n1_lo, tall_all)],
        [(shaped((2 * chans, model)), whole((2 * chans, model)))],
        name="out_query_grad",
        flops=0.5 * unit,
    )[0]

    dq_hi, kv_hi = after((dq_hi, kv_hi), grad_oq, grad_kv)
    g_kv = dp_sum(jnp.concatenate([grad_oq, grad_kv], axis=0))
    grad_oq, grad_kv = g_kv[: 2 * chans], g_kv[2 * chans :]
    d_pair = pair_sum(d_pair, place)
    keep, send, sums = call(
        project_back_kernel, steps,
        [scalars, (dq_hi, across(chans)), (dq_lo, across(chans)), (kv_hi, across(2 * chans)), (kv_lo, across(2 * chans))]
        + [(wqt_hi, whole((model, 3 * chans))), (wqt_lo, whole((model, 3 * chans))), *x_ins, (stats_one, across(8)), cols_in],
        [half_out, half_out, rows8],
        [pltpu.VMEM((model, WIDE), F32), pltpu.VMEM((model, WIDE), F32)],
        name="project_back",
        flops=0.75 * unit,
    )
    sums = sums + swap(sums, 1)
    sums = sums + swap(sums, 2)
    mine, send = cut(keep + swap(send, 1), far_bit)
    d_inputs, s_gain1, s_bias1 = call(
        partial(input_back_kernel, float(model)), steps,
        [(mine, across(chans)), (swap(send, 2), across(chans)), (d_inner_own, across(chans)), (x_parts[0], across(chans))]
        + [(stats_one, across(8)), (sums, across(8)), (ln1_gain[:, None], whole((chans, 1)))],
        [thin, lanes_own, lanes_own],
        name="input_back",
    )

    small = jnp.concatenate(
        [
            jnp.sum(s, axis=1)
            for s in (s_gain1, s_bias1, s_query, s_value, s_out, s_gain2, s_bias2, s_down, s_up)
        ]
    )
    small = dp_sum_small(small)
    vecs = [small[i * chans : (i + 1) * chans] for i in range(8)]
    return (
        result.T[None],
        d_inputs.T[None],
        vecs[0],
        vecs[1],
        grad_oq[chans:].T,
        grad_kv[:chans].T,
        grad_kv[chans:].T,
        vecs[2],
        vecs[3],
        d_pair,
        grad_oq[:chans],
        vecs[4],
        vecs[5],
        vecs[6],
        g_up,
        small[8 * chans :],
        g_down,
        vecs[7],
    )


def solution(mesh):
    rows = P("dp", None, "mp")
    vec = P("mp")
    out_dim = P(None, "mp")
    in_dim = P("mp", None)
    return jax.shard_map(
        body,
        mesh=mesh,
        in_specs=(
            rows, P("dp"), vec, vec, out_dim, out_dim, out_dim, vec, vec, P(), in_dim, vec, vec, vec,
            out_dim, vec, in_dim, vec, rows,
        ),
        out_specs=(
            rows, rows, vec, vec, out_dim, out_dim, out_dim, vec, vec, P(), in_dim, vec, vec, vec,
            out_dim, vec, in_dim, vec,
        ),
        check_vma=False,
    )
```

```python
import math
from functools import partial

import jax
import jax.numpy as jnp
from jax import lax
from jax.experimental import pallas as pl
from jax.experimental.pallas import tpu as pltpu
from jax.sharding import PartitionSpec as P

EPSILON = 1e-05
TB = 256
WIDE = 512
SCALE = 0.0
PIN_MID = True
PIN_GLUE = False
PIN_ATT = True
PIN_HIN = True
PIN_DG = False
PIN_HID = False
NN = (((1,), (0,)), ((), ()))
NT = (((1,), (1,)), ((), ()))
F32 = jnp.float32
BF16 = jnp.bfloat16


def split(wide):
    high = wide.astype(BF16)
    return high, (wide - high.astype(F32)).astype(BF16)


def dot3(left, right, dims):
    def one(a, b):
        return lax.dot_general(a, b, dims, preferred_element_type=F32)

    return one(left[0], right[0]) + (one(left[0], right[1]) + one(left[1], right[0]))


def put(high_ref, low_ref, wide):
    high, low = split(wide)
    high_ref[...] = high
    low_ref[...] = low


def get(high_ref, low_ref):
    return high_ref[...], low_ref[...]


def reverse_lanes(wide):
    size = wide.shape[1]
    row = lax.broadcasted_iota(jnp.int32, (size, size), 0)
    col = lax.broadcasted_iota(jnp.int32, (size, size), 1)
    turn = (row + col == size - 1).astype(F32).astype(BF16)
    high, rest = split(wide)
    middle = wide - high.astype(F32)
    low = (middle - rest.astype(F32)).astype(BF16)

    def one(part):
        return lax.dot_general(part, turn, NN, preferred_element_type=F32)

    return one(high) + (one(rest) + one(low))


def live_row(length, start, width):
    return (lax.broadcasted_iota(jnp.int32, (1, width), 1) + start < length).astype(F32)


def whole(shape):
    return pl.BlockSpec(shape, lambda i: (0,) * len(shape))


def across(rows, width=WIDE):
    return pl.BlockSpec((rows, width), lambda i: (0, i))


SCALARS = pl.BlockSpec(memory_space=pltpu.SMEM)


def shaped(shape, dtype=F32):
    return jax.ShapeDtypeStruct(shape, dtype)


def to_hbm(array):
    return pltpu.with_memory_space_constraint(array, pltpu.HBM)


def call(kernel, grid, ins, outs, scratch=(), name=None, pin=True, pin_out=True):
    held = sum(2 * math.prod(spec.block_shape) * array.dtype.itemsize for array, spec in ins if spec.block_shape)
    held += sum(2 * math.prod(spec.block_shape) * shape.dtype.itemsize for shape, spec in outs)
    held += sum(math.prod(ref.shape) * jnp.dtype(ref.dtype).itemsize for ref in scratch)
    moved = sum(array.size * array.dtype.itemsize for array, _ in ins)
    moved += sum(math.prod(shape.shape) * shape.dtype.itemsize for shape, _ in outs)
    arrays = [array if spec is SCALARS or not pin else to_hbm(array) for array, spec in ins]
    run = pl.pallas_call(
        kernel,
        grid=(grid,),
        in_specs=[spec for _, spec in ins],
        out_specs=[spec for _, spec in outs],
        out_shape=[pltpu.HBM(shape.shape, shape.dtype) if pin_out else shape for shape, _ in outs],
        scratch_shapes=list(scratch),
        compiler_params=pltpu.CompilerParams(
            dimension_semantics=("arbitrary",), vmem_limit_bytes=min(held + 16 * 2**20, 58 * 2**20)
        ),
        cost_estimate=pl.CostEstimate(flops=0, transcendentals=0, bytes_accessed=int(moved * SCALE)),
        name=name,
    )
    return list(run(*arrays))


def place_rows(target, place, parts):
    for flip, part in enumerate(parts):
        rows = part.shape[0]
        target[pl.ds(pl.multiple_of((place ^ flip) * rows, rows), rows), :] = part[...]


def take_rows(source, index, rows):
    return source[pl.ds(pl.multiple_of(index * rows, rows), rows), :]


def fold(wide):
    total = wide[:, :128]
    for at in range(128, wide.shape[1], 128):
        total = total + wide[:, at : at + 128]
    return total


def band_kernel(bias, high, low):
    window = bias.shape[1]
    turned = reverse_lanes(jnp.exp(bias[...]))
    wide = jnp.concatenate([turned, jnp.zeros_like(turned)], axis=1)
    skewed = pltpu.roll(wide, 1, 1, stride=1, stride_axis=0)
    row = lax.broadcasted_iota(jnp.int32, wide.shape, 0)
    col = lax.broadcasted_iota(jnp.int32, wide.shape, 1)
    band = skewed + (col <= row).astype(F32)
    first = (pl.program_id(0) == 0) & (col < window)
    put(high, low, jnp.where(first, 0.0, band))


def qkv_weights_kernel(w_q, w_k, w_v, high, low, high_t, low_t):
    stacked = jnp.concatenate([w_q[...], w_k[...], w_v[...]], axis=0)
    put(high, low, stacked)
    put(high_t, low_t, stacked.T)


def weights_kernel(w, high, low, high_t, low_t):
    put(high, low, w[...])
    put(high_t, low_t, w[...].T)


def out_weights_kernel(own, near, far, far_near, high_t, low_t):
    stacked = jnp.concatenate([own[...], near[...], far[...], far_near[...]], axis=0)
    put(high_t, low_t, stacked.T)


def column_stats(values_in):
    mean = jnp.mean(values_in, axis=0, keepdims=True)
    var = jnp.mean(values_in * values_in, axis=0, keepdims=True) - mean * mean
    return mean, lax.rsqrt(var + EPSILON)


def attend_kernel(
    info, x0, x1, x2, x3, v0, v1, v2, v3, w_hi, w_lo, band_hi, band_lo,
    cols, mixed, quotient, f_query, f_numer, pair_hi, pair_lo, n_hi, n_lo, stats,
    x_all, far, last_hi, last_lo,
):
    step = pl.program_id(0)
    chans = x0.shape[0]
    window = TB

    @pl.when(step == 0)
    def _():
        for flip, part in enumerate((v0, v1, v2, v3)):
            start = pl.multiple_of((info[0] ^ flip) * chans, chans)
            cols[pl.ds(start, chans), :] = part[...].T[:chans]

    biases = v0[...].T[:chans]
    place_rows(x_all, info[0], (x0, x1, x2, x3))
    x = x_all[...]
    mean, scale = column_stats(x)
    stats[0:1, :] = mean
    stats[1:2, :] = scale
    normed = split((x - mean) * scale * cols[:, 0:1] + cols[:, 1:2])
    n_hi[...], n_lo[...] = normed
    projected = dot3(get(w_hi, w_lo), normed, NN)
    exp_keys = jnp.exp(projected[chans : 2 * chans])
    carried = exp_keys * (projected[2 * chans :] + biases[:, 6:7])
    pair = split(jnp.concatenate([carried, exp_keys], axis=0))
    pair_hi[...], pair_lo[...] = pair

    @pl.when(step == 0)
    def _():
        far[...] = jnp.zeros_like(far)
        last_hi[...] = jnp.zeros_like(last_hi)
        last_lo[...] = jnp.zeros_like(last_lo)

    last = get(last_hi, last_lo)
    total = far[:, 0:1]
    gates = jax.nn.sigmoid(projected[:chans] + biases[:, 5:6])
    for at in range(0, x.shape[1], window):
        here = slice(at, at + window)
        near = (band_hi[here, :], band_lo[here, :])
        block = (pair[0][:, here], pair[1][:, here])
        sums = dot3(block, (near[0][:, window:], near[1][:, window:]), NT)
        sums = sums + dot3(last, (near[0][:, :window], near[1][:, :window]), NT)
        sums = sums + total
        total = total + jnp.sum(last[0].astype(F32) + last[1].astype(F32), axis=1, keepdims=True)
        last = block
        inverse = 1.0 / sums[chans:]
        ratio = sums[:chans] * inverse
        gate = gates[:, here]
        quotient[:, here] = ratio
        mixed[:, here] = gate * ratio
        f_query[:, here] = ratio * gate * (1.0 - gate)
        f_numer[:, here] = gate * inverse
    far[...] = jnp.broadcast_to(total, far.shape)
    last_hi[...], last_lo[...] = last


def hidden_kernel(
    info, m0, m1, m2, m3, x0, x1, x2, x3, cols, wo_hi, wo_lo, wu_hi, wu_lo, up_bias,
    act_hi, act_lo, slope, n_hi, n_lo, inner_own, stats,
    x_all,
):
    step = pl.program_id(0)
    place_rows(x_all, info[0], (x0, x1, x2, x3))
    live = live_row(info[1], step * WIDE, WIDE)
    parts = jnp.concatenate([m0[...], m1[...], m2[...], m3[...]], axis=0)
    out = dot3(get(wo_hi, wo_lo), split(parts), NN)
    inner = x_all[...] + live * (out + cols[:, 2:3])
    x_all[...] = inner
    inner_own[...] = take_rows(x_all, info[0], x0.shape[0])
    mean, scale = column_stats(inner)
    stats[0:1, :] = scale
    unit = (inner - mean) * scale
    normed = split(unit * cols[:, 3:4] + cols[:, 4:5])
    n_hi[...], n_lo[...] = normed
    pre = dot3(get(wu_hi, wu_lo), normed, NN) + up_bias[...]
    root = 0.7978845608028654
    cubic = 0.044715
    square = pre * pre
    bent = jnp.tanh(root * pre * (1.0 + cubic * square))
    put(act_hi, act_lo, 0.5 * pre * (1.0 + bent))
    slope[...] = 0.5 * (1.0 + bent) + 0.5 * pre * (1.0 - bent * bent) * (
        root * (1.0 + 3.0 * cubic * square)
    )


def parted(rows, info):
    step = rows // 4
    for half in range(2):
        bit = info[2 + half]
        yield pl.multiple_of((2 * half + bit) * step, step)
        yield pl.multiple_of((2 * half + 1 - bit) * step, step)


def outer_kernel(info, a_hi, a_lo, b_hi, b_lo, *rest):
    outs, (s_hi, s_lo) = rest[:4], rest[4:]
    rows = a_hi.shape[0]
    step = rows // 4

    @pl.when(pl.program_id(0) == 0)
    def _():
        for at, start in enumerate(parted(rows, info)):
            here = slice(at * step, (at + 1) * step)
            s_hi[here, :] = a_hi[pl.ds(start, step), :]
            s_lo[here, :] = a_lo[pl.ds(start, step), :]

    grad = dot3(get(s_hi, s_lo), get(b_hi, b_lo), NT)
    for at, out in enumerate(outs):
        out[...] = grad[at * step : (at + 1) * step]


def down_grad_kernel(info, a_hi, a_lo, c0, c1, c2, c3, *rest):
    outs, (c_hi, c_lo, own_sum, s_hi, s_lo, c_all) = rest[:4], rest[4:]
    rows = a_hi.shape[0]
    step = rows // 4
    live = live_row(info[1], 0, c_all.shape[1])
    for at, start in enumerate(parted(rows, info)):
        here = slice(at * step, (at + 1) * step)
        s_hi[here, :] = a_hi[pl.ds(start, step), :]
        s_lo[here, :] = a_lo[pl.ds(start, step), :]
    place_rows(c_all, info[0], (c0, c1, c2, c3))
    put(c_hi, c_lo, c_all[...] * live)
    own_sum[...] = fold(c0[...] * live)
    grad = dot3(get(s_hi, s_lo), get(c_hi, c_lo), NT)
    for at, out in enumerate(outs):
        out[...] = grad[at * step : (at + 1) * step]


def order_pair(bit, first, second, keep, send):
    keep[...] = jnp.where(bit == 0, first, second)
    send[...] = jnp.where(bit == 0, second, first)


def projection_grads_kernel(
    info, mixed, b_hi, b_lo, q_hi, q_lo, kv_hi, kv_lo, n_hi, n_lo, keep_0, send_0, keep_1, send_1
):
    rows = mixed.shape[0]
    normed = get(n_hi, n_lo)
    d_out = dot3(split(mixed[...]), get(b_hi, b_lo), NT)
    d_query = dot3(get(q_hi, q_lo), normed, NT)
    order_pair(info[2], d_out, d_query, keep_0, send_0)
    d_kv = dot3(get(kv_hi, kv_lo), normed, NT)
    order_pair(info[3], d_kv[:rows], d_kv[rows:], keep_1, send_1)


def projection_done_kernel(info, h_0, c_0, h_1, c_1, d_out, d_query, d_key, d_value):
    order_pair(info[2], h_0[...], c_0[...], d_out, d_query)
    order_pair(info[3], h_1[...], c_1[...], d_key, d_value)


def halve_kernel(places, info, *refs):
    count = len(places)
    for i, at in enumerate(places):
        kept, come = refs[2 * i], refs[2 * i + 1]
        mine, send = refs[2 * count + 2 * i], refs[2 * count + 2 * i + 1]
        rows = mine.shape[0]
        mine[...] = take_rows(kept, info[at], rows) + take_rows(come, info[at], rows)
        send[...] = take_rows(kept, 1 - info[at], rows) + take_rows(come, 1 - info[at], rows)


def add_kernel(info, *refs):
    count = len(refs) // 3
    for i in range(count):
        refs[2 * count + i][...] = refs[2 * i][...] + refs[2 * i + 1][...]


def pack_kernel(info, *refs):
    rows = refs[0].shape[0]
    refs[4][:rows, :] = refs[0][...] + refs[1][...]
    refs[4][rows:, :] = refs[2][...] + refs[3][...]


def unpack_kernel(info, held, come, first, second):
    rows = first.shape[0]
    first[...] = held[:rows, :] + come[:rows, :]
    second[...] = held[rows:, :] + come[rows:, :]


def join_kernel(places, merged, info, *refs):
    count = len(places)
    for i, at in enumerate(places):
        held, come = refs[2 * i], refs[2 * i + 1]
        out = refs[2 * count] if merged else refs[2 * count + i]
        rows = held.shape[0]
        base = 2 * i if merged else 0
        out[pl.ds(pl.multiple_of((base + info[at]) * rows, rows), rows), :] = held[...]
        out[pl.ds(pl.multiple_of((base + 1 - info[at]) * rows, rows), rows), :] = come[...]


def lane_sums_kernel(*refs):
    ins, out = refs[:-1], refs[-1]
    wide = jnp.concatenate([ref[...] for ref in ins], axis=0)
    high, rest = split(wide)
    low = (wide - high.astype(F32) - rest.astype(F32)).astype(BF16)
    ones = jnp.ones((8, wide.shape[1]), BF16)

    def one(part):
        return lax.dot_general(ones, part, NT, preferred_element_type=F32)

    out[...] = one(high) + (one(rest) + one(low))


def part_halves(grid, place, keep, send):
    rows = grid.shape[0] // 4
    core = place & 1
    for far in range(2):
        here = slice(far * rows, (far + 1) * rows)
        keep[here, :] = take_rows(grid, 2 * far + core, rows)
        send[here, :] = take_rows(grid, 2 * far + 1 - core, rows)


def hidden_back_kernel(
    info, c_hi, c_lo, wd_hi, wd_lo, slope, wu_hi, wu_lo, d_hi, d_lo, keep, send, bias_sum, grid
):
    @pl.when(pl.program_id(0) == 0)
    def _():
        bias_sum[...] = jnp.zeros_like(bias_sum)

    d_pre = dot3(get(wd_hi, wd_lo), get(c_hi, c_lo), NN) * slope[...]
    bias_sum[...] += fold(d_pre)
    parts = split(d_pre)
    d_hi[...], d_lo[...] = parts
    grid[...] = dot3(get(wu_hi, wu_lo), parts, NN)
    part_halves(grid, info[0], keep, send)


def down_kernel(info, wd_hi, wd_lo, act_hi, act_lo, keep, send, grid):
    grid[...] = dot3(get(wd_hi, wd_lo), get(act_hi, act_lo), NN)
    part_halves(grid, info[0], keep, send)


def inner_back_kernel(
    info, half, other, n_hi, n_lo, stats, cols, c0, c1, c2, c3, w_out, f_query, f_numer, quotient,
    b_hi, b_lo, dq_hi, dq_lo, dp_hi, dp_lo, inner_own, sum_gain, sum_bias, sum_out, sum_query,
    c_all, d_all, normal, wo_hi, wo_lo,
):
    step = pl.program_id(0)
    place = info[0]
    core = place & 1
    chans = c0.shape[0]
    place_rows(c_all, place, (c0, c1, c2, c3))
    for far in range(2):
        here = slice(far * chans, (far + 1) * chans)
        d_all[pl.ds(pl.multiple_of((2 * far + core) * chans, chans), chans), :] = half[here, :]
        d_all[pl.ds(pl.multiple_of((2 * far + 1 - core) * chans, chans), chans), :] = other[here, :]
    live = live_row(info[1], step * WIDE, WIDE)
    scaled = d_all[...] * cols[:, 3:4]
    unit = (n_hi[...].astype(F32) + n_lo[...].astype(F32) - cols[:, 4:5]) / cols[:, 3:4]
    normal[...] = unit
    mean_one = jnp.mean(scaled, axis=0, keepdims=True)
    mean_two = jnp.mean(scaled * unit, axis=0, keepdims=True)
    d_inner = c_all[...] + stats[0:1, :] * (scaled - mean_one - unit * mean_two)
    c_all[...] = d_inner
    own = take_rows(c_all, place, chans)
    inner_own[...] = own
    d_own = take_rows(d_all, place, chans)

    @pl.when(step == 0)
    def _():
        put(wo_hi, wo_lo, w_out[...])
        for total in (sum_gain, sum_bias, sum_out, sum_query):
            total[...] = jnp.zeros_like(total)

    sum_gain[...] += fold(d_own * take_rows(normal, place, chans))
    sum_bias[...] += fold(d_own)
    sum_out[...] += fold(own * live)
    branch = split(d_inner * live)
    b_hi[...], b_lo[...] = branch
    d_mixed = dot3(get(wo_hi, wo_lo), branch, NN)
    d_query = d_mixed * f_query[...]
    sum_query[...] += fold(d_query)
    put(dq_hi, dq_lo, d_query)
    d_numer = d_mixed * f_numer[...]
    put(dp_hi, dp_lo, jnp.concatenate([d_numer, -d_numer * quotient[...]], axis=0))


def mix_back_kernel(
    d_hi, d_lo, before_hi, before_lo, here_hi, here_lo, band_hi, band_lo, bias,
    kv_hi, kv_lo, d_bias, sum_value,
    carry, later, ahead,
):
    step = pl.program_id(0)
    block = pl.num_programs(0) - 1 - step
    window = TB
    chans = d_hi.shape[0] // 2

    @pl.when(step == 0)
    def _():
        for total in (carry, later, ahead, sum_value):
            total[...] = jnp.zeros_like(total)

    d_pair = get(d_hi, d_lo)
    d_wide = d_pair[0].astype(F32) + d_pair[1].astype(F32)
    into = dot3(d_pair, get(band_hi, band_lo), NN)
    back = into[:, window:] + carry[...] + later[:, 0:1]
    carry[...] = into[:, :window]
    later[...] = later[...] + ahead[...]
    ahead[...] = jnp.broadcast_to(jnp.sum(d_wide, axis=1, keepdims=True), ahead.shape)
    turned = split(d_wide.T)
    right = dot3(turned, get(here_hi, here_lo), NN)
    left = dot3(turned, get(before_hi, before_lo), NN)
    left = jnp.where(block == 0, 0.0, left)
    wide = jnp.concatenate([reverse_lanes(right), reverse_lanes(left)], axis=1)
    placed = pltpu.roll(wide, window + 1, 1, stride=1, stride_axis=0)
    d_bias[...] = placed[:, :window] * jnp.exp(bias[...])
    pair = here_hi[...].astype(F32) + here_lo[...].astype(F32)
    d_value = pair[chans:] * back[:chans]
    d_key = pair[:chans] * back[:chans] + pair[chans:] * back[chans:]
    sum_value[...] += fold(d_value)
    put(kv_hi, kv_lo, jnp.concatenate([d_key, d_value], axis=0))


def project_back_kernel(
    info, dq_hi, dq_lo, kv_hi, kv_lo, w_hi, w_lo, x0, x1, x2, x3, stats, cols, d_pair, keep, send,
    x_all, grid,
):
    place_rows(x_all, info[0], (x0, x1, x2, x3))
    d_all = (
        jnp.concatenate([dq_hi[...], kv_hi[...]], axis=0),
        jnp.concatenate([dq_lo[...], kv_lo[...]], axis=0),
    )
    terms = dot3(get(w_hi, w_lo), d_all, NN)
    grid[...] = terms
    part_halves(grid, info[0], keep, send)
    scaled = terms * cols[:, 0:1]
    unit = (x_all[...] - stats[0:1, :]) * stats[1:2, :]
    at = grid.shape[0] // 2
    sums = (jnp.sum(scaled, axis=0, keepdims=True), jnp.sum(scaled * unit, axis=0, keepdims=True))
    sums = jnp.concatenate([*sums, jnp.zeros((6, grid.shape[1]), F32)], axis=0)
    rows, window = d_pair.shape[0] // 8, d_pair.shape[1]
    for out, core in ((keep, info[4]), (send, 1 - info[4])):
        out[at : at + 8, :] = sums
        for block in range(grid.shape[1] // window):
            start = 4 * rows * core + rows * (grid.shape[1] // window * pl.program_id(0) + block)
            lanes = slice(block * window, (block + 1) * window)
            out[at + 8 :, lanes] = d_pair[pl.ds(pl.multiple_of(start, rows), rows), :]


def core_halves_kernel(info, keep, come, mine, send):
    rows = (mine.shape[0] - 8) * 3 // 4
    for out, far in ((mine, info[5]), (send, 1 - info[5])):
        out[:rows, :] = take_rows(keep, far, rows) + take_rows(come, far, rows)
        out[rows : rows + 8, :] = keep[2 * rows : 2 * rows + 8, :] + come[2 * rows : 2 * rows + 8, :]
        half = keep[2 * rows + 8 :, :] + come[2 * rows + 8 :, :]
        wide = half.shape[1] // 2
        part = jnp.where(far == 0, half[:, :wide], half[:, wide:])
        tall = part.shape[0] // 2
        out[rows + 8 :, :wide] = part[:tall]
        out[rows + 8 :, wide:] = part[tall:]


def chip_sum_kernel(info, mine, come, pair, sums):
    rows = mine.shape[0] - pair.shape[0] - 8
    sums[...] = mine[rows : rows + 8, :] + come[rows : rows + 8, :]
    pair[...] = mine[rows + 8 :, :] + come[rows + 8 :, :]


def pair_chips_kernel(info, own, other, half):
    tall, wide = own.shape[0], own.shape[1] // 2
    for low, lanes in ((True, slice(0, wide)), (False, slice(wide, 2 * wide))):
        near = info[5] == (0 if low else 1)
        for top in range(2):
            here = slice(top * wide, (top + 1) * wide)
            half[top * tall : (top + 1) * tall, lanes] = jnp.where(near, own[:, here], other[:, here])


def pair_cores_kernel(info, own, other, d_pair):
    rows, window = own.shape[0], d_pair.shape[1]
    for half, core in ((own, info[4]), (other, 1 - info[4])):
        for block in range(4):
            start = 4 * rows * core + rows * block
            d_pair[pl.ds(pl.multiple_of(start, rows), rows), :] = half[:, block * window : (block + 1) * window]


def input_back_kernel(model, mine, come, inner_own, x_own, stats, sums, gain, d_in, sum_gain, sum_bias):
    rows = inner_own.shape[0]
    d_normed = mine[:rows, :] + come[:rows, :]
    unit = (x_own[...] - stats[0:1, :]) * stats[1:2, :]

    @pl.when(pl.program_id(0) == 0)
    def _():
        for total in (sum_gain, sum_bias):
            total[...] = jnp.zeros_like(total)

    sum_gain[...] += fold(d_normed * unit)
    sum_bias[...] += fold(d_normed)
    d_in[...] = inner_own[...] + stats[1:2, :] * (
        d_normed * gain[...] - sums[0:1, :] / model - unit * (sums[1:2, :] / model)
    )


def swap(block, bit):
    return lax.ppermute(block, "mp", [(i, i ^ bit) for i in range(4)])


def gather_parts(own):
    far = swap(own, 2)
    near = swap(own, 1)
    return own, near, far, swap(far, 1)


def in_order(parts, place):
    stacked = jnp.stack(parts)
    return jnp.concatenate(
        [lax.dynamic_index_in_dim(stacked, place ^ i, 0, keepdims=False) for i in range(4)], axis=0
    )


def after(value, *earlier):
    return lax.optimization_barrier((value, earlier))[0]


def trade(block, flip):
    size = lax.axis_size("dp")
    return lax.ppermute(block, "dp", [(i, i ^ flip) for i in range(size)])


def glue(kernel, scalars, ins, outs, name, steps=1):
    def columns(shape):
        return pl.BlockSpec((shape[0], shape[1] // steps), lambda i: (0, i))

    return call(
        kernel, steps,
        [scalars, *[(x, columns(x.shape)) for x in ins]],
        [(shaped(shape), columns(shape)) for shape in outs],
        name=name,
        pin=False,
        pin_out=PIN_GLUE,
    )


def add_trade(block, flip, *gate):
    if lax.axis_size("dp") != 8:
        return jnp.zeros_like(block)
    return trade(after(block, *gate), flip)


def settle(sums, arrived, *gates):
    comes = [s.come for s in sums]
    comes, arrived, _ = lax.optimization_barrier((comes, arrived, gates))
    for s, come in zip(sums, comes):
        s.come = come
        s.take()
    return arrived


class Sum:
    FLIPS = ((1, 2), (2, 1), (4,), (2, 1), (1, 2))

    def __init__(self, scalars, blocks, merged):
        self.merged = merged
        self.come = []
        self.scalars = scalars
        self.direct = lax.axis_size("dp") != 8
        self.stage = 0
        if self.direct:
            self.total = lax.psum(blocks, "dp")
            if merged:
                self.total = [jnp.concatenate(self.total, axis=0)]
            self.out = self.total
        else:
            self.mine, self.out = blocks[0::2], blocks[1::2]

    def send(self, *gate):
        if not self.direct:
            pairs = zip(self.out, self.FLIPS[self.stage])
            self.come = [trade(after(block, *gate), flip) for block, flip in pairs]

    def take(self):
        if self.direct:
            return
        ins = [x for pair in zip(self.mine, self.come) for x in pair]
        rows, width = self.mine[0].shape
        name = f"sum_stage_{self.stage}"
        if self.stage == 0:
            half = (rows // 2, width)
            got = glue(partial(halve_kernel, (3, 2)), self.scalars, ins, [half] * 4, name, 2)
            self.mine, self.out = got[0::2], got[1::2]
        elif self.stage == 1:
            self.mine = self.out = glue(pack_kernel, self.scalars, ins, [(2 * rows, width)], name)
        elif self.stage == 2:
            self.mine = self.out = glue(unpack_kernel, self.scalars, ins, [(rows // 2, width)] * 2, name)
        elif self.stage == 3:
            kernel = partial(join_kernel, (3, 2), False)
            self.mine = self.out = glue(kernel, self.scalars, ins, [(2 * rows, width)] * 2, name)
        else:
            shapes = [(4 * rows, width)] if self.merged else [(rows, width)] * 4
            kernel = partial(join_kernel, (2, 3), True) if self.merged else projection_done_kernel
            self.out = self.total = glue(kernel, self.scalars, ins, shapes, name, 2)
        self.stage += 1


def body(
    inputs,
    lengths,
    ln1_gain,
    ln1_bias,
    w_query,
    w_key,
    w_value,
    query_bias,
    value_bias,
    pair_bias,
    w_out,
    out_bias,
    ln2_gain,
    ln2_bias,
    w_up,
    up_bias,
    w_down,
    down_bias,
    cotangent,
):
    seq_rows, span, chans = inputs.shape
    window = pair_bias.shape[1]
    model = 4 * chans
    units = w_up.shape[1]
    steps = span // WIDE
    blocks = span // TB
    assert seq_rows == 1 and window == TB
    place = lax.axis_index("mp")
    row = lax.axis_index("dp")
    halving = lax.axis_size("dp") == 8
    bits = [row % 2, (row // 2) % 2] if halving else [jnp.int32(0)] * 2
    info = jnp.stack([place.astype(jnp.int32), lengths[0], *bits, place % 2, place // 2])

    x_own = inputs[0].T
    x_far = swap(x_own, 2)
    x_near = swap(x_own, 1)
    vectors = jnp.stack([ln1_gain, ln1_bias, out_bias, ln2_gain, ln2_bias, query_bias, value_bias])
    vectors = jnp.pad(vectors, ((0, 1), (0, 256 - chans)))
    v_far = swap(vectors, 2)
    v_near = swap(vectors, 1)

    band = call(
        band_kernel, blocks,
        [(pair_bias, pl.BlockSpec((TB, window), lambda i: (i, 0)))],
        [(shaped((span, 2 * window), BF16), pl.BlockSpec((TB, 2 * window), lambda i: (i, 0)))] * 2,
        name="band",
    )
    wide_qkv, tall_qkv = (3 * chans, model), (model, 3 * chans)
    up_dims, down_dims = (model, units), (units, model)

    def prepare(kernel, ins, dims, name):
        return call(
            kernel, 1, [(w, whole(w.shape)) for w in ins], [(shaped(d, BF16), whole(d)) for d in dims for _ in range(2)], name=name
        )

    wq_hi, wq_lo, wqt_hi, wqt_lo = prepare(
        qkv_weights_kernel, [w_query.T, w_key.T, w_value.T], [wide_qkv, tall_qkv], "qkv_weights"
    )
    wu_hi, wu_lo, wut_hi, wut_lo = prepare(weights_kernel, [w_up], [up_dims, down_dims], "up_weights")
    up_column, gain_column = up_bias[:, None], ln1_gain[:, None]
    v_far, x_far, up_column, gain_column = lax.optimization_barrier(
        (v_far, x_far, up_column, gain_column, band, wq_hi, wu_hi)
    )[:4]
    x_parts = (x_own, x_near, x_far, swap(x_far, 1))
    v_parts = (vectors, v_near, v_far, swap(v_far, 1))
    wo_own = after(w_out, x_far, v_far)
    wo_far = swap(wo_own, 2)
    wo_near = swap(w_out, 1)

    thin = (shaped((chans, span)), across(chans))
    tall_half = (shaped((model, span), BF16), across(model))
    hid_half = (shaped((units, span), BF16), across(units))
    pair_half = (shaped((2 * chans, span), BF16), across(2 * chans))
    thin_half = (shaped((chans, span), BF16), across(chans))
    rows8 = (shaped((8, span)), across(8))
    x_ins = [(x, across(chans)) for x in x_parts]
    scalars = (info, SCALARS)

    cols_out = (shaped((model, 8)), whole((model, 8)))
    cols, mixed, quotient, f_query, f_numer, pair_hi, pair_lo, n1_hi, n1_lo, stats_one = call(
        attend_kernel, steps,
        [scalars, *x_ins, *[(v, whole((8, 256))) for v in v_parts], (wq_hi, whole(wide_qkv)), (wq_lo, whole(wide_qkv))]
        + [(b, pl.BlockSpec((WIDE, 2 * window), lambda i: (i, 0))) for b in band],
        [cols_out, thin, thin, thin, thin, pair_half, pair_half, tall_half, tall_half, rows8],
        [
            pltpu.VMEM((model, WIDE), F32),
            pltpu.VMEM((2 * chans, 128), F32),
            pltpu.VMEM((2 * chans, TB), BF16),
            pltpu.VMEM((2 * chans, TB), BF16),
        ],
        name="attend",
        pin=PIN_ATT,
    )

    cols_in = (cols, whole((model, 8)))
    mixed_far = swap(mixed, 2)
    mixed_near = swap(mixed, 1)
    wo_parts = (w_out, wo_near, wo_far, swap(wo_far, 1))
    wot_hi, wot_lo = prepare(out_weights_kernel, wo_parts, [(model, model)], "out_weights")
    wd_hi, wd_lo, wdt_hi, wdt_lo = prepare(weights_kernel, [w_down], [down_dims, up_dims], "down_weights")
    mixed_far = after(mixed_far, wot_hi, wd_hi)
    mixed_parts = (mixed, mixed_near, mixed_far, swap(mixed_far, 1))
    cot_own = cotangent[0].T
    cot_far = swap(after(cot_own, mixed_far), 2)
    cot_near = swap(cot_own, 1)
    lanes_own = (shaped((chans, 128)), whole((chans, 128)))

    act_hi, act_lo, slope, n2_hi, n2_lo, inner_own, stats_two = call(
        hidden_kernel, steps,
        [scalars, *[(p, across(chans)) for p in mixed_parts], *x_ins, cols_in]
        + [(wot_hi, whole((model, model))), (wot_lo, whole((model, model)))]
        + [(wut_hi, whole(down_dims)), (wut_lo, whole(down_dims)), (up_column, whole((units, 1)))],
        [hid_half, hid_half, (shaped((units, span)), across(units)), tall_half, tall_half, thin, rows8],
        [pltpu.VMEM((model, WIDE), F32)],
        name="hidden",
        pin=PIN_HIN,
        pin_out=PIN_HID,
    )

    cot_far = after(cot_far, act_hi)
    cot_parts = (cot_own, cot_near, cot_far, swap(cot_far, 1))
    cot_ins = [(c, across(chans)) for c in cot_parts]
    def outer(a_hi, a_lo, b_hi, b_lo, name, steps=2):
        rows, inner_len = a_hi.shape
        deep = b_hi.shape[0]
        left = whole((rows, inner_len))
        right = pl.BlockSpec((deep // steps, inner_len), lambda i: (i, 0))
        part = (shaped((rows // 4, deep)), across(rows // 4, deep // steps))
        grads = call(
            outer_kernel, steps,
            [scalars, (a_hi, left), (a_lo, left), (b_hi, right), (b_lo, right)],
            [part] * 4,
            [pltpu.VMEM((rows, inner_len), BF16)] * 2,
            name=name,
            pin=False,
        )
        return Sum(scalars, grads, True)

    whole_half = (shaped((model, span), BF16), whole((model, span)))
    block = (shaped((units // 4, model)), whole((units // 4, model)))
    *grads, c_hi, c_lo, s_down = call(
        down_grad_kernel, 1,
        [scalars, (act_hi, whole((units, span))), (act_lo, whole((units, span))), *[(c, whole((chans, span))) for c in cot_parts]],
        [block] * 4 + [whole_half, whole_half, lanes_own],
        [pltpu.VMEM((units, span), BF16)] * 2 + [pltpu.VMEM((model, span), F32)],
        name="down_grad",
        pin=PIN_DG,
    )
    g_down = Sum(scalars, grads, True)
    g_down.send()
    c_hi, c_lo = after((c_hi, c_lo), g_down.out)
    half_out = (shaped((2 * chans, span)), across(2 * chans))
    half_shape = (2 * chans, span)
    dpre_hi, dpre_lo, keep, send, s_up = call(
        hidden_back_kernel, steps,
        [scalars, (c_hi, across(model)), (c_lo, across(model)), (wd_hi, whole(down_dims)), (wd_lo, whole(down_dims))]
        + [(slope, across(units)), (wu_hi, whole(up_dims)), (wu_lo, whole(up_dims))],
        [hid_half, hid_half, half_out, half_out, (shaped((units, 128)), whole((units, 128)))],
        [pltpu.VMEM((model, WIDE), F32)],
        name="hidden_back",
        pin=False,
        pin_out=PIN_MID,
    )
    send = settle([g_down], send, keep)
    half = glue(add_kernel, scalars, [keep, swap(after(send, g_down.out), 1)], [half_shape], "core_sum", 2)[0]
    half_far = swap(half, 2)
    g_down.send(half)
    g_up = outer(after(n2_hi, half), n2_lo, dpre_hi, dpre_lo, "up_grad")
    settle([g_down], [], g_up.out)
    g_down.send()
    g_up.send(g_down.out)
    keep_down, send_down = call(
        down_kernel, steps,
        [scalars, (wdt_hi, whole(up_dims)), (wdt_lo, whole(up_dims)), (after(act_hi, g_down.out), across(units)), (act_lo, across(units))],
        [half_out, half_out],
        [pltpu.VMEM((model, WIDE), F32)],
        name="down",
        pin=False,
        pin_out=PIN_MID,
    )
    half_far, send_down = settle([g_down, g_up], (half_far, send_down), keep_down)
    half = glue(add_kernel, scalars, [half, half_far], [half_shape], "chip_sum", 2)[0]
    half = after(half, g_down.out, g_up.out)
    other = swap(half, 1)
    come = swap(after(send_down, half), 1)
    other, come = lax.optimization_barrier((other, come))
    own_shape = (chans, span)
    mine_down, send_down = glue(
        partial(halve_kernel, (5,)), scalars, [keep_down, come], [own_shape] * 2, "down_halves", 2
    )
    other = after(other, send_down)
    g_down.send(other)
    g_up.send(other)

    b_hi, b_lo, dq_hi, dq_lo, dp_hi, dp_lo, d_inner_own, s_gain2, s_bias2, s_out, s_query = call(
        inner_back_kernel, steps,
        [scalars, (half, across(2 * chans)), (other, across(2 * chans)), (n2_hi, across(model)), (n2_lo, across(model)), (stats_two, across(8)), cols_in]
        + cot_ins
        + [(w_out, whole((chans, model)))]
        + [(f_query, across(chans)), (f_numer, across(chans)), (quotient, across(chans))],
        [tall_half, tall_half, thin_half, thin_half, pair_half, pair_half, thin, lanes_own, lanes_own, lanes_own, lanes_own],
        [pltpu.VMEM((model, WIDE), F32)] * 3 + [pltpu.VMEM((chans, model), BF16)] * 2,
        name="inner_back",
        pin=False,
        pin_out=PIN_MID,
    )
    dp_hi = settle([g_down, g_up], dp_hi, b_hi)
    g_down.send()
    g_up.send()
    come_down = swap(after(send_down, g_down.out, g_up.out), 2)
    dp_hi = after(dp_hi, g_down.out, g_up.out)
    thin_all, tall_all = whole((chans, span)), whole((model, span))

    def back_at(i):
        return blocks - 1 - i

    pair_spec = pl.BlockSpec((2 * chans, TB), lambda i: (0, back_at(i)))
    prev_spec = pl.BlockSpec((2 * chans, TB), lambda i: (0, jnp.maximum(back_at(i) - 1, 0)))
    band_spec = pl.BlockSpec((TB, 2 * window), lambda i: (back_at(i), 0))
    row_spec = pl.BlockSpec((TB, window), lambda i: (back_at(i), 0))
    kv_hi, kv_lo, d_pair, s_value = call(
        mix_back_kernel, blocks,
        [(dp_hi, pair_spec), (dp_lo, pair_spec), (pair_hi, prev_spec), (pair_lo, prev_spec), (pair_hi, pair_spec), (pair_lo, pair_spec)]
        + [(band[0], band_spec), (band[1], band_spec), (pair_bias, row_spec)],
        [(shaped((2 * chans, span), BF16), pair_spec)] * 2 + [(shaped((span, window)), row_spec), lanes_own],
        [pltpu.VMEM((2 * chans, TB), F32), pltpu.VMEM((2 * chans, 128), F32), pltpu.VMEM((2 * chans, 128), F32)],
        name="mix_back",
        pin=False,
        pin_out=PIN_MID,
    )
    slab = pl.BlockSpec((model // 2, span), lambda i: (i, 0))
    grads = call(
        projection_grads_kernel, 2,
        [scalars, (mixed, thin_all), (b_hi, slab), (b_lo, slab), (dq_hi, thin_all), (dq_lo, thin_all)]
        + [(kv_hi, whole((2 * chans, span))), (kv_lo, whole((2 * chans, span))), (n1_hi, slab), (n1_lo, slab)],
        [(shaped((chans, model)), across(chans, model // 2))] * 4,
        name="projection_grads", pin=False,
    )
    g_mix = Sum(scalars, grads, False)
    dq_hi, kv_hi = after((dq_hi, kv_hi), grads)
    payload_rows = 2 * chans + 8 + span // 8
    payload = (shaped((payload_rows, span)), across(payload_rows))
    keep, send = call(
        project_back_kernel, steps,
        [scalars, (dq_hi, across(chans)), (dq_lo, across(chans)), (kv_hi, across(2 * chans)), (kv_lo, across(2 * chans))]
        + [(wqt_hi, whole(tall_qkv)), (wqt_lo, whole(tall_qkv)), *x_ins, (stats_one, across(8)), cols_in, (d_pair, whole((span, window)))],
        [payload, payload],
        [pltpu.VMEM((model, WIDE), F32)] * 2,
        name="project_back",
        pin=False,
        pin_out=PIN_MID,
    )
    send, come_down = settle([g_down, g_up], (send, come_down), keep, grads)
    live = (jnp.arange(span, dtype=jnp.int32) < lengths[0]).astype(F32)[None, :]
    result = inner_own + live * (mine_down + come_down + down_bias[:, None])
    come = swap(after(send, g_up.out, g_down.out, result), 1)
    mine, send = glue(core_halves_kernel, scalars, [keep, come], [(chans + 8 + span // 16, span)] * 2, "core_halves")
    g_mix.send(send)
    g_up.send(send)
    come = settle([g_mix, g_up], swap(send, 2))
    quarter = (span // 16, span)
    pair_sum, sums = glue(chip_sum_kernel, scalars, [mine, come], [quarter, (8, span)], "chip_sums")
    come, sums, pair_sum = after((come, sums, pair_sum), g_mix.out, g_up.out)
    come, sums, pair_sum = lax.optimization_barrier((come, sums, pair_sum))
    g_mix.send(pair_sum)
    pair_come = add_trade(pair_sum, 4)
    d_inputs, s_gain1, s_bias1 = call(
        partial(input_back_kernel, float(model)), steps,
        [(mine, across(mine.shape[0])), (come, across(mine.shape[0])), (d_inner_own, across(chans)), (x_parts[0], across(chans))]
        + [(stats_one, across(8)), (sums, across(8)), (gain_column, whole((chans, 1)))],
        [thin, lanes_own, lanes_own],
        name="input_back",
        pin=False,
        pin_out=PIN_MID,
    )

    lanes = (s_gain1, s_bias1, s_query, s_value, s_out, s_gain2, s_bias2, s_down, s_up)
    count = sum(x.shape[0] for x in lanes)
    small = call(
        lane_sums_kernel, 1, [(x, whole(x.shape)) for x in lanes], [(shaped((8, count)), whole((8, count)))],
        name="lane_sums", pin=False,
    )[0]
    small, pair_come = settle([g_mix], (small, pair_come))
    pair_sum = glue(add_kernel, scalars, [pair_sum, pair_come], [quarter], "pair_far")[0]
    small, pair_sum = after((small, pair_sum), g_mix.out)
    g_mix.send(small, pair_sum)
    g_up.send(small, pair_sum)
    small_come, pair_come = settle([g_mix, g_up], (add_trade(small, 1), add_trade(pair_sum, 1)))
    pair_sum = glue(add_kernel, scalars, [pair_sum, pair_come], [quarter], "pair_x")[0]
    small = glue(add_kernel, scalars, [small, small_come], [(8, count)], "small_x")[0]
    small, pair_sum = after((small, pair_sum), g_mix.out, g_up.out)
    g_mix.send(small, pair_sum)
    small_come, pair_come = settle([g_mix], (add_trade(small, 2), add_trade(pair_sum, 2)))
    pair_sum = glue(add_kernel, scalars, [pair_sum, pair_come], [quarter], "pair_z")[0]
    small = glue(add_kernel, scalars, [small, small_come], [(8, count)], "small_z")[0]
    small, pair_sum = after((small, pair_sum), g_mix.out)
    g_mix.send(small, pair_sum)
    small_come, pair_come = settle([g_mix], (add_trade(small, 4), swap(pair_sum, 2)))
    pair_half = glue(pair_chips_kernel, scalars, [pair_sum, pair_come], [(span // 8, span)], "pair_chips")[0]
    small = (small + small_come)[0]
    pair_come = swap(pair_half, 1)
    d_pair = glue(pair_cores_kernel, scalars, [pair_half, pair_come], [(span, window)], "pair_cores")[0]
    if not halving:
        d_pair = lax.psum(d_pair, "dp")
        small = lax.psum(small, "dp")
    d_w_out, d_w_query, d_w_key, d_w_value = g_mix.total
    vecs = [small[i * chans : (i + 1) * chans] for i in range(8)]
    return (
        result.T[None],
        d_inputs.T[None],
        vecs[0],
        vecs[1],
        d_w_query.T,
        d_w_key.T,
        d_w_value.T,
        vecs[2],
        vecs[3],
        d_pair,
        d_w_out,
        vecs[4],
        vecs[5],
        vecs[6],
        g_up.total[0],
        small[8 * chans :],
        g_down.total[0],
        vecs[7],
    )


def solution(mesh):
    rows = P("dp", None, "mp")
    vec = P("mp")
    out_dim = P(None, "mp")
    in_dim = P("mp", None)
    return jax.shard_map(
        body,
        mesh=mesh,
        in_specs=(
            rows, P("dp"), vec, vec, out_dim, out_dim, out_dim, vec, vec, P(), in_dim, vec, vec, vec,
            out_dim, vec, in_dim, vec, rows,
        ),
        out_specs=(
            rows, rows, vec, vec, out_dim, out_dim, out_dim, vec, vec, P(), in_dim, vec, vec, vec,
            out_dim, vec, in_dim, vec,
        ),
        check_vma=False,
    )
```

```python
import math
from functools import partial

import jax
import jax.numpy as jnp
from jax import lax
from jax.experimental import pallas as pl
from jax.experimental.pallas import tpu as pltpu
from jax.sharding import PartitionSpec as P

EPSILON = 1e-05
TB = 256
WIDE = 512
SCALE = 0.0
PIN_MID = True
PIN_HB = False
PIN_MB = False
PIN_IB = False
PIN_PB = False
PIN_PG = False
PIN_UG = False
PIN_GO = False
PIN_GLUE = False
PIN_ATT = True
PIN_HIN = True
PIN_DG = False
PIN_HID = False
NN = (((1,), (0,)), ((), ()))
NT = (((1,), (1,)), ((), ()))
F32 = jnp.float32
BF16 = jnp.bfloat16


def split(wide):
    high = wide.astype(BF16)
    return high, (wide - high.astype(F32)).astype(BF16)


def dot3(left, right, dims):
    def one(a, b):
        return lax.dot_general(a, b, dims, preferred_element_type=F32)

    return one(left[0], right[0]) + (one(left[0], right[1]) + one(left[1], right[0]))


def put(high_ref, low_ref, wide):
    high, low = split(wide)
    high_ref[...] = high
    low_ref[...] = low


def get(high_ref, low_ref):
    return high_ref[...], low_ref[...]


def reverse_lanes(wide):
    size = wide.shape[1]
    row = lax.broadcasted_iota(jnp.int32, (size, size), 0)
    col = lax.broadcasted_iota(jnp.int32, (size, size), 1)
    turn = (row + col == size - 1).astype(F32).astype(BF16)
    high, rest = split(wide)
    middle = wide - high.astype(F32)
    low = (middle - rest.astype(F32)).astype(BF16)

    def one(part):
        return lax.dot_general(part, turn, NN, preferred_element_type=F32)

    return one(high) + (one(rest) + one(low))


def live_row(length, start, width):
    return (lax.broadcasted_iota(jnp.int32, (1, width), 1) + start < length).astype(F32)


def whole(shape):
    return pl.BlockSpec(shape, lambda i: (0,) * len(shape))


def across(rows, width=WIDE):
    return pl.BlockSpec((rows, width), lambda i: (0, i))


SCALARS = pl.BlockSpec(memory_space=pltpu.SMEM)


def shaped(shape, dtype=F32):
    return jax.ShapeDtypeStruct(shape, dtype)


def to_hbm(array):
    return pltpu.with_memory_space_constraint(array, pltpu.HBM)


def call(kernel, grid, ins, outs, scratch=(), name=None, pin=True, pin_out=True):
    held = sum(2 * math.prod(spec.block_shape) * array.dtype.itemsize for array, spec in ins if spec.block_shape)
    held += sum(2 * math.prod(spec.block_shape) * shape.dtype.itemsize for shape, spec in outs)
    held += sum(math.prod(ref.shape) * jnp.dtype(ref.dtype).itemsize for ref in scratch)
    moved = sum(array.size * array.dtype.itemsize for array, _ in ins)
    moved += sum(math.prod(shape.shape) * shape.dtype.itemsize for shape, _ in outs)
    arrays = [array if spec is SCALARS or not pin else to_hbm(array) for array, spec in ins]
    run = pl.pallas_call(
        kernel,
        grid=(grid,),
        in_specs=[spec for _, spec in ins],
        out_specs=[spec for _, spec in outs],
        out_shape=[pltpu.HBM(shape.shape, shape.dtype) if pin_out else shape for shape, _ in outs],
        scratch_shapes=list(scratch),
        compiler_params=pltpu.CompilerParams(
            dimension_semantics=("arbitrary",), vmem_limit_bytes=min(held + 16 * 2**20, 58 * 2**20)
        ),
        cost_estimate=pl.CostEstimate(flops=0, transcendentals=0, bytes_accessed=int(moved * SCALE)),
        name=name,
    )
    return list(run(*arrays))


def place_rows(target, place, parts):
    for flip, part in enumerate(parts):
        rows = part.shape[0]
        target[pl.ds(pl.multiple_of((place ^ flip) * rows, rows), rows), :] = part[...]


def take_rows(source, index, rows):
    return source[pl.ds(pl.multiple_of(index * rows, rows), rows), :]


def fold(wide):
    total = wide[:, :128]
    for at in range(128, wide.shape[1], 128):
        total = total + wide[:, at : at + 128]
    return total


def band_kernel(bias, high, low):
    window = bias.shape[1]
    turned = reverse_lanes(jnp.exp(bias[...]))
    wide = jnp.concatenate([turned, jnp.zeros_like(turned)], axis=1)
    skewed = pltpu.roll(wide, 1, 1, stride=1, stride_axis=0)
    row = lax.broadcasted_iota(jnp.int32, wide.shape, 0)
    col = lax.broadcasted_iota(jnp.int32, wide.shape, 1)
    band = skewed + (col <= row).astype(F32)
    first = (pl.program_id(0) == 0) & (col < window)
    put(high, low, jnp.where(first, 0.0, band))


def qkv_weights_kernel(w_q, w_k, w_v, high, low, high_t, low_t):
    stacked = jnp.concatenate([w_q[...], w_k[...], w_v[...]], axis=0)
    put(high, low, stacked)
    put(high_t, low_t, stacked.T)


def weights_kernel(w, high, low, high_t, low_t):
    put(high, low, w[...])
    put(high_t, low_t, w[...].T)


def out_weights_kernel(own, near, far, far_near, high_t, low_t):
    stacked = jnp.concatenate([own[...], near[...], far[...], far_near[...]], axis=0)
    put(high_t, low_t, stacked.T)


def column_stats(values_in):
    mean = jnp.mean(values_in, axis=0, keepdims=True)
    var = jnp.mean(values_in * values_in, axis=0, keepdims=True) - mean * mean
    return mean, lax.rsqrt(var + EPSILON)


def attend_kernel(
    info, x0, x1, x2, x3, v0, v1, v2, v3, w_hi, w_lo, band_hi, band_lo,
    cols, mixed, quotient, f_query, f_numer, pair_hi, pair_lo, n_hi, n_lo, stats,
    x_all, far, last_hi, last_lo,
):
    step = pl.program_id(0)
    chans = x0.shape[0]
    window = TB

    @pl.when(step == 0)
    def _():
        for flip, part in enumerate((v0, v1, v2, v3)):
            start = pl.multiple_of((info[0] ^ flip) * chans, chans)
            cols[pl.ds(start, chans), :] = part[...].T[:chans]

    biases = v0[...].T[:chans]
    place_rows(x_all, info[0], (x0, x1, x2, x3))
    x = x_all[...]
    mean, scale = column_stats(x)
    stats[0:1, :] = mean
    stats[1:2, :] = scale
    normed = split((x - mean) * scale * cols[:, 0:1] + cols[:, 1:2])
    n_hi[...], n_lo[...] = normed
    projected = dot3(get(w_hi, w_lo), normed, NN)
    exp_keys = jnp.exp(projected[chans : 2 * chans])
    carried = exp_keys * (projected[2 * chans :] + biases[:, 6:7])
    pair = split(jnp.concatenate([carried, exp_keys], axis=0))
    pair_hi[...], pair_lo[...] = pair

    @pl.when(step == 0)
    def _():
        far[...] = jnp.zeros_like(far)
        last_hi[...] = jnp.zeros_like(last_hi)
        last_lo[...] = jnp.zeros_like(last_lo)

    last = get(last_hi, last_lo)
    total = far[:, 0:1]
    gates = jax.nn.sigmoid(projected[:chans] + biases[:, 5:6])
    for at in range(0, x.shape[1], window):
        here = slice(at, at + window)
        near = (band_hi[here, :], band_lo[here, :])
        block = (pair[0][:, here], pair[1][:, here])
        sums = dot3(block, (near[0][:, window:], near[1][:, window:]), NT)
        sums = sums + dot3(last, (near[0][:, :window], near[1][:, :window]), NT)
        sums = sums + total
        total = total + jnp.sum(last[0].astype(F32) + last[1].astype(F32), axis=1, keepdims=True)
        last = block
        inverse = 1.0 / sums[chans:]
        ratio = sums[:chans] * inverse
        gate = gates[:, here]
        quotient[:, here] = ratio
        mixed[:, here] = gate * ratio
        f_query[:, here] = ratio * gate * (1.0 - gate)
        f_numer[:, here] = gate * inverse
    far[...] = jnp.broadcast_to(total, far.shape)
    last_hi[...], last_lo[...] = last


def hidden_kernel(
    info, m0, m1, m2, m3, x0, x1, x2, x3, cols, wo_hi, wo_lo, wu_hi, wu_lo, up_bias,
    act_hi, act_lo, slope, n_hi, n_lo, inner_own, stats,
    x_all,
):
    step = pl.program_id(0)
    place_rows(x_all, info[0], (x0, x1, x2, x3))
    live = live_row(info[1], step * WIDE, WIDE)
    parts = jnp.concatenate([m0[...], m1[...], m2[...], m3[...]], axis=0)
    out = dot3(get(wo_hi, wo_lo), split(parts), NN)
    inner = x_all[...] + live * (out + cols[:, 2:3])
    x_all[...] = inner
    inner_own[...] = take_rows(x_all, info[0], x0.shape[0])
    mean, scale = column_stats(inner)
    stats[0:1, :] = scale
    unit = (inner - mean) * scale
    normed = split(unit * cols[:, 3:4] + cols[:, 4:5])
    n_hi[...], n_lo[...] = normed
    pre = dot3(get(wu_hi, wu_lo), normed, NN) + up_bias[...]
    root = 0.7978845608028654
    cubic = 0.044715
    square = pre * pre
    bent = jnp.tanh(root * pre * (1.0 + cubic * square))
    put(act_hi, act_lo, 0.5 * pre * (1.0 + bent))
    slope[...] = 0.5 * (1.0 + bent) + 0.5 * pre * (1.0 - bent * bent) * (
        root * (1.0 + 3.0 * cubic * square)
    )


def parted(rows, info):
    step = rows // 4
    for half in range(2):
        bit = info[2 + half]
        yield pl.multiple_of((2 * half + bit) * step, step)
        yield pl.multiple_of((2 * half + 1 - bit) * step, step)


def outer_kernel(info, a_hi, a_lo, b_hi, b_lo, *rest):
    outs, (s_hi, s_lo) = rest[:4], rest[4:]
    rows = a_hi.shape[0]
    step = rows // 4

    @pl.when(pl.program_id(0) == 0)
    def _():
        for at, start in enumerate(parted(rows, info)):
            here = slice(at * step, (at + 1) * step)
            s_hi[here, :] = a_hi[pl.ds(start, step), :]
            s_lo[here, :] = a_lo[pl.ds(start, step), :]

    grad = dot3(get(s_hi, s_lo), get(b_hi, b_lo), NT)
    for at, out in enumerate(outs):
        out[...] = grad[at * step : (at + 1) * step]


def down_grad_kernel(info, a_hi, a_lo, c0, c1, c2, c3, *rest):
    outs, (c_hi, c_lo, own_sum, s_hi, s_lo, c_all) = rest[:4], rest[4:]
    rows = a_hi.shape[0]
    step = rows // 4
    live = live_row(info[1], 0, c_all.shape[1])
    for at, start in enumerate(parted(rows, info)):
        here = slice(at * step, (at + 1) * step)
        s_hi[here, :] = a_hi[pl.ds(start, step), :]
        s_lo[here, :] = a_lo[pl.ds(start, step), :]
    place_rows(c_all, info[0], (c0, c1, c2, c3))
    put(c_hi, c_lo, c_all[...] * live)
    own_sum[...] = fold(c0[...] * live)
    grad = dot3(get(s_hi, s_lo), get(c_hi, c_lo), NT)
    for at, out in enumerate(outs):
        out[...] = grad[at * step : (at + 1) * step]


def order_pair(bit, first, second, keep, send):
    keep[...] = jnp.where(bit == 0, first, second)
    send[...] = jnp.where(bit == 0, second, first)


def projection_grads_kernel(
    info, mixed, b_hi, b_lo, q_hi, q_lo, kv_hi, kv_lo, n_hi, n_lo, keep_0, send_0, keep_1, send_1
):
    rows = mixed.shape[0]
    normed = get(n_hi, n_lo)
    d_out = dot3(split(mixed[...]), get(b_hi, b_lo), NT)
    left = (
        jnp.concatenate([q_hi[...], kv_hi[...]], axis=0),
        jnp.concatenate([q_lo[...], kv_lo[...]], axis=0),
    )
    d_qkv = dot3(left, normed, NT)
    order_pair(info[2], d_out, d_qkv[:rows], keep_0, send_0)
    order_pair(info[3], d_qkv[rows : 2 * rows], d_qkv[2 * rows :], keep_1, send_1)


def projection_done_kernel(info, h_0, c_0, h_1, c_1, d_out, d_query, d_key, d_value):
    order_pair(info[2], h_0[...], c_0[...], d_out, d_query)
    order_pair(info[3], h_1[...], c_1[...], d_key, d_value)


def halve_kernel(places, info, *refs):
    count = len(places)
    for i, at in enumerate(places):
        kept, come = refs[2 * i], refs[2 * i + 1]
        mine, send = refs[2 * count + 2 * i], refs[2 * count + 2 * i + 1]
        rows = mine.shape[0]
        mine[...] = take_rows(kept, info[at], rows) + take_rows(come, info[at], rows)
        send[...] = take_rows(kept, 1 - info[at], rows) + take_rows(come, 1 - info[at], rows)


def add_kernel(info, *refs):
    count = len(refs) // 3
    for i in range(count):
        refs[2 * count + i][...] = refs[2 * i][...] + refs[2 * i + 1][...]


def pack_kernel(info, *refs):
    rows = refs[0].shape[0]
    refs[4][:rows, :] = refs[0][...] + refs[1][...]
    refs[4][rows:, :] = refs[2][...] + refs[3][...]


def unpack_kernel(info, held, come, first, second):
    rows = first.shape[0]
    first[...] = held[:rows, :] + come[:rows, :]
    second[...] = held[rows:, :] + come[rows:, :]


def join_kernel(places, merged, info, *refs):
    count = len(places)
    for i, at in enumerate(places):
        held, come = refs[2 * i], refs[2 * i + 1]
        out = refs[2 * count] if merged else refs[2 * count + i]
        rows = held.shape[0]
        base = 2 * i if merged else 0
        out[pl.ds(pl.multiple_of((base + info[at]) * rows, rows), rows), :] = held[...]
        out[pl.ds(pl.multiple_of((base + 1 - info[at]) * rows, rows), rows), :] = come[...]


def lane_sums_kernel(*refs):
    ins, out = refs[:-1], refs[-1]
    wide = jnp.concatenate([ref[...] for ref in ins], axis=0)
    high, rest = split(wide)
    low = (wide - high.astype(F32) - rest.astype(F32)).astype(BF16)
    ones = jnp.ones((8, wide.shape[1]), BF16)

    def one(part):
        return lax.dot_general(ones, part, NT, preferred_element_type=F32)

    sums = one(high) + (one(rest) + one(low))
    width = out.shape[1]
    out[...] = jnp.zeros_like(out)
    for at in range(0, sums.shape[1], width):
        part = sums[0:1, at : at + width]
        out[at // width : at // width + 1, : part.shape[1]] = part


def part_halves(grid, place, keep, send):
    rows = grid.shape[0] // 4
    core = place & 1
    for far in range(2):
        here = slice(far * rows, (far + 1) * rows)
        keep[here, :] = take_rows(grid, 2 * far + core, rows)
        send[here, :] = take_rows(grid, 2 * far + 1 - core, rows)


def hidden_back_kernel(
    info, c_hi, c_lo, wd_hi, wd_lo, slope, wu_hi, wu_lo, d_hi, d_lo, keep, send, bias_sum, grid
):
    @pl.when(pl.program_id(0) == 0)
    def _():
        bias_sum[...] = jnp.zeros_like(bias_sum)

    d_pre = dot3(get(wd_hi, wd_lo), get(c_hi, c_lo), NN) * slope[...]
    bias_sum[...] += fold(d_pre)
    parts = split(d_pre)
    d_hi[...], d_lo[...] = parts
    grid[...] = dot3(get(wu_hi, wu_lo), parts, NN)
    part_halves(grid, info[0], keep, send)


def down_kernel(info, wd_hi, wd_lo, act_hi, act_lo, keep, send, grid):
    grid[...] = dot3(get(wd_hi, wd_lo), get(act_hi, act_lo), NN)
    part_halves(grid, info[0], keep, send)


def inner_back_kernel(
    info, half, other, n_hi, n_lo, stats, cols, c0, c1, c2, c3, w_out, f_query, f_numer, quotient,
    b_hi, b_lo, dq_hi, dq_lo, dp_hi, dp_lo, inner_own, sum_gain, sum_bias, sum_out, sum_query,
    c_all, d_all, normal, wo_hi, wo_lo,
):
    step = pl.program_id(0)
    place = info[0]
    core = place & 1
    chans = c0.shape[0]
    place_rows(c_all, place, (c0, c1, c2, c3))
    for far in range(2):
        here = slice(far * chans, (far + 1) * chans)
        d_all[pl.ds(pl.multiple_of((2 * far + core) * chans, chans), chans), :] = half[here, :]
        d_all[pl.ds(pl.multiple_of((2 * far + 1 - core) * chans, chans), chans), :] = other[here, :]
    live = live_row(info[1], step * WIDE, WIDE)
    scaled = d_all[...] * cols[:, 3:4]
    unit = (n_hi[...].astype(F32) + n_lo[...].astype(F32) - cols[:, 4:5]) * (1.0 / cols[:, 3:4])
    normal[...] = unit
    mean_one = jnp.mean(scaled, axis=0, keepdims=True)
    mean_two = jnp.mean(scaled * unit, axis=0, keepdims=True)
    d_inner = c_all[...] + stats[0:1, :] * (scaled - mean_one - unit * mean_two)
    c_all[...] = d_inner
    own = take_rows(c_all, place, chans)
    inner_own[...] = own
    d_own = take_rows(d_all, place, chans)

    @pl.when(step == 0)
    def _():
        put(wo_hi, wo_lo, w_out[...])
        for total in (sum_gain, sum_bias, sum_out, sum_query):
            total[...] = jnp.zeros_like(total)

    sum_gain[...] += fold(d_own * take_rows(normal, place, chans))
    sum_bias[...] += fold(d_own)
    sum_out[...] += fold(own * live)
    branch = split(d_inner * live)
    b_hi[...], b_lo[...] = branch
    d_mixed = dot3(get(wo_hi, wo_lo), branch, NN)
    d_query = d_mixed * f_query[...]
    sum_query[...] += fold(d_query)
    put(dq_hi, dq_lo, d_query)
    d_numer = d_mixed * f_numer[...]
    put(dp_hi, dp_lo, jnp.concatenate([d_numer, -d_numer * quotient[...]], axis=0))


def mix_back_kernel(
    d_hi, d_lo, before_hi, before_lo, here_hi, here_lo, band_hi, band_lo, bias,
    kv_hi, kv_lo, d_bias, sum_value,
    carry, later, ahead,
):
    step = pl.program_id(0)
    block = pl.num_programs(0) - 1 - step
    window = TB
    chans = d_hi.shape[0] // 2

    @pl.when(step == 0)
    def _():
        for total in (carry, later, ahead, sum_value):
            total[...] = jnp.zeros_like(total)

    d_pair = get(d_hi, d_lo)
    d_wide = d_pair[0].astype(F32) + d_pair[1].astype(F32)
    into = dot3(d_pair, get(band_hi, band_lo), NN)
    back = into[:, window:] + carry[...] + later[:, 0:1]
    carry[...] = into[:, :window]
    later[...] = later[...] + ahead[...]
    ahead[...] = jnp.broadcast_to(jnp.sum(d_wide, axis=1, keepdims=True), ahead.shape)
    turned = split(d_wide.T)
    right = dot3(turned, get(here_hi, here_lo), NN)
    left = dot3(turned, get(before_hi, before_lo), NN)
    left = jnp.where(block == 0, 0.0, left)
    wide = jnp.concatenate([reverse_lanes(right), reverse_lanes(left)], axis=1)
    placed = pltpu.roll(wide, window + 1, 1, stride=1, stride_axis=0)
    d_bias[...] = placed[:, :window] * jnp.exp(bias[...])
    pair = here_hi[...].astype(F32) + here_lo[...].astype(F32)
    d_value = pair[chans:] * back[:chans]
    d_key = pair[:chans] * back[:chans] + pair[chans:] * back[chans:]
    sum_value[...] += fold(d_value)
    put(kv_hi, kv_lo, jnp.concatenate([d_key, d_value], axis=0))


def project_back_kernel(
    info, dq_hi, dq_lo, kv_hi, kv_lo, w_hi, w_lo, x0, x1, x2, x3, stats, cols, d_pair, keep, send,
    x_all, grid,
):
    place_rows(x_all, info[0], (x0, x1, x2, x3))
    d_all = (
        jnp.concatenate([dq_hi[...], kv_hi[...]], axis=0),
        jnp.concatenate([dq_lo[...], kv_lo[...]], axis=0),
    )
    terms = dot3(get(w_hi, w_lo), d_all, NN)
    grid[...] = terms
    part_halves(grid, info[0], keep, send)
    scaled = terms * cols[:, 0:1]
    unit = (x_all[...] - stats[0:1, :]) * stats[1:2, :]
    at = grid.shape[0] // 2
    sums = (jnp.sum(scaled, axis=0, keepdims=True), jnp.sum(scaled * unit, axis=0, keepdims=True))
    sums = jnp.concatenate([*sums, jnp.zeros((6, grid.shape[1]), F32)], axis=0)
    rows, window = d_pair.shape[0] // 8, d_pair.shape[1]
    for out, core in ((keep, info[4]), (send, 1 - info[4])):
        out[at : at + 8, :] = sums
        for block in range(grid.shape[1] // window):
            start = 4 * rows * core + rows * (grid.shape[1] // window * pl.program_id(0) + block)
            lanes = slice(block * window, (block + 1) * window)
            out[at + 8 :, lanes] = d_pair[pl.ds(pl.multiple_of(start, rows), rows), :]


def core_halves_kernel(info, keep, come, mine_a, send_a, mine_b, send_b):
    rows = mine_b.shape[0]
    at = 4 * rows
    for out_a, out_b, far in ((mine_a, mine_b, info[5]), (send_a, send_b, 1 - info[5])):
        out_a[:rows, :] = take_rows(keep, 2 * far, rows) + take_rows(come, 2 * far, rows)
        out_b[...] = take_rows(keep, 2 * far + 1, rows) + take_rows(come, 2 * far + 1, rows)
        out_a[rows : rows + 8, :] = keep[at : at + 8, :] + come[at : at + 8, :]
        half = keep[at + 8 :, :] + come[at + 8 :, :]
        wide = half.shape[1] // 2
        part = jnp.where(far == 0, half[:, :wide], half[:, wide:])
        tall = part.shape[0] // 2
        out_a[rows + 8 :, :wide] = part[:tall]
        out_a[rows + 8 :, wide:] = part[tall:]


def chip_sum_kernel(info, mine, come, pair, sums):
    rows = mine.shape[0] - pair.shape[0] - 8
    sums[...] = mine[rows : rows + 8, :] + come[rows : rows + 8, :]
    pair[...] = mine[rows + 8 :, :] + come[rows + 8 :, :]


def pair_small_kernel(info, pair, come, small, out):
    rows = pair.shape[0]
    out[:rows, :] = pair[...] + come[...]
    out[rows:, :] = small[...]


def pair_small_sum_kernel(info, held, come, pair, small):
    rows = pair.shape[0]
    pair[...] = held[:rows, :] + come[:rows, :]
    small[...] = held[rows:, :] + come[rows:, :]


def pair_chips_kernel(info, own, other, half):
    tall, wide = own.shape[0], own.shape[1] // 2
    for low, lanes in ((True, slice(0, wide)), (False, slice(wide, 2 * wide))):
        near = info[5] == (0 if low else 1)
        for top in range(2):
            here = slice(top * wide, (top + 1) * wide)
            half[top * tall : (top + 1) * tall, lanes] = jnp.where(near, own[:, here], other[:, here])


def pair_cores_kernel(info, own, other, d_pair):
    rows, window = own.shape[0], d_pair.shape[1]
    for half, core in ((own, info[4]), (other, 1 - info[4])):
        for block in range(4):
            start = 4 * rows * core + rows * block
            d_pair[pl.ds(pl.multiple_of(start, rows), rows), :] = half[:, block * window : (block + 1) * window]


def input_back_kernel(model, mine_a, come_a, mine_b, come_b, inner_own, x_own, stats, sums, gain, d_in, sum_gain, sum_bias):
    rows = mine_b.shape[0]
    d_normed = jnp.concatenate([mine_a[:rows, :] + come_a[:rows, :], mine_b[...] + come_b[...]], axis=0)
    unit = (x_own[...] - stats[0:1, :]) * stats[1:2, :]

    @pl.when(pl.program_id(0) == 0)
    def _():
        for total in (sum_gain, sum_bias):
            total[...] = jnp.zeros_like(total)

    sum_gain[...] += fold(d_normed * unit)
    sum_bias[...] += fold(d_normed)
    d_in[...] = inner_own[...] + stats[1:2, :] * (
        d_normed * gain[...] - sums[0:1, :] / model - unit * (sums[1:2, :] / model)
    )


def swap(block, bit):
    return lax.ppermute(block, "mp", [(i, i ^ bit) for i in range(4)])


def gather_parts(own):
    far = swap(own, 2)
    near = swap(own, 1)
    return own, near, far, swap(far, 1)


def in_order(parts, place):
    stacked = jnp.stack(parts)
    return jnp.concatenate(
        [lax.dynamic_index_in_dim(stacked, place ^ i, 0, keepdims=False) for i in range(4)], axis=0
    )


def after(value, *earlier):
    return lax.optimization_barrier((value, earlier))[0]


def trade(block, flip):
    size = lax.axis_size("dp")
    return lax.ppermute(block, "dp", [(i, i ^ flip) for i in range(size)])


def glue(kernel, scalars, ins, outs, name, steps=1):
    def columns(shape):
        return pl.BlockSpec((shape[0], shape[1] // steps), lambda i: (0, i))

    return call(
        kernel, steps,
        [scalars, *[(x, columns(x.shape)) for x in ins]],
        [(shaped(shape), columns(shape)) for shape in outs],
        name=name,
        pin=False,
        pin_out=PIN_GLUE,
    )


def add_trade(block, flip, *gate):
    if lax.axis_size("dp") != 8:
        return jnp.zeros_like(block)
    return trade(after(block, *gate), flip)


def settle(sums, arrived, *gates):
    comes = [s.come for s in sums]
    comes, arrived, _ = lax.optimization_barrier((comes, arrived, gates))
    for s, come in zip(sums, comes):
        s.come = come
        if s.stage < 4:
            s.take()
    return arrived


class Sum:
    FLIPS = ((1, 2), (2, 1), (4,), (2, 1), (1, 2))

    def __init__(self, scalars, blocks, merged):
        self.merged = merged
        self.come = []
        self.scalars = scalars
        self.direct = lax.axis_size("dp") != 8
        self.stage = 0
        if self.direct:
            self.total = lax.psum(blocks, "dp")
            if merged:
                self.total = [jnp.concatenate(self.total, axis=0)]
            self.out = self.total
        else:
            self.mine, self.out = blocks[0::2], blocks[1::2]

    def send(self, *gate):
        if not self.direct:
            pairs = zip(self.out, self.FLIPS[self.stage])
            self.come = [trade(after(block, *gate), flip) for block, flip in pairs]

    def finish(self, *gate):
        if not self.direct:
            self.mine = after(self.mine, *gate)
            self.take()
        return self.total

    def take(self):
        if self.direct:
            return
        ins = [x for pair in zip(self.mine, self.come) for x in pair]
        rows, width = self.mine[0].shape
        name = f"sum_stage_{self.stage}"
        if self.stage == 0:
            half = (rows // 2, width)
            got = glue(partial(halve_kernel, (3, 2)), self.scalars, ins, [half] * 4, name, 2)
            self.mine, self.out = got[0::2], got[1::2]
        elif self.stage == 1:
            self.mine = self.out = glue(pack_kernel, self.scalars, ins, [(2 * rows, width)], name)
        elif self.stage == 2:
            self.mine = self.out = glue(unpack_kernel, self.scalars, ins, [(rows // 2, width)] * 2, name)
        elif self.stage == 3:
            kernel = partial(join_kernel, (3, 2), False)
            self.mine = self.out = glue(kernel, self.scalars, ins, [(2 * rows, width)] * 2, name)
        else:
            shapes = [(4 * rows, width)] if self.merged else [(rows, width)] * 4
            kernel = partial(join_kernel, (2, 3), True) if self.merged else projection_done_kernel
            self.out = self.total = glue(kernel, self.scalars, ins, shapes, name, 2)
        self.stage += 1


def body(
    inputs,
    lengths,
    ln1_gain,
    ln1_bias,
    w_query,
    w_key,
    w_value,
    query_bias,
    value_bias,
    pair_bias,
    w_out,
    out_bias,
    ln2_gain,
    ln2_bias,
    w_up,
    up_bias,
    w_down,
    down_bias,
    cotangent,
):
    seq_rows, span, chans = inputs.shape
    window = pair_bias.shape[1]
    model = 4 * chans
    units = w_up.shape[1]
    steps = span // WIDE
    blocks = span // TB
    assert seq_rows == 1 and window == TB
    place = lax.axis_index("mp")
    row = lax.axis_index("dp")
    halving = lax.axis_size("dp") == 8
    bits = [row % 2, (row // 2) % 2] if halving else [jnp.int32(0)] * 2
    info = jnp.stack([place.astype(jnp.int32), lengths[0], *bits, place % 2, place // 2])

    x_own = inputs[0].T
    x_far = swap(x_own, 2)
    x_near = swap(x_own, 1)
    vectors = jnp.stack([ln1_gain, ln1_bias, out_bias, ln2_gain, ln2_bias, query_bias, value_bias])
    vectors = jnp.pad(vectors, ((0, 1), (0, 256 - chans)))
    v_far = swap(vectors, 2)
    v_near = swap(vectors, 1)

    band = call(
        band_kernel, blocks,
        [(pair_bias, pl.BlockSpec((TB, window), lambda i: (i, 0)))],
        [(shaped((span, 2 * window), BF16), pl.BlockSpec((TB, 2 * window), lambda i: (i, 0)))] * 2,
        name="band",
    )
    wide_qkv, tall_qkv = (3 * chans, model), (model, 3 * chans)
    up_dims, down_dims = (model, units), (units, model)

    def prepare(kernel, ins, dims, name):
        return call(
            kernel, 1, [(w, whole(w.shape)) for w in ins], [(shaped(d, BF16), whole(d)) for d in dims for _ in range(2)], name=name
        )

    wq_hi, wq_lo, wqt_hi, wqt_lo = prepare(
        qkv_weights_kernel, [w_query.T, w_key.T, w_value.T], [wide_qkv, tall_qkv], "qkv_weights"
    )
    wu_hi, wu_lo, wut_hi, wut_lo = prepare(weights_kernel, [w_up], [up_dims, down_dims], "up_weights")
    up_column, gain_column = up_bias[:, None], ln1_gain[:, None]
    v_far, x_far, up_column, gain_column = lax.optimization_barrier(
        (v_far, x_far, up_column, gain_column, band, wq_hi, wu_hi)
    )[:4]
    x_parts = (x_own, x_near, x_far, swap(x_far, 1))
    v_parts = (vectors, v_near, v_far, swap(v_far, 1))
    wo_own = after(w_out, x_far, v_far)
    wo_far = swap(wo_own, 2)
    wo_near = swap(w_out, 1)

    thin = (shaped((chans, span)), across(chans))
    tall_half = (shaped((model, span), BF16), across(model))
    hid_half = (shaped((units, span), BF16), across(units))
    pair_half = (shaped((2 * chans, span), BF16), across(2 * chans))
    thin_half = (shaped((chans, span), BF16), across(chans))
    rows8 = (shaped((8, span)), across(8))
    x_ins = [(x, across(chans)) for x in x_parts]
    scalars = (info, SCALARS)

    cols_out = (shaped((model, 8)), whole((model, 8)))
    cols, mixed, quotient, f_query, f_numer, pair_hi, pair_lo, n1_hi, n1_lo, stats_one = call(
        attend_kernel, steps,
        [scalars, *x_ins, *[(v, whole((8, 256))) for v in v_parts], (wq_hi, whole(wide_qkv)), (wq_lo, whole(wide_qkv))]
        + [(b, pl.BlockSpec((WIDE, 2 * window), lambda i: (i, 0))) for b in band],
        [cols_out, thin, thin, thin, thin, pair_half, pair_half, tall_half, tall_half, rows8],
        [
            pltpu.VMEM((model, WIDE), F32),
            pltpu.VMEM((2 * chans, 128), F32),
            pltpu.VMEM((2 * chans, TB), BF16),
            pltpu.VMEM((2 * chans, TB), BF16),
        ],
        name="attend",
        pin=PIN_ATT,
    )

    cols_in = (cols, whole((model, 8)))
    mixed_far = swap(mixed, 2)
    mixed_near = swap(mixed, 1)
    wo_parts = (w_out, wo_near, wo_far, swap(wo_far, 1))
    wot_hi, wot_lo = prepare(out_weights_kernel, wo_parts, [(model, model)], "out_weights")
    wd_hi, wd_lo, wdt_hi, wdt_lo = prepare(weights_kernel, [w_down], [down_dims, up_dims], "down_weights")
    mixed_far = after(mixed_far, wot_hi, wd_hi)
    mixed_parts = (mixed, mixed_near, mixed_far, swap(mixed_far, 1))
    cot_own = cotangent[0].T
    cot_far = swap(after(cot_own, mixed_far), 2)
    cot_near = swap(cot_own, 1)
    lanes_own = (shaped((chans, 128)), whole((chans, 128)))

    act_hi, act_lo, slope, n2_hi, n2_lo, inner_own, stats_two = call(
        hidden_kernel, steps,
        [scalars, *[(p, across(chans)) for p in mixed_parts], *x_ins, cols_in]
        + [(wot_hi, whole((model, model))), (wot_lo, whole((model, model)))]
        + [(wut_hi, whole(down_dims)), (wut_lo, whole(down_dims)), (up_column, whole((units, 1)))],
        [hid_half, hid_half, (shaped((units, span)), across(units)), tall_half, tall_half, thin, rows8],
        [pltpu.VMEM((model, WIDE), F32)],
        name="hidden",
        pin=PIN_HIN,
        pin_out=PIN_HID,
    )

    cot_far = after(cot_far, act_hi)
    cot_parts = (cot_own, cot_near, cot_far, swap(cot_far, 1))
    cot_ins = [(c, across(chans)) for c in cot_parts]
    def outer(a_hi, a_lo, b_hi, b_lo, name, steps=2):
        rows, inner_len = a_hi.shape
        deep = b_hi.shape[0]
        left = whole((rows, inner_len))
        right = pl.BlockSpec((deep // steps, inner_len), lambda i: (i, 0))
        part = (shaped((rows // 4, deep)), across(rows // 4, deep // steps))
        grads = call(
            outer_kernel, steps,
            [scalars, (a_hi, left), (a_lo, left), (b_hi, right), (b_lo, right)],
            [part] * 4,
            [pltpu.VMEM((rows, inner_len), BF16)] * 2,
            name=name,
            pin=PIN_UG,
            pin_out=PIN_GO,
        )
        return Sum(scalars, grads, True)

    whole_half = (shaped((model, span), BF16), whole((model, span)))
    block = (shaped((units // 4, model)), whole((units // 4, model)))
    *grads, c_hi, c_lo, s_down = call(
        down_grad_kernel, 1,
        [scalars, (act_hi, whole((units, span))), (act_lo, whole((units, span))), *[(c, whole((chans, span))) for c in cot_parts]],
        [block] * 4 + [whole_half, whole_half, lanes_own],
        [pltpu.VMEM((units, span), BF16)] * 2 + [pltpu.VMEM((model, span), F32)],
        name="down_grad",
        pin=PIN_DG,
        pin_out=PIN_GO,
    )
    g_down = Sum(scalars, grads, True)
    g_down.send()
    c_hi, c_lo = after((c_hi, c_lo), g_down.out)
    half_out = (shaped((2 * chans, span)), across(2 * chans))
    half_shape = (2 * chans, span)
    dpre_hi, dpre_lo, keep, send, s_up = call(
        hidden_back_kernel, steps,
        [scalars, (c_hi, across(model)), (c_lo, across(model)), (wd_hi, whole(down_dims)), (wd_lo, whole(down_dims))]
        + [(slope, across(units)), (wu_hi, whole(up_dims)), (wu_lo, whole(up_dims))],
        [hid_half, hid_half, half_out, half_out, (shaped((units, 128)), whole((units, 128)))],
        [pltpu.VMEM((model, WIDE), F32)],
        name="hidden_back",
        pin=PIN_HB,
        pin_out=PIN_MID,
    )
    send = settle([g_down], send, keep)
    half = glue(add_kernel, scalars, [keep, swap(after(send, g_down.out), 1)], [half_shape], "core_sum", 2)[0]
    half_far = swap(half, 2)
    g_down.send(half)
    g_up = outer(after(n2_hi, half), n2_lo, dpre_hi, dpre_lo, "up_grad")
    settle([g_down], [], g_up.out)
    g_down.send()
    g_up.send(g_down.out)
    keep_down, send_down = call(
        down_kernel, steps,
        [scalars, (wdt_hi, whole(up_dims)), (wdt_lo, whole(up_dims)), (after(act_hi, g_down.out), across(units)), (act_lo, across(units))],
        [half_out, half_out],
        [pltpu.VMEM((model, WIDE), F32)],
        name="down",
        pin=False,
        pin_out=PIN_MID,
    )
    half_far, send_down = settle([g_down, g_up], (half_far, send_down), keep_down)
    half = glue(add_kernel, scalars, [half, half_far], [half_shape], "chip_sum", 2)[0]
    half = after(half, g_down.out, g_up.out)
    other = swap(half, 1)
    own_shape = (chans, span)
    g_down.send(other)
    g_up.send(other)
    core_down = swap(after(send_down, other), 1)

    b_hi, b_lo, dq_hi, dq_lo, dp_hi, dp_lo, d_inner_own, s_gain2, s_bias2, s_out, s_query = call(
        inner_back_kernel, steps,
        [scalars, (half, across(2 * chans)), (other, across(2 * chans)), (n2_hi, across(model)), (n2_lo, across(model)), (stats_two, across(8)), cols_in]
        + cot_ins
        + [(w_out, whole((chans, model)))]
        + [(f_query, across(chans)), (f_numer, across(chans)), (quotient, across(chans))],
        [tall_half, tall_half, thin_half, thin_half, pair_half, pair_half, thin, lanes_own, lanes_own, lanes_own, lanes_own],
        [pltpu.VMEM((model, WIDE), F32)] * 3 + [pltpu.VMEM((chans, model), BF16)] * 2,
        name="inner_back",
        pin=PIN_IB,
        pin_out=PIN_MID,
    )
    dp_hi, core_down = settle([g_down, g_up], (dp_hi, core_down), b_hi)
    mine_down, send_down = glue(
        partial(halve_kernel, (5,)), scalars, [keep_down, core_down], [own_shape] * 2, "down_halves", 2
    )
    g_down.send()
    g_up.send()
    come_down = swap(after(send_down, g_down.out, g_up.out), 2)
    dp_hi = after(dp_hi, g_down.out, g_up.out)
    thin_all, tall_all = whole((chans, span)), whole((model, span))

    def back_at(i):
        return blocks - 1 - i

    pair_spec = pl.BlockSpec((2 * chans, TB), lambda i: (0, back_at(i)))
    prev_spec = pl.BlockSpec((2 * chans, TB), lambda i: (0, jnp.maximum(back_at(i) - 1, 0)))
    band_spec = pl.BlockSpec((TB, 2 * window), lambda i: (back_at(i), 0))
    row_spec = pl.BlockSpec((TB, window), lambda i: (back_at(i), 0))
    kv_hi, kv_lo, d_pair, s_value = call(
        mix_back_kernel, blocks,
        [(dp_hi, pair_spec), (dp_lo, pair_spec), (pair_hi, prev_spec), (pair_lo, prev_spec), (pair_hi, pair_spec), (pair_lo, pair_spec)]
        + [(band[0], band_spec), (band[1], band_spec), (pair_bias, row_spec)],
        [(shaped((2 * chans, span), BF16), pair_spec)] * 2 + [(shaped((span, window)), row_spec), lanes_own],
        [pltpu.VMEM((2 * chans, TB), F32), pltpu.VMEM((2 * chans, 128), F32), pltpu.VMEM((2 * chans, 128), F32)],
        name="mix_back",
        pin=PIN_MB,
        pin_out=PIN_MID,
    )
    slab = pl.BlockSpec((model // 2, span), lambda i: (i, 0))
    grads = call(
        projection_grads_kernel, 2,
        [scalars, (mixed, thin_all), (b_hi, slab), (b_lo, slab), (dq_hi, thin_all), (dq_lo, thin_all)]
        + [(kv_hi, whole((2 * chans, span))), (kv_lo, whole((2 * chans, span))), (n1_hi, slab), (n1_lo, slab)],
        [(shaped((chans, model)), across(chans, model // 2))] * 4,
        name="projection_grads", pin=PIN_PG, pin_out=PIN_GO,
    )
    g_mix = Sum(scalars, grads, False)
    dq_hi, kv_hi = after((dq_hi, kv_hi), grads)
    payload_rows = 2 * chans + 8 + span // 8
    payload = (shaped((payload_rows, span)), across(payload_rows))
    keep, send = call(
        project_back_kernel, steps,
        [scalars, (dq_hi, across(chans)), (dq_lo, across(chans)), (kv_hi, across(2 * chans)), (kv_lo, across(2 * chans))]
        + [(wqt_hi, whole(tall_qkv)), (wqt_lo, whole(tall_qkv)), *x_ins, (stats_one, across(8)), cols_in, (d_pair, whole((span, window)))],
        [payload, payload],
        [pltpu.VMEM((model, WIDE), F32)] * 2,
        name="project_back",
        pin=PIN_PB,
        pin_out=PIN_MID,
    )
    send, come_down = settle([g_down, g_up], (send, come_down), keep, grads)
    g_up.send(send)
    come = settle([g_up], swap(after(send, g_up.out), 1))
    rest_shape = (chans // 2, span)
    mine, send, mine_rest, send_rest = glue(
        core_halves_kernel, scalars, [keep, come], [(chans // 2 + 8 + span // 16, span)] * 2 + [rest_shape] * 2, "core_halves"
    )
    send = after(send, send_rest, g_up.out)
    g_mix.send(send)
    come = settle([g_mix], swap(send, 2))
    quarter = (span // 16, span)
    pair_sum, sums = glue(chip_sum_kernel, scalars, [mine, come], [quarter, (8, span)], "chip_sums")
    come, sums, pair_sum = after((come, sums, pair_sum), g_mix.out)
    come, sums, pair_sum = lax.optimization_barrier((come, sums, pair_sum))
    g_mix.send(pair_sum)
    come_rest, pair_come = settle([g_mix], (swap(after(send_rest, pair_sum), 2), add_trade(pair_sum, 4)))
    pair_sum = glue(add_kernel, scalars, [pair_sum, pair_come], [quarter], "pair_far")[0]
    pair_sum, come_rest = after((pair_sum, come_rest), g_mix.out)
    g_mix.send(pair_sum)
    g_up.send(pair_sum)
    d_inputs, s_gain1, s_bias1 = call(
        partial(input_back_kernel, float(model)), steps,
        [(x, across(x.shape[0])) for x in (mine, come, mine_rest, come_rest, d_inner_own, x_own, stats_one, sums)]
        + [(gain_column, whole((chans, 1)))],
        [thin, lanes_own, lanes_own],
        name="input_back",
        pin=False,
        pin_out=PIN_MID,
    )
    lanes = (s_gain1, s_bias1, s_query, s_value, s_out, s_gain2, s_bias2, s_down, s_up)
    count = sum(x.shape[0] for x in lanes)
    small = call(
        lane_sums_kernel, 1, [(x, whole(x.shape)) for x in lanes], [(shaped((8, span)), whole((8, span)))],
        name="lane_sums", pin=False,
    )[0]
    sum_down = g_down.finish(pair_sum)[0]
    live = (jnp.arange(span, dtype=jnp.int32) < lengths[0]).astype(F32)[None, :]
    result = inner_own + live * (mine_down + after(come_down, pair_sum) + down_bias[:, None])
    pair_come, small, sum_down, result = settle([g_mix, g_up], (add_trade(pair_sum, 1), small, sum_down, result))
    packed = (span // 16 + 8, span)
    packed_sum = glue(pair_small_kernel, scalars, [pair_sum, pair_come, small], [packed], "pair_x")[0]
    packed_sum = after(packed_sum, g_mix.out)
    g_mix.send(packed_sum)
    come = settle([g_mix], add_trade(packed_sum, 2))
    pair_sum, small = glue(pair_small_sum_kernel, scalars, [packed_sum, come], [quarter, (8, span)], "pair_z")
    small, pair_sum = after((small, pair_sum), g_mix.out)
    g_mix.send(small, pair_sum)
    sum_up = g_up.finish(small)[0]
    small_come, pair_come, sum_up = settle([g_mix], (add_trade(small, 4), swap(pair_sum, 2), sum_up))
    pair_half = glue(pair_chips_kernel, scalars, [pair_sum, pair_come], [(span // 8, span)], "pair_chips")[0]
    small = glue(add_kernel, scalars, [small, small_come], [(8, span)], "small_far")[0]
    small, pair_half = lax.optimization_barrier((small, pair_half))
    pair_come = swap(pair_half, 1)
    small = (small + add_trade(small, 1)).reshape(-1)[:count]
    d_w_out, d_w_query, d_w_key, d_w_value = g_mix.finish(pair_half)
    d_pair = glue(pair_cores_kernel, scalars, [pair_half, pair_come], [(span, window)], "pair_cores")[0]
    if not halving:
        d_pair = lax.psum(d_pair, "dp")
        small = lax.psum(small, "dp")
    vecs = [small[i * chans : (i + 1) * chans] for i in range(8)]
    return (
        result.T[None],
        d_inputs.T[None],
        vecs[0],
        vecs[1],
        d_w_query.T,
        d_w_key.T,
        d_w_value.T,
        vecs[2],
        vecs[3],
        d_pair,
        d_w_out,
        vecs[4],
        vecs[5],
        vecs[6],
        sum_up,
        small[8 * chans :],
        sum_down,
        vecs[7],
    )


def solution(mesh):
    rows = P("dp", None, "mp")
    vec = P("mp")
    out_dim = P(None, "mp")
    in_dim = P("mp", None)
    return jax.shard_map(
        body,
        mesh=mesh,
        in_specs=(
            rows, P("dp"), vec, vec, out_dim, out_dim, out_dim, vec, vec, P(), in_dim, vec, vec, vec,
            out_dim, vec, in_dim, vec, rows,
        ),
        out_specs=(
            rows, rows, vec, vec, out_dim, out_dim, out_dim, vec, vec, P(), in_dim, vec, vec, vec,
            out_dim, vec, in_dim, vec,
        ),
        check_vma=False,
    )
```

```python
import math
from functools import partial

import jax
import jax.numpy as jnp
from jax import lax
from jax.experimental import pallas as pl
from jax.experimental.pallas import tpu as pltpu
from jax.sharding import PartitionSpec as P

EPSILON = 1e-05
TB = 256
WIDE = 512
SCALE = 0.0
FIRST_ROWS = 64
PIN_MID = True
PIN_HB = False
PIN_MB = False
PIN_IB = False
PIN_PB = False
PIN_PG = False
PIN_UG = False
PIN_GO = False
PIN_GLUE = False
PIN_ATT = True
PIN_HIN = True
PIN_DG = False
PIN_HID = False
NN = (((1,), (0,)), ((), ()))
NT = (((1,), (1,)), ((), ()))
F32 = jnp.float32
BF16 = jnp.bfloat16


def split(wide):
    high = wide.astype(BF16)
    return high, (wide - high.astype(F32)).astype(BF16)


def dot3(left, right, dims):
    def one(a, b):
        return lax.dot_general(a, b, dims, preferred_element_type=F32)

    return one(left[0], right[0]) + (one(left[0], right[1]) + one(left[1], right[0]))


def put(high_ref, low_ref, wide):
    high, low = split(wide)
    high_ref[...] = high
    low_ref[...] = low


def get(high_ref, low_ref):
    return high_ref[...], low_ref[...]


def reverse_lanes(wide):
    size = wide.shape[1]
    row = lax.broadcasted_iota(jnp.int32, (size, size), 0)
    col = lax.broadcasted_iota(jnp.int32, (size, size), 1)
    turn = (row + col == size - 1).astype(F32).astype(BF16)
    high, rest = split(wide)
    middle = wide - high.astype(F32)
    low = (middle - rest.astype(F32)).astype(BF16)

    def one(part):
        return lax.dot_general(part, turn, NN, preferred_element_type=F32)

    return one(high) + (one(rest) + one(low))


def live_row(length, start, width):
    return (lax.broadcasted_iota(jnp.int32, (1, width), 1) + start < length).astype(F32)


def whole(shape):
    return pl.BlockSpec(shape, lambda i: (0,) * len(shape))


def across(rows, width=WIDE):
    return pl.BlockSpec((rows, width), lambda i: (0, i))


SCALARS = pl.BlockSpec(memory_space=pltpu.SMEM)


def shaped(shape, dtype=F32):
    return jax.ShapeDtypeStruct(shape, dtype)


def to_hbm(array):
    return pltpu.with_memory_space_constraint(array, pltpu.HBM)


def call(kernel, grid, ins, outs, scratch=(), name=None, pin=True, pin_out=True):
    held = sum(2 * math.prod(spec.block_shape) * array.dtype.itemsize for array, spec in ins if spec.block_shape)
    held += sum(2 * math.prod(spec.block_shape) * shape.dtype.itemsize for shape, spec in outs)
    held += sum(math.prod(ref.shape) * jnp.dtype(ref.dtype).itemsize for ref in scratch)
    moved = sum(array.size * array.dtype.itemsize for array, _ in ins)
    moved += sum(math.prod(shape.shape) * shape.dtype.itemsize for shape, _ in outs)
    arrays = [array if spec is SCALARS or not pin else to_hbm(array) for array, spec in ins]
    run = pl.pallas_call(
        kernel,
        grid=(grid,),
        in_specs=[spec for _, spec in ins],
        out_specs=[spec for _, spec in outs],
        out_shape=[pltpu.HBM(shape.shape, shape.dtype) if pin_out else shape for shape, _ in outs],
        scratch_shapes=list(scratch),
        compiler_params=pltpu.CompilerParams(
            dimension_semantics=("arbitrary",), vmem_limit_bytes=min(held + 16 * 2**20, 58 * 2**20)
        ),
        cost_estimate=pl.CostEstimate(flops=0, transcendentals=0, bytes_accessed=int(moved * SCALE)),
        name=name,
    )
    return list(run(*arrays))


def place_rows(target, place, parts):
    for flip, part in enumerate(parts):
        rows = part.shape[0]
        target[pl.ds(pl.multiple_of((place ^ flip) * rows, rows), rows), :] = part[...]


def take_rows(source, index, rows):
    return source[pl.ds(pl.multiple_of(index * rows, rows), rows), :]


def fold(wide):
    total = wide[:, :128]
    for at in range(128, wide.shape[1], 128):
        total = total + wide[:, at : at + 128]
    return total


def band_kernel(bias, high, low):
    window = bias.shape[1]
    turned = reverse_lanes(jnp.exp(bias[...]))
    wide = jnp.concatenate([turned, jnp.zeros_like(turned)], axis=1)
    skewed = pltpu.roll(wide, 1, 1, stride=1, stride_axis=0)
    row = lax.broadcasted_iota(jnp.int32, wide.shape, 0)
    col = lax.broadcasted_iota(jnp.int32, wide.shape, 1)
    band = skewed + (col <= row).astype(F32)
    first = (pl.program_id(0) == 0) & (col < window)
    put(high, low, jnp.where(first, 0.0, band))


def qkv_weights_kernel(w_q, w_k, w_v, high, low, high_t, low_t):
    stacked = jnp.concatenate([w_q[...], w_k[...], w_v[...]], axis=0)
    put(high, low, stacked)
    put(high_t, low_t, stacked.T)


def weights_kernel(w, high, low, high_t, low_t):
    put(high, low, w[...])
    put(high_t, low_t, w[...].T)


def out_weights_kernel(own, near, far, far_near, high_t, low_t):
    stacked = jnp.concatenate([own[...], near[...], far[...], far_near[...]], axis=0)
    put(high_t, low_t, stacked.T)


def column_stats(values_in):
    mean = jnp.mean(values_in, axis=0, keepdims=True)
    var = jnp.mean(values_in * values_in, axis=0, keepdims=True) - mean * mean
    return mean, lax.rsqrt(var + EPSILON)


def attend_kernel(
    info, x0, x1, x2, x3, v0, v1, v2, v3, w_hi, w_lo, band_hi, band_lo,
    cols, mixed, quotient, f_query, f_numer, pair_hi, pair_lo, n_hi, n_lo, stats,
    x_all, far, last_hi, last_lo,
):
    step = pl.program_id(0)
    chans = x0.shape[0]
    window = TB

    @pl.when(step == 0)
    def _():
        for flip, part in enumerate((v0, v1, v2, v3)):
            start = pl.multiple_of((info[0] ^ flip) * chans, chans)
            cols[pl.ds(start, chans), :] = part[...].T[:chans]

    biases = v0[...].T[:chans]
    place_rows(x_all, info[0], (x0, x1, x2, x3))
    x = x_all[...]
    mean, scale = column_stats(x)
    stats[0:1, :] = mean
    stats[1:2, :] = scale
    normed = split((x - mean) * scale * cols[:, 0:1] + cols[:, 1:2])
    n_hi[...], n_lo[...] = normed
    projected = dot3(get(w_hi, w_lo), normed, NN)
    exp_keys = jnp.exp(projected[chans : 2 * chans])
    carried = exp_keys * (projected[2 * chans :] + biases[:, 6:7])
    pair = split(jnp.concatenate([carried, exp_keys], axis=0))
    pair_hi[...], pair_lo[...] = pair

    @pl.when(step == 0)
    def _():
        far[...] = jnp.zeros_like(far)
        last_hi[...] = jnp.zeros_like(last_hi)
        last_lo[...] = jnp.zeros_like(last_lo)

    last = get(last_hi, last_lo)
    total = far[:, 0:1]
    gates = jax.nn.sigmoid(projected[:chans] + biases[:, 5:6])
    for at in range(0, x.shape[1], window):
        here = slice(at, at + window)
        near = (band_hi[here, :], band_lo[here, :])
        block = (pair[0][:, here], pair[1][:, here])
        sums = dot3(block, (near[0][:, window:], near[1][:, window:]), NT)
        sums = sums + dot3(last, (near[0][:, :window], near[1][:, :window]), NT)
        sums = sums + total
        total = total + jnp.sum(last[0].astype(F32) + last[1].astype(F32), axis=1, keepdims=True)
        last = block
        inverse = 1.0 / sums[chans:]
        ratio = sums[:chans] * inverse
        gate = gates[:, here]
        quotient[:, here] = ratio
        mixed[:, here] = gate * ratio
        f_query[:, here] = ratio * gate * (1.0 - gate)
        f_numer[:, here] = gate * inverse
    far[...] = jnp.broadcast_to(total, far.shape)
    last_hi[...], last_lo[...] = last


def hidden_kernel(
    info, m0, m1, m2, m3, x0, x1, x2, x3, cols, wo_hi, wo_lo, wu_hi, wu_lo, up_bias,
    act_hi, act_lo, slope, n_hi, n_lo, inner_own, stats,
    x_all,
):
    step = pl.program_id(0)
    place_rows(x_all, info[0], (x0, x1, x2, x3))
    live = live_row(info[1], step * WIDE, WIDE)
    parts = jnp.concatenate([m0[...], m1[...], m2[...], m3[...]], axis=0)
    out = dot3(get(wo_hi, wo_lo), split(parts), NN)
    inner = x_all[...] + live * (out + cols[:, 2:3])
    x_all[...] = inner
    inner_own[...] = take_rows(x_all, info[0], x0.shape[0])
    mean, scale = column_stats(inner)
    stats[0:1, :] = scale
    unit = (inner - mean) * scale
    normed = split(unit * cols[:, 3:4] + cols[:, 4:5])
    n_hi[...], n_lo[...] = normed
    pre = dot3(get(wu_hi, wu_lo), normed, NN) + up_bias[...]
    root = 0.7978845608028654
    cubic = 0.044715
    square = pre * pre
    bent = jnp.tanh(root * pre * (1.0 + cubic * square))
    put(act_hi, act_lo, 0.5 * pre * (1.0 + bent))
    slope[...] = 0.5 * (1.0 + bent) + 0.5 * pre * (1.0 - bent * bent) * (
        root * (1.0 + 3.0 * cubic * square)
    )


def parted(rows, info):
    step = rows // 4
    for half in range(2):
        bit = info[2 + half]
        yield pl.multiple_of((2 * half + bit) * step, step)
        yield pl.multiple_of((2 * half + 1 - bit) * step, step)


def outer_kernel(info, a_hi, a_lo, b_hi, b_lo, *rest):
    outs, (s_hi, s_lo) = rest[:4], rest[4:]
    rows = a_hi.shape[0]
    step = rows // 4

    @pl.when(pl.program_id(0) == 0)
    def _():
        for at, start in enumerate(parted(rows, info)):
            here = slice(at * step, (at + 1) * step)
            s_hi[here, :] = a_hi[pl.ds(start, step), :]
            s_lo[here, :] = a_lo[pl.ds(start, step), :]

    grad = dot3(get(s_hi, s_lo), get(b_hi, b_lo), NT)
    for at, out in enumerate(outs):
        out[...] = grad[at * step : (at + 1) * step]


def down_grad_kernel(info, a_hi, a_lo, c0, c1, c2, c3, *rest):
    outs, (c_hi, c_lo, own_sum, s_hi, s_lo, c_all) = rest[:4], rest[4:]
    rows = a_hi.shape[0]
    step = rows // 4
    live = live_row(info[1], 0, c_all.shape[1])
    for at, start in enumerate(parted(rows, info)):
        here = slice(at * step, (at + 1) * step)
        s_hi[here, :] = a_hi[pl.ds(start, step), :]
        s_lo[here, :] = a_lo[pl.ds(start, step), :]
    place_rows(c_all, info[0], (c0, c1, c2, c3))
    put(c_hi, c_lo, c_all[...] * live)
    own_sum[...] = fold(c0[...] * live)
    grad = dot3(get(s_hi, s_lo), get(c_hi, c_lo), NT)
    for at, out in enumerate(outs):
        out[...] = grad[at * step : (at + 1) * step]


def order_pair(bit, first, second, keep, send):
    keep[...] = jnp.where(bit == 0, first, second)
    send[...] = jnp.where(bit == 0, second, first)


def projection_grads_kernel(
    info, d_out, q_hi, q_lo, kv_hi, kv_lo, n_hi, n_lo, keep_0, send_0, keep_1, send_1
):
    rows = d_out.shape[0]
    normed = get(n_hi, n_lo)
    left = (
        jnp.concatenate([q_hi[...], kv_hi[...]], axis=0),
        jnp.concatenate([q_lo[...], kv_lo[...]], axis=0),
    )
    d_qkv = dot3(left, normed, NT)
    order_pair(info[2], d_out[...], d_qkv[:rows], keep_0, send_0)
    order_pair(info[3], d_qkv[rows : 2 * rows], d_qkv[2 * rows :], keep_1, send_1)


def projection_done_kernel(info, h_0, c_0, h_1, c_1, d_out, d_query, d_key, d_value):
    order_pair(info[2], h_0[...], c_0[...], d_out, d_query)
    order_pair(info[3], h_1[...], c_1[...], d_key, d_value)


def halve_kernel(places, info, *refs):
    count = len(places)
    for i, at in enumerate(places):
        kept, come = refs[2 * i], refs[2 * i + 1]
        mine, send = refs[2 * count + 2 * i], refs[2 * count + 2 * i + 1]
        rows = mine.shape[0]
        mine[...] = take_rows(kept, info[at], rows) + take_rows(come, info[at], rows)
        send[...] = take_rows(kept, 1 - info[at], rows) + take_rows(come, 1 - info[at], rows)


def add_kernel(info, *refs):
    count = len(refs) // 3
    for i in range(count):
        refs[2 * count + i][...] = refs[2 * i][...] + refs[2 * i + 1][...]


def pack_kernel(info, *refs):
    rows = refs[0].shape[0]
    refs[4][:rows, :] = refs[0][...] + refs[1][...]
    refs[4][rows:, :] = refs[2][...] + refs[3][...]


def unpack_kernel(info, held, come, first, second):
    rows = first.shape[0]
    first[...] = held[:rows, :] + come[:rows, :]
    second[...] = held[rows:, :] + come[rows:, :]


def join_kernel(places, merged, info, *refs):
    count = len(places)
    for i, at in enumerate(places):
        held, come = refs[2 * i], refs[2 * i + 1]
        out = refs[2 * count] if merged else refs[2 * count + i]
        rows = held.shape[0]
        base = 2 * i if merged else 0
        out[pl.ds(pl.multiple_of((base + info[at]) * rows, rows), rows), :] = held[...]
        out[pl.ds(pl.multiple_of((base + 1 - info[at]) * rows, rows), rows), :] = come[...]


def lane_sums_kernel(*refs):
    ins, out = refs[:-1], refs[-1]
    wide = jnp.concatenate([ref[...] for ref in ins], axis=0)
    high, rest = split(wide)
    low = (wide - high.astype(F32) - rest.astype(F32)).astype(BF16)
    ones = jnp.ones((8, wide.shape[1]), BF16)

    def one(part):
        return lax.dot_general(ones, part, NT, preferred_element_type=F32)

    sums = one(high) + (one(rest) + one(low))
    width = out.shape[1]
    out[...] = jnp.zeros_like(out)
    for at in range(0, sums.shape[1], width):
        part = sums[0:1, at : at + width]
        out[at // width : at // width + 1, : part.shape[1]] = part


def part_halves(grid, place, keep, send):
    rows = grid.shape[0] // 4
    core = place & 1
    for far in range(2):
        here = slice(far * rows, (far + 1) * rows)
        keep[here, :] = take_rows(grid, 2 * far + core, rows)
        send[here, :] = take_rows(grid, 2 * far + 1 - core, rows)


def hidden_back_kernel(
    info, c_hi, c_lo, wd_hi, wd_lo, slope, wu_hi, wu_lo, d_hi, d_lo, keep, send, bias_sum, grid
):
    @pl.when(pl.program_id(0) == 0)
    def _():
        bias_sum[...] = jnp.zeros_like(bias_sum)

    d_pre = dot3(get(wd_hi, wd_lo), get(c_hi, c_lo), NN) * slope[...]
    bias_sum[...] += fold(d_pre)
    parts = split(d_pre)
    d_hi[...], d_lo[...] = parts
    grid[...] = dot3(get(wu_hi, wu_lo), parts, NN)
    part_halves(grid, info[0], keep, send)


def down_kernel(info, wd_hi, wd_lo, act_hi, act_lo, keep, send, grid):
    grid[...] = dot3(get(wd_hi, wd_lo), get(act_hi, act_lo), NN)
    part_halves(grid, info[0], keep, send)


def inner_back_kernel(
    info, half, other, n_hi, n_lo, stats, cols, c0, c1, c2, c3, w_out, f_query, f_numer, quotient, mixed,
    d_out, dq_hi, dq_lo, dp_hi, dp_lo, inner_own, sum_gain, sum_bias, sum_out, sum_query,
    c_all, d_all, normal, wo_hi, wo_lo,
):
    step = pl.program_id(0)
    place = info[0]
    core = place & 1
    chans = c0.shape[0]
    place_rows(c_all, place, (c0, c1, c2, c3))
    for far in range(2):
        here = slice(far * chans, (far + 1) * chans)
        d_all[pl.ds(pl.multiple_of((2 * far + core) * chans, chans), chans), :] = half[here, :]
        d_all[pl.ds(pl.multiple_of((2 * far + 1 - core) * chans, chans), chans), :] = other[here, :]
    live = live_row(info[1], step * WIDE, WIDE)
    scaled = d_all[...] * cols[:, 3:4]
    unit = (n_hi[...].astype(F32) + n_lo[...].astype(F32) - cols[:, 4:5]) * (1.0 / cols[:, 3:4])
    normal[...] = unit
    mean_one = jnp.mean(scaled, axis=0, keepdims=True)
    mean_two = jnp.mean(scaled * unit, axis=0, keepdims=True)
    d_inner = c_all[...] + stats[0:1, :] * (scaled - mean_one - unit * mean_two)
    c_all[...] = d_inner
    own = take_rows(c_all, place, chans)
    inner_own[...] = own
    d_own = take_rows(d_all, place, chans)

    @pl.when(step == 0)
    def _():
        put(wo_hi, wo_lo, w_out[...])
        for total in (sum_gain, sum_bias, sum_out, sum_query, d_out):
            total[...] = jnp.zeros_like(total)

    sum_gain[...] += fold(d_own * take_rows(normal, place, chans))
    sum_bias[...] += fold(d_own)
    sum_out[...] += fold(own * live)
    branch = split(d_inner * live)
    d_out[...] += dot3(split(mixed[...]), branch, NT)
    d_mixed = dot3(get(wo_hi, wo_lo), branch, NN)
    d_query = d_mixed * f_query[...]
    sum_query[...] += fold(d_query)
    put(dq_hi, dq_lo, d_query)
    d_numer = d_mixed * f_numer[...]
    put(dp_hi, dp_lo, jnp.concatenate([d_numer, -d_numer * quotient[...]], axis=0))


def mix_back_kernel(
    d_hi, d_lo, before_hi, before_lo, here_hi, here_lo, band_hi, band_lo, bias,
    kv_hi, kv_lo, d_bias, sum_value,
    carry, later, ahead,
):
    step = pl.program_id(0)
    block = pl.num_programs(0) - 1 - step
    window = TB
    chans = d_hi.shape[0] // 2

    @pl.when(step == 0)
    def _():
        for total in (carry, later, ahead, sum_value):
            total[...] = jnp.zeros_like(total)

    d_pair = get(d_hi, d_lo)
    d_wide = d_pair[0].astype(F32) + d_pair[1].astype(F32)
    into = dot3(d_pair, get(band_hi, band_lo), NN)
    back = into[:, window:] + carry[...] + later[:, 0:1]
    carry[...] = into[:, :window]
    later[...] = later[...] + ahead[...]
    ahead[...] = jnp.broadcast_to(jnp.sum(d_wide, axis=1, keepdims=True), ahead.shape)
    turned = split(d_wide.T)
    right = dot3(turned, get(here_hi, here_lo), NN)
    left = dot3(turned, get(before_hi, before_lo), NN)
    left = jnp.where(block == 0, 0.0, left)
    wide = jnp.concatenate([reverse_lanes(right), reverse_lanes(left)], axis=1)
    placed = pltpu.roll(wide, window + 1, 1, stride=1, stride_axis=0)
    d_bias[...] = placed[:, :window] * jnp.exp(bias[...])
    pair = here_hi[...].astype(F32) + here_lo[...].astype(F32)
    d_value = pair[chans:] * back[:chans]
    d_key = pair[:chans] * back[:chans] + pair[chans:] * back[chans:]
    sum_value[...] += fold(d_value)
    put(kv_hi, kv_lo, jnp.concatenate([d_key, d_value], axis=0))


def project_back_kernel(
    info, dq_hi, dq_lo, kv_hi, kv_lo, w_hi, w_lo, x0, x1, x2, x3, stats, cols, d_pair, keep, send,
    x_all, grid,
):
    place_rows(x_all, info[0], (x0, x1, x2, x3))
    d_all = (
        jnp.concatenate([dq_hi[...], kv_hi[...]], axis=0),
        jnp.concatenate([dq_lo[...], kv_lo[...]], axis=0),
    )
    terms = dot3(get(w_hi, w_lo), d_all, NN)
    grid[...] = terms
    part_halves(grid, info[0], keep, send)
    scaled = terms * cols[:, 0:1]
    unit = (x_all[...] - stats[0:1, :]) * stats[1:2, :]
    at = grid.shape[0] // 2
    sums = (jnp.sum(scaled, axis=0, keepdims=True), jnp.sum(scaled * unit, axis=0, keepdims=True))
    sums = jnp.concatenate([*sums, jnp.zeros((6, grid.shape[1]), F32)], axis=0)
    rows, window = d_pair.shape[0] // 8, d_pair.shape[1]
    for out, core in ((keep, info[4]), (send, 1 - info[4])):
        out[at : at + 8, :] = sums
        for block in range(grid.shape[1] // window):
            start = 4 * rows * core + rows * (grid.shape[1] // window * pl.program_id(0) + block)
            lanes = slice(block * window, (block + 1) * window)
            out[at + 8 :, lanes] = d_pair[pl.ds(pl.multiple_of(start, rows), rows), :]


def core_halves_kernel(info, keep, come, mine_a, send_a, mine_b, send_b):
    rows = mine_a.shape[0] - 8 - (keep.shape[1] // 16)
    chans = rows + mine_b.shape[0]
    at = 2 * chans
    for out_a, out_b, far in ((mine_a, mine_b, info[5]), (send_a, send_b, 1 - info[5])):
        here = pl.ds(pl.multiple_of(far * chans, 8), rows)
        below = pl.ds(pl.multiple_of(far * chans + rows, 8), chans - rows)
        out_a[:rows, :] = keep[here, :] + come[here, :]
        out_b[...] = keep[below, :] + come[below, :]
        out_a[rows : rows + 8, :] = keep[at : at + 8, :] + come[at : at + 8, :]
        half = keep[at + 8 :, :] + come[at + 8 :, :]
        wide = half.shape[1] // 2
        part = jnp.where(far == 0, half[:, :wide], half[:, wide:])
        tall = part.shape[0] // 2
        out_a[rows + 8 :, :wide] = part[:tall]
        out_a[rows + 8 :, wide:] = part[tall:]


def chip_sum_kernel(info, mine, come, pair, sums):
    rows = mine.shape[0] - pair.shape[0] - 8
    sums[...] = mine[rows : rows + 8, :] + come[rows : rows + 8, :]
    pair[...] = mine[rows + 8 :, :] + come[rows + 8 :, :]


def pair_small_kernel(info, pair, come, small, out):
    rows = pair.shape[0]
    out[:rows, :] = pair[...] + come[...]
    out[rows:, :] = small[...]


def pair_small_sum_kernel(info, held, come, pair, small):
    rows = pair.shape[0]
    pair[...] = held[:rows, :] + come[:rows, :]
    small[...] = held[rows:, :] + come[rows:, :]


def pair_chips_kernel(info, own, other, half):
    tall, wide = own.shape[0], own.shape[1] // 2
    for low, lanes in ((True, slice(0, wide)), (False, slice(wide, 2 * wide))):
        near = info[5] == (0 if low else 1)
        for top in range(2):
            here = slice(top * wide, (top + 1) * wide)
            half[top * tall : (top + 1) * tall, lanes] = jnp.where(near, own[:, here], other[:, here])


def pair_cores_kernel(info, own, other, d_pair):
    rows, window = own.shape[0], d_pair.shape[1]
    for half, core in ((own, info[4]), (other, 1 - info[4])):
        for block in range(4):
            start = 4 * rows * core + rows * block
            d_pair[pl.ds(pl.multiple_of(start, rows), rows), :] = half[:, block * window : (block + 1) * window]


def input_back_kernel(model, mine_a, come_a, mine_b, come_b, inner_own, x_own, stats, sums, gain, d_in, sum_gain, sum_bias):
    rows = inner_own.shape[0] - mine_b.shape[0]
    d_normed = jnp.concatenate([mine_a[:rows, :] + come_a[:rows, :], mine_b[...] + come_b[...]], axis=0)
    unit = (x_own[...] - stats[0:1, :]) * stats[1:2, :]

    @pl.when(pl.program_id(0) == 0)
    def _():
        for total in (sum_gain, sum_bias):
            total[...] = jnp.zeros_like(total)

    sum_gain[...] += fold(d_normed * unit)
    sum_bias[...] += fold(d_normed)
    d_in[...] = inner_own[...] + stats[1:2, :] * (
        d_normed * gain[...] - sums[0:1, :] / model - unit * (sums[1:2, :] / model)
    )


def swap(block, bit):
    return lax.ppermute(block, "mp", [(i, i ^ bit) for i in range(4)])


def gather_parts(own):
    far = swap(own, 2)
    near = swap(own, 1)
    return own, near, far, swap(far, 1)


def in_order(parts, place):
    stacked = jnp.stack(parts)
    return jnp.concatenate(
        [lax.dynamic_index_in_dim(stacked, place ^ i, 0, keepdims=False) for i in range(4)], axis=0
    )


def after(value, *earlier):
    return lax.optimization_barrier((value, earlier))[0]


def trade(block, flip):
    size = lax.axis_size("dp")
    return lax.ppermute(block, "dp", [(i, i ^ flip) for i in range(size)])


def glue(kernel, scalars, ins, outs, name, steps=1):
    def columns(shape):
        return pl.BlockSpec((shape[0], shape[1] // steps), lambda i: (0, i))

    return call(
        kernel, steps,
        [scalars, *[(x, columns(x.shape)) for x in ins]],
        [(shaped(shape), columns(shape)) for shape in outs],
        name=name,
        pin=False,
        pin_out=PIN_GLUE,
    )


def add_trade(block, flip, *gate):
    if lax.axis_size("dp") != 8:
        return jnp.zeros_like(block)
    return trade(after(block, *gate), flip)


def settle(sums, arrived, *gates):
    comes = [s.come for s in sums]
    comes, arrived, _ = lax.optimization_barrier((comes, arrived, gates))
    for s, come in zip(sums, comes):
        s.come = come
        if s.stage < 4:
            s.take()
    return arrived


class Sum:
    FLIPS = ((1, 2), (2, 1), (4,), (2, 1), (1, 2))

    def __init__(self, scalars, blocks, merged):
        self.merged = merged
        self.come = []
        self.scalars = scalars
        self.direct = lax.axis_size("dp") != 8
        self.stage = 0
        if self.direct:
            self.total = lax.psum(blocks, "dp")
            if merged:
                self.total = [jnp.concatenate(self.total, axis=0)]
            self.out = self.total
        else:
            self.mine, self.out = blocks[0::2], blocks[1::2]

    def send(self, *gate):
        if not self.direct:
            pairs = zip(self.out, self.FLIPS[self.stage])
            self.come = [trade(after(block, *gate), flip) for block, flip in pairs]

    def finish(self, *gate):
        if not self.direct:
            self.mine = after(self.mine, *gate)
            self.take()
        return self.total

    def take(self):
        if self.direct:
            return
        ins = [x for pair in zip(self.mine, self.come) for x in pair]
        rows, width = self.mine[0].shape
        name = f"sum_stage_{self.stage}"
        if self.stage == 0:
            half = (rows // 2, width)
            got = glue(partial(halve_kernel, (3, 2)), self.scalars, ins, [half] * 4, name, 2)
            self.mine, self.out = got[0::2], got[1::2]
        elif self.stage == 1:
            self.mine = self.out = glue(pack_kernel, self.scalars, ins, [(2 * rows, width)], name)
        elif self.stage == 2:
            self.mine = self.out = glue(unpack_kernel, self.scalars, ins, [(rows // 2, width)] * 2, name)
        elif self.stage == 3:
            kernel = partial(join_kernel, (3, 2), False)
            self.mine = self.out = glue(kernel, self.scalars, ins, [(2 * rows, width)] * 2, name)
        else:
            shapes = [(4 * rows, width)] if self.merged else [(rows, width)] * 4
            kernel = partial(join_kernel, (2, 3), True) if self.merged else projection_done_kernel
            self.out = self.total = glue(kernel, self.scalars, ins, shapes, name, 2)
        self.stage += 1


def body(
    inputs,
    lengths,
    ln1_gain,
    ln1_bias,
    w_query,
    w_key,
    w_value,
    query_bias,
    value_bias,
    pair_bias,
    w_out,
    out_bias,
    ln2_gain,
    ln2_bias,
    w_up,
    up_bias,
    w_down,
    down_bias,
    cotangent,
):
    seq_rows, span, chans = inputs.shape
    window = pair_bias.shape[1]
    model = 4 * chans
    units = w_up.shape[1]
    steps = span // WIDE
    blocks = span // TB
    assert seq_rows == 1 and window == TB
    place = lax.axis_index("mp")
    row = lax.axis_index("dp")
    halving = lax.axis_size("dp") == 8
    bits = [row % 2, (row // 2) % 2] if halving else [jnp.int32(0)] * 2
    info = jnp.stack([place.astype(jnp.int32), lengths[0], *bits, place % 2, place // 2])

    x_own = inputs[0].T
    x_far = swap(x_own, 2)
    x_near = swap(x_own, 1)
    vectors = jnp.stack([ln1_gain, ln1_bias, out_bias, ln2_gain, ln2_bias, query_bias, value_bias])
    vectors = jnp.pad(vectors, ((0, 1), (0, 256 - chans)))
    v_far = swap(vectors, 2)
    v_near = swap(vectors, 1)

    band = call(
        band_kernel, blocks,
        [(pair_bias, pl.BlockSpec((TB, window), lambda i: (i, 0)))],
        [(shaped((span, 2 * window), BF16), pl.BlockSpec((TB, 2 * window), lambda i: (i, 0)))] * 2,
        name="band",
    )
    wide_qkv, tall_qkv = (3 * chans, model), (model, 3 * chans)
    up_dims, down_dims = (model, units), (units, model)

    def prepare(kernel, ins, dims, name):
        return call(
            kernel, 1, [(w, whole(w.shape)) for w in ins], [(shaped(d, BF16), whole(d)) for d in dims for _ in range(2)], name=name
        )

    wq_hi, wq_lo, wqt_hi, wqt_lo = prepare(
        qkv_weights_kernel, [w_query.T, w_key.T, w_value.T], [wide_qkv, tall_qkv], "qkv_weights"
    )
    wu_hi, wu_lo, wut_hi, wut_lo = prepare(weights_kernel, [w_up], [up_dims, down_dims], "up_weights")
    up_column, gain_column = up_bias[:, None], ln1_gain[:, None]
    v_far, x_far, up_column, gain_column = lax.optimization_barrier(
        (v_far, x_far, up_column, gain_column, band, wq_hi, wu_hi)
    )[:4]
    x_parts = (x_own, x_near, x_far, swap(x_far, 1))
    v_parts = (vectors, v_near, v_far, swap(v_far, 1))
    wo_own = after(w_out, x_far, v_far)
    wo_far = swap(wo_own, 2)
    wo_near = swap(w_out, 1)

    thin = (shaped((chans, span)), across(chans))
    tall_half = (shaped((model, span), BF16), across(model))
    hid_half = (shaped((units, span), BF16), across(units))
    pair_half = (shaped((2 * chans, span), BF16), across(2 * chans))
    thin_half = (shaped((chans, span), BF16), across(chans))
    rows8 = (shaped((8, span)), across(8))
    x_ins = [(x, across(chans)) for x in x_parts]
    scalars = (info, SCALARS)

    cols_out = (shaped((model, 8)), whole((model, 8)))
    cols, mixed, quotient, f_query, f_numer, pair_hi, pair_lo, n1_hi, n1_lo, stats_one = call(
        attend_kernel, steps,
        [scalars, *x_ins, *[(v, whole((8, 256))) for v in v_parts], (wq_hi, whole(wide_qkv)), (wq_lo, whole(wide_qkv))]
        + [(b, pl.BlockSpec((WIDE, 2 * window), lambda i: (i, 0))) for b in band],
        [cols_out, thin, thin, thin, thin, pair_half, pair_half, tall_half, tall_half, rows8],
        [
            pltpu.VMEM((model, WIDE), F32),
            pltpu.VMEM((2 * chans, 128), F32),
            pltpu.VMEM((2 * chans, TB), BF16),
            pltpu.VMEM((2 * chans, TB), BF16),
        ],
        name="attend",
        pin=PIN_ATT,
    )

    cols_in = (cols, whole((model, 8)))
    mixed_far = swap(mixed, 2)
    mixed_near = swap(mixed, 1)
    wo_parts = (w_out, wo_near, wo_far, swap(wo_far, 1))
    wot_hi, wot_lo = prepare(out_weights_kernel, wo_parts, [(model, model)], "out_weights")
    wd_hi, wd_lo, wdt_hi, wdt_lo = prepare(weights_kernel, [w_down], [down_dims, up_dims], "down_weights")
    mixed_far = after(mixed_far, wot_hi, wd_hi)
    mixed_parts = (mixed, mixed_near, mixed_far, swap(mixed_far, 1))
    cot_own = cotangent[0].T
    cot_far = swap(after(cot_own, mixed_far), 2)
    cot_near = swap(cot_own, 1)
    lanes_own = (shaped((chans, 128)), whole((chans, 128)))

    act_hi, act_lo, slope, n2_hi, n2_lo, inner_own, stats_two = call(
        hidden_kernel, steps,
        [scalars, *[(p, across(chans)) for p in mixed_parts], *x_ins, cols_in]
        + [(wot_hi, whole((model, model))), (wot_lo, whole((model, model)))]
        + [(wut_hi, whole(down_dims)), (wut_lo, whole(down_dims)), (up_column, whole((units, 1)))],
        [hid_half, hid_half, (shaped((units, span)), across(units)), tall_half, tall_half, thin, rows8],
        [pltpu.VMEM((model, WIDE), F32)],
        name="hidden",
        pin=PIN_HIN,
        pin_out=PIN_HID,
    )

    cot_far = after(cot_far, act_hi)
    cot_parts = (cot_own, cot_near, cot_far, swap(cot_far, 1))
    cot_ins = [(c, across(chans)) for c in cot_parts]
    def outer(a_hi, a_lo, b_hi, b_lo, name, steps=2):
        rows, inner_len = a_hi.shape
        deep = b_hi.shape[0]
        left = whole((rows, inner_len))
        right = pl.BlockSpec((deep // steps, inner_len), lambda i: (i, 0))
        part = (shaped((rows // 4, deep)), across(rows // 4, deep // steps))
        grads = call(
            outer_kernel, steps,
            [scalars, (a_hi, left), (a_lo, left), (b_hi, right), (b_lo, right)],
            [part] * 4,
            [pltpu.VMEM((rows, inner_len), BF16)] * 2,
            name=name,
            pin=PIN_UG,
            pin_out=PIN_GO,
        )
        return Sum(scalars, grads, True)

    whole_half = (shaped((model, span), BF16), whole((model, span)))
    block = (shaped((units // 4, model)), whole((units // 4, model)))
    *grads, c_hi, c_lo, s_down = call(
        down_grad_kernel, 1,
        [scalars, (act_hi, whole((units, span))), (act_lo, whole((units, span))), *[(c, whole((chans, span))) for c in cot_parts]],
        [block] * 4 + [whole_half, whole_half, lanes_own],
        [pltpu.VMEM((units, span), BF16)] * 2 + [pltpu.VMEM((model, span), F32)],
        name="down_grad",
        pin=PIN_DG,
        pin_out=PIN_GO,
    )
    g_down = Sum(scalars, grads, True)
    g_down.send()
    c_hi, c_lo = after((c_hi, c_lo), g_down.out)
    half_out = (shaped((2 * chans, span)), across(2 * chans))
    half_shape = (2 * chans, span)
    dpre_hi, dpre_lo, keep, send, s_up = call(
        hidden_back_kernel, steps,
        [scalars, (c_hi, across(model)), (c_lo, across(model)), (wd_hi, whole(down_dims)), (wd_lo, whole(down_dims))]
        + [(slope, across(units)), (wu_hi, whole(up_dims)), (wu_lo, whole(up_dims))],
        [hid_half, hid_half, half_out, half_out, (shaped((units, 128)), whole((units, 128)))],
        [pltpu.VMEM((model, WIDE), F32)],
        name="hidden_back",
        pin=PIN_HB,
        pin_out=PIN_MID,
    )
    send = settle([g_down], send, keep)
    half = glue(add_kernel, scalars, [keep, swap(after(send, g_down.out), 1)], [half_shape], "core_sum", 2)[0]
    half_far = swap(half, 2)
    g_down.send(half)
    g_up = outer(after(n2_hi, half), n2_lo, dpre_hi, dpre_lo, "up_grad")
    settle([g_down], [], g_up.out)
    g_down.send()
    g_up.send(g_down.out)
    keep_down, send_down = call(
        down_kernel, steps,
        [scalars, (wdt_hi, whole(up_dims)), (wdt_lo, whole(up_dims)), (after(act_hi, g_down.out), across(units)), (act_lo, across(units))],
        [half_out, half_out],
        [pltpu.VMEM((model, WIDE), F32)],
        name="down",
        pin=False,
        pin_out=PIN_MID,
    )
    half_far, send_down = settle([g_down, g_up], (half_far, send_down), keep_down)
    half = glue(add_kernel, scalars, [half, half_far], [half_shape], "chip_sum", 2)[0]
    other, g_down.out, g_up.out = lax.optimization_barrier((swap(half, 1), g_down.out, g_up.out))
    own_shape = (chans, span)
    g_down.send(other)
    g_up.send(other)
    core_down = swap(after(send_down, other), 1)

    d_w_out, dq_hi, dq_lo, dp_hi, dp_lo, d_inner_own, s_gain2, s_bias2, s_out, s_query = call(
        inner_back_kernel, steps,
        [scalars, (half, across(2 * chans)), (other, across(2 * chans)), (n2_hi, across(model)), (n2_lo, across(model)), (stats_two, across(8)), cols_in]
        + cot_ins
        + [(w_out, whole((chans, model)))]
        + [(f_query, across(chans)), (f_numer, across(chans)), (quotient, across(chans)), (mixed, across(chans))],
        [(shaped((chans, model)), whole((chans, model))), thin_half, thin_half, pair_half, pair_half, thin, lanes_own, lanes_own, lanes_own, lanes_own],
        [pltpu.VMEM((model, WIDE), F32)] * 3 + [pltpu.VMEM((chans, model), BF16)] * 2,
        name="inner_back",
        pin=PIN_IB,
        pin_out=PIN_MID,
    )
    dp_hi, core_down = settle([g_down, g_up], (dp_hi, core_down), d_w_out)
    mine_down, send_down = glue(
        partial(halve_kernel, (5,)), scalars, [keep_down, core_down], [own_shape] * 2, "down_halves", 2
    )
    g_down.send()
    g_up.send()
    come_down = swap(after(send_down, g_down.out, g_up.out), 2)
    dp_hi = after(dp_hi, g_down.out, g_up.out)
    thin_all, tall_all = whole((chans, span)), whole((model, span))

    def back_at(i):
        return blocks - 1 - i

    pair_spec = pl.BlockSpec((2 * chans, TB), lambda i: (0, back_at(i)))
    prev_spec = pl.BlockSpec((2 * chans, TB), lambda i: (0, jnp.maximum(back_at(i) - 1, 0)))
    band_spec = pl.BlockSpec((TB, 2 * window), lambda i: (back_at(i), 0))
    row_spec = pl.BlockSpec((TB, window), lambda i: (back_at(i), 0))
    kv_hi, kv_lo, d_pair, s_value = call(
        mix_back_kernel, blocks,
        [(dp_hi, pair_spec), (dp_lo, pair_spec), (pair_hi, prev_spec), (pair_lo, prev_spec), (pair_hi, pair_spec), (pair_lo, pair_spec)]
        + [(band[0], band_spec), (band[1], band_spec), (pair_bias, row_spec)],
        [(shaped((2 * chans, span), BF16), pair_spec)] * 2 + [(shaped((span, window)), row_spec), lanes_own],
        [pltpu.VMEM((2 * chans, TB), F32), pltpu.VMEM((2 * chans, 128), F32), pltpu.VMEM((2 * chans, 128), F32)],
        name="mix_back",
        pin=PIN_MB,
        pin_out=PIN_MID,
    )
    slab = pl.BlockSpec((model // 2, span), lambda i: (i, 0))
    grads = call(
        projection_grads_kernel, 2,
        [scalars, (d_w_out, across(chans, model // 2)), (dq_hi, thin_all), (dq_lo, thin_all)]
        + [(kv_hi, whole((2 * chans, span))), (kv_lo, whole((2 * chans, span))), (n1_hi, slab), (n1_lo, slab)],
        [(shaped((chans, model)), across(chans, model // 2))] * 4,
        name="projection_grads", pin=PIN_PG, pin_out=PIN_GO,
    )
    g_mix = Sum(scalars, grads, False)
    dq_hi, kv_hi = after((dq_hi, kv_hi), grads)
    payload_rows = 2 * chans + 8 + span // 8
    payload = (shaped((payload_rows, span)), across(payload_rows))
    keep, send = call(
        project_back_kernel, steps,
        [scalars, (dq_hi, across(chans)), (dq_lo, across(chans)), (kv_hi, across(2 * chans)), (kv_lo, across(2 * chans))]
        + [(wqt_hi, whole(tall_qkv)), (wqt_lo, whole(tall_qkv)), *x_ins, (stats_one, across(8)), cols_in, (d_pair, whole((span, window)))],
        [payload, payload],
        [pltpu.VMEM((model, WIDE), F32)] * 2,
        name="project_back",
        pin=PIN_PB,
        pin_out=PIN_MID,
    )
    send, come_down = settle([g_down, g_up], (send, come_down), keep, grads)
    g_up.send(send)
    come = settle([g_up], swap(after(send, g_up.out), 1))
    first_rows = FIRST_ROWS
    rest_shape = (chans - first_rows, span)
    mine, send, mine_rest, send_rest = glue(
        core_halves_kernel, scalars, [keep, come], [(first_rows + 8 + span // 16, span)] * 2 + [rest_shape] * 2, "core_halves"
    )
    send = after(send, send_rest)
    g_mix.send(send)
    come, g_up.out = settle([g_mix], (swap(send, 2), g_up.out))
    quarter = (span // 16, span)
    pair_sum, sums = glue(chip_sum_kernel, scalars, [mine, come], [quarter, (8, span)], "chip_sums")
    come, sums, pair_sum = after((come, sums, pair_sum), g_mix.out)
    come, sums, pair_sum = lax.optimization_barrier((come, sums, pair_sum))
    g_mix.send(pair_sum)
    come_rest, pair_come = settle([g_mix], (swap(after(send_rest, pair_sum), 2), add_trade(pair_sum, 4)))
    pair_sum = glue(add_kernel, scalars, [pair_sum, pair_come], [quarter], "pair_far")[0]
    pair_sum, come_rest = after((pair_sum, come_rest), g_mix.out)
    g_mix.send(pair_sum)
    g_up.send(pair_sum)
    d_inputs, s_gain1, s_bias1 = call(
        partial(input_back_kernel, float(model)), steps,
        [(x, across(x.shape[0])) for x in (mine, come, mine_rest, come_rest, d_inner_own, x_own, stats_one, sums)]
        + [(gain_column, whole((chans, 1)))],
        [thin, lanes_own, lanes_own],
        name="input_back",
        pin=False,
        pin_out=PIN_MID,
    )
    lanes = (s_gain1, s_bias1, s_query, s_value, s_out, s_gain2, s_bias2, s_down, s_up)
    count = sum(x.shape[0] for x in lanes)
    small = call(
        lane_sums_kernel, 1, [(x, whole(x.shape)) for x in lanes], [(shaped((8, span)), whole((8, span)))],
        name="lane_sums", pin=False,
    )[0]
    sum_down = g_down.finish(pair_sum)[0]
    live = (jnp.arange(span, dtype=jnp.int32) < lengths[0]).astype(F32)[None, :]
    result = inner_own + live * (mine_down + after(come_down, pair_sum) + down_bias[:, None])
    pair_come, small, sum_down, result = settle([g_mix, g_up], (add_trade(pair_sum, 1), small, sum_down, result))
    packed = (span // 16 + 8, span)
    packed_sum = glue(pair_small_kernel, scalars, [pair_sum, pair_come, small], [packed], "pair_x")[0]
    packed_sum = after(packed_sum, g_mix.out)
    g_mix.send(packed_sum)
    come = settle([g_mix], add_trade(packed_sum, 2))
    pair_sum, small = glue(pair_small_sum_kernel, scalars, [packed_sum, come], [quarter, (8, span)], "pair_z")
    small, pair_sum = after((small, pair_sum), g_mix.out)
    g_mix.send(small, pair_sum)
    sum_up = g_up.finish(small)[0]
    small_come, pair_come, sum_up = settle([g_mix], (add_trade(small, 4), swap(pair_sum, 2), sum_up))
    pair_half = glue(pair_chips_kernel, scalars, [pair_sum, pair_come], [(span // 8, span)], "pair_chips")[0]
    small = glue(add_kernel, scalars, [small, small_come], [(8, span)], "small_far")[0]
    small, pair_half = lax.optimization_barrier((small, pair_half))
    pair_come = swap(pair_half, 1)
    small = (small + add_trade(small, 1)).reshape(-1)[:count]
    d_w_out, d_w_query, d_w_key, d_w_value = g_mix.finish(pair_half)
    d_pair = glue(pair_cores_kernel, scalars, [pair_half, pair_come], [(span, window)], "pair_cores")[0]
    if not halving:
        d_pair = lax.psum(d_pair, "dp")
        small = lax.psum(small, "dp")
    vecs = [small[i * chans : (i + 1) * chans] for i in range(8)]
    return (
        result.T[None],
        d_inputs.T[None],
        vecs[0],
        vecs[1],
        d_w_query.T,
        d_w_key.T,
        d_w_value.T,
        vecs[2],
        vecs[3],
        d_pair,
        d_w_out,
        vecs[4],
        vecs[5],
        vecs[6],
        sum_up,
        small[8 * chans :],
        sum_down,
        vecs[7],
    )


def solution(mesh):
    rows = P("dp", None, "mp")
    vec = P("mp")
    out_dim = P(None, "mp")
    in_dim = P("mp", None)
    return jax.shard_map(
        body,
        mesh=mesh,
        in_specs=(
            rows, P("dp"), vec, vec, out_dim, out_dim, out_dim, vec, vec, P(), in_dim, vec, vec, vec,
            out_dim, vec, in_dim, vec, rows,
        ),
        out_specs=(
            rows, rows, vec, vec, out_dim, out_dim, out_dim, vec, vec, P(), in_dim, vec, vec, vec,
            out_dim, vec, in_dim, vec,
        ),
        check_vma=False,
    )
```

```python
import math
from functools import partial

import jax
import jax.numpy as jnp
from jax import lax
from jax.experimental import pallas as pl
from jax.experimental.pallas import tpu as pltpu
from jax.sharding import PartitionSpec as P

EPSILON = 1e-05
TB = 256
WIDE = 512
SCALE = 0.0
FIRST_ROWS = 64
PIN_MID = True
PIN_HB = False
PIN_MB = False
PIN_IB = False
PIN_PB = False
PIN_PG = False
PIN_UG = False
PIN_GO = False
PIN_GLUE = False
PIN_ATT = True
PIN_HIN = True
PIN_DG = False
PIN_HID = False
NN = (((1,), (0,)), ((), ()))
NT = (((1,), (1,)), ((), ()))
F32 = jnp.float32
BF16 = jnp.bfloat16


def split(wide):
    high = wide.astype(BF16)
    return high, (wide - high.astype(F32)).astype(BF16)


def dot3(left, right, dims):
    def one(a, b):
        return lax.dot_general(a, b, dims, preferred_element_type=F32)

    return one(left[0], right[0]) + (one(left[0], right[1]) + one(left[1], right[0]))


def put(high_ref, low_ref, wide):
    high, low = split(wide)
    high_ref[...] = high
    low_ref[...] = low


def get(high_ref, low_ref):
    return high_ref[...], low_ref[...]


def reverse_lanes(wide):
    size = wide.shape[1]
    row = lax.broadcasted_iota(jnp.int32, (size, size), 0)
    col = lax.broadcasted_iota(jnp.int32, (size, size), 1)
    turn = (row + col == size - 1).astype(F32).astype(BF16)
    high, rest = split(wide)
    middle = wide - high.astype(F32)
    low = (middle - rest.astype(F32)).astype(BF16)

    def one(part):
        return lax.dot_general(part, turn, NN, preferred_element_type=F32)

    return one(high) + (one(rest) + one(low))


def live_row(length, start, width):
    return (lax.broadcasted_iota(jnp.int32, (1, width), 1) + start < length).astype(F32)


def whole(shape):
    return pl.BlockSpec(shape, lambda i: (0,) * len(shape))


def across(rows, width=WIDE):
    return pl.BlockSpec((rows, width), lambda i: (0, i))


SCALARS = pl.BlockSpec(memory_space=pltpu.SMEM)


def shaped(shape, dtype=F32):
    return jax.ShapeDtypeStruct(shape, dtype)


def to_hbm(array):
    return pltpu.with_memory_space_constraint(array, pltpu.HBM)


def call(kernel, grid, ins, outs, scratch=(), name=None, pin=True, pin_out=True):
    held = sum(2 * math.prod(spec.block_shape) * array.dtype.itemsize for array, spec in ins if spec.block_shape)
    held += sum(2 * math.prod(spec.block_shape) * shape.dtype.itemsize for shape, spec in outs)
    held += sum(math.prod(ref.shape) * jnp.dtype(ref.dtype).itemsize for ref in scratch)
    moved = sum(array.size * array.dtype.itemsize for array, _ in ins)
    moved += sum(math.prod(shape.shape) * shape.dtype.itemsize for shape, _ in outs)
    arrays = [array if spec is SCALARS or not pin else to_hbm(array) for array, spec in ins]
    run = pl.pallas_call(
        kernel,
        grid=(grid,),
        in_specs=[spec for _, spec in ins],
        out_specs=[spec for _, spec in outs],
        out_shape=[pltpu.HBM(shape.shape, shape.dtype) if pin_out else shape for shape, _ in outs],
        scratch_shapes=list(scratch),
        compiler_params=pltpu.CompilerParams(
            dimension_semantics=("arbitrary",), vmem_limit_bytes=min(held + 16 * 2**20, 58 * 2**20)
        ),
        cost_estimate=pl.CostEstimate(flops=0, transcendentals=0, bytes_accessed=int(moved * SCALE)),
        name=name,
    )
    return list(run(*arrays))


def place_rows(target, place, parts):
    for flip, part in enumerate(parts):
        rows = part.shape[0]
        target[pl.ds(pl.multiple_of((place ^ flip) * rows, rows), rows), :] = part[...]


def take_rows(source, index, rows):
    return source[pl.ds(pl.multiple_of(index * rows, rows), rows), :]


def fold(wide):
    total = wide[:, :128]
    for at in range(128, wide.shape[1], 128):
        total = total + wide[:, at : at + 128]
    return total


def band_kernel(bias, high, low):
    window = bias.shape[1]
    turned = reverse_lanes(jnp.exp(bias[...]))
    wide = jnp.concatenate([turned, jnp.zeros_like(turned)], axis=1)
    skewed = pltpu.roll(wide, 1, 1, stride=1, stride_axis=0)
    row = lax.broadcasted_iota(jnp.int32, wide.shape, 0)
    col = lax.broadcasted_iota(jnp.int32, wide.shape, 1)
    band = skewed + (col <= row).astype(F32)
    first = (pl.program_id(0) == 0) & (col < window)
    put(high, low, jnp.where(first, 0.0, band))


def qkv_weights_kernel(w_q, w_k, w_v, high, low, high_t, low_t):
    stacked = jnp.concatenate([w_q[...], w_k[...], w_v[...]], axis=0)
    put(high, low, stacked)
    put(high_t, low_t, stacked.T)


def weights_kernel(w, high, low, high_t, low_t):
    put(high, low, w[...])
    put(high_t, low_t, w[...].T)


def out_weights_kernel(own, near, far, far_near, high_t, low_t):
    stacked = jnp.concatenate([own[...], near[...], far[...], far_near[...]], axis=0)
    put(high_t, low_t, stacked.T)


def column_stats(values_in):
    mean = jnp.mean(values_in, axis=0, keepdims=True)
    var = jnp.mean(values_in * values_in, axis=0, keepdims=True) - mean * mean
    return mean, lax.rsqrt(var + EPSILON)


def attend_kernel(
    info, x0, x1, x2, x3, v0, v1, v2, v3, w_hi, w_lo, band_hi, band_lo,
    cols, mixed, quotient, f_query, f_numer, pair_hi, pair_lo, n_hi, n_lo, stats,
    x_all, far, last_hi, last_lo,
):
    step = pl.program_id(0)
    chans = x0.shape[0]
    window = TB

    @pl.when(step == 0)
    def _():
        for flip, part in enumerate((v0, v1, v2, v3)):
            start = pl.multiple_of((info[0] ^ flip) * chans, chans)
            cols[pl.ds(start, chans), :] = part[...].T[:chans]

    biases = v0[...].T[:chans]
    place_rows(x_all, info[0], (x0, x1, x2, x3))
    x = x_all[...]
    mean, scale = column_stats(x)
    stats[0:1, :] = mean
    stats[1:2, :] = scale
    normed = split((x - mean) * scale * cols[:, 0:1] + cols[:, 1:2])
    n_hi[...], n_lo[...] = normed
    projected = dot3(get(w_hi, w_lo), normed, NN)
    exp_keys = jnp.exp(projected[chans : 2 * chans])
    carried = exp_keys * (projected[2 * chans :] + biases[:, 6:7])
    pair = split(jnp.concatenate([carried, exp_keys], axis=0))
    pair_hi[...], pair_lo[...] = pair

    @pl.when(step == 0)
    def _():
        far[...] = jnp.zeros_like(far)
        last_hi[...] = jnp.zeros_like(last_hi)
        last_lo[...] = jnp.zeros_like(last_lo)

    last = get(last_hi, last_lo)
    total = far[:, 0:1]
    gates = jax.nn.sigmoid(projected[:chans] + biases[:, 5:6])
    for at in range(0, x.shape[1], window):
        here = slice(at, at + window)
        near = (band_hi[here, :], band_lo[here, :])
        block = (pair[0][:, here], pair[1][:, here])
        sums = dot3(block, (near[0][:, window:], near[1][:, window:]), NT)
        sums = sums + dot3(last, (near[0][:, :window], near[1][:, :window]), NT)
        sums = sums + total
        total = total + jnp.sum(last[0].astype(F32) + last[1].astype(F32), axis=1, keepdims=True)
        last = block
        inverse = 1.0 / sums[chans:]
        ratio = sums[:chans] * inverse
        gate = gates[:, here]
        quotient[:, here] = ratio
        mixed[:, here] = gate * ratio
        f_query[:, here] = ratio * gate * (1.0 - gate)
        f_numer[:, here] = gate * inverse
    far[...] = jnp.broadcast_to(total, far.shape)
    last_hi[...], last_lo[...] = last


def hidden_kernel(
    info, m0, m1, m2, m3, x0, x1, x2, x3, cols, wo_hi, wo_lo, wu_hi, wu_lo, up_bias,
    act_hi, act_lo, slope, n_hi, n_lo, inner_own, stats,
    x_all,
):
    step = pl.program_id(0)
    place_rows(x_all, info[0], (x0, x1, x2, x3))
    live = live_row(info[1], step * WIDE, WIDE)
    parts = jnp.concatenate([m0[...], m1[...], m2[...], m3[...]], axis=0)
    out = dot3(get(wo_hi, wo_lo), split(parts), NN)
    inner = x_all[...] + live * (out + cols[:, 2:3])
    x_all[...] = inner
    inner_own[...] = take_rows(x_all, info[0], x0.shape[0])
    mean, scale = column_stats(inner)
    stats[0:1, :] = scale
    unit = (inner - mean) * scale
    normed = split(unit * cols[:, 3:4] + cols[:, 4:5])
    n_hi[...], n_lo[...] = normed
    pre = dot3(get(wu_hi, wu_lo), normed, NN) + up_bias[...]
    root = 0.7978845608028654
    cubic = 0.044715
    square = pre * pre
    bent = jnp.tanh(root * pre * (1.0 + cubic * square))
    put(act_hi, act_lo, 0.5 * pre * (1.0 + bent))
    slope[...] = 0.5 * (1.0 + bent) + 0.5 * pre * (1.0 - bent * bent) * (
        root * (1.0 + 3.0 * cubic * square)
    )


def parted(rows, info):
    step = rows // 4
    for half in range(2):
        bit = info[2 + half]
        yield pl.multiple_of((2 * half + bit) * step, step)
        yield pl.multiple_of((2 * half + 1 - bit) * step, step)


def outer_kernel(info, a_hi, a_lo, b_hi, b_lo, *rest):
    outs, (s_hi, s_lo) = rest[:4], rest[4:]
    rows = a_hi.shape[0]
    step = rows // 4

    @pl.when(pl.program_id(0) == 0)
    def _():
        for at, start in enumerate(parted(rows, info)):
            here = slice(at * step, (at + 1) * step)
            s_hi[here, :] = a_hi[pl.ds(start, step), :]
            s_lo[here, :] = a_lo[pl.ds(start, step), :]

    grad = dot3(get(s_hi, s_lo), get(b_hi, b_lo), NT)
    for at, out in enumerate(outs):
        out[...] = grad[at * step : (at + 1) * step]


def down_grad_kernel(info, a_hi, a_lo, c0, c1, c2, c3, *rest):
    outs, (c_hi, c_lo, own_sum, s_hi, s_lo, c_all) = rest[:4], rest[4:]
    rows = a_hi.shape[0]
    step = rows // 4
    live = live_row(info[1], 0, c_all.shape[1])
    for at, start in enumerate(parted(rows, info)):
        here = slice(at * step, (at + 1) * step)
        s_hi[here, :] = a_hi[pl.ds(start, step), :]
        s_lo[here, :] = a_lo[pl.ds(start, step), :]
    place_rows(c_all, info[0], (c0, c1, c2, c3))
    put(c_hi, c_lo, c_all[...] * live)
    own_sum[...] = fold(c0[...] * live)
    grad = dot3(get(s_hi, s_lo), get(c_hi, c_lo), NT)
    for at, out in enumerate(outs):
        out[...] = grad[at * step : (at + 1) * step]


def order_pair(bit, first, second, keep, send):
    keep[...] = jnp.where(bit == 0, first, second)
    send[...] = jnp.where(bit == 0, second, first)


def projection_grads_kernel(
    info, mixed, b_hi, b_lo, q_hi, q_lo, kv_hi, kv_lo, n_hi, n_lo, keep_0, send_0, keep_1, send_1
):
    rows = mixed.shape[0]
    normed = get(n_hi, n_lo)
    d_out = dot3(split(mixed[...]), get(b_hi, b_lo), NT)
    left = (
        jnp.concatenate([q_hi[...], kv_hi[...]], axis=0),
        jnp.concatenate([q_lo[...], kv_lo[...]], axis=0),
    )
    d_qkv = dot3(left, normed, NT)
    order_pair(info[2], d_out, d_qkv[:rows], keep_0, send_0)
    order_pair(info[3], d_qkv[rows : 2 * rows], d_qkv[2 * rows :], keep_1, send_1)


def projection_done_kernel(info, h_0, c_0, h_1, c_1, d_out, d_query, d_key, d_value):
    order_pair(info[2], h_0[...], c_0[...], d_out, d_query)
    order_pair(info[3], h_1[...], c_1[...], d_key, d_value)


def halve_kernel(places, info, *refs):
    count = len(places)
    for i, at in enumerate(places):
        kept, come = refs[2 * i], refs[2 * i + 1]
        mine, send = refs[2 * count + 2 * i], refs[2 * count + 2 * i + 1]
        rows = mine.shape[0]
        mine[...] = take_rows(kept, info[at], rows) + take_rows(come, info[at], rows)
        send[...] = take_rows(kept, 1 - info[at], rows) + take_rows(come, 1 - info[at], rows)


def add_kernel(info, *refs):
    count = len(refs) // 3
    for i in range(count):
        refs[2 * count + i][...] = refs[2 * i][...] + refs[2 * i + 1][...]


def pack_kernel(info, *refs):
    rows = refs[0].shape[0]
    refs[4][:rows, :] = refs[0][...] + refs[1][...]
    refs[4][rows:, :] = refs[2][...] + refs[3][...]


def unpack_kernel(info, held, come, first, second):
    rows = first.shape[0]
    first[...] = held[:rows, :] + come[:rows, :]
    second[...] = held[rows:, :] + come[rows:, :]


def join_kernel(places, merged, info, *refs):
    count = len(places)
    for i, at in enumerate(places):
        held, come = refs[2 * i], refs[2 * i + 1]
        out = refs[2 * count] if merged else refs[2 * count + i]
        rows = held.shape[0]
        base = 2 * i if merged else 0
        out[pl.ds(pl.multiple_of((base + info[at]) * rows, rows), rows), :] = held[...]
        out[pl.ds(pl.multiple_of((base + 1 - info[at]) * rows, rows), rows), :] = come[...]


def lane_sums_kernel(*refs):
    ins, out = refs[:-1], refs[-1]
    wide = jnp.concatenate([ref[...] for ref in ins], axis=0)
    high, rest = split(wide)
    low = (wide - high.astype(F32) - rest.astype(F32)).astype(BF16)
    ones = jnp.ones((8, wide.shape[1]), BF16)

    def one(part):
        return lax.dot_general(ones, part, NT, preferred_element_type=F32)

    sums = one(high) + (one(rest) + one(low))
    width = out.shape[1]
    out[...] = jnp.zeros_like(out)
    for at in range(0, sums.shape[1], width):
        part = sums[0:1, at : at + width]
        out[at // width : at // width + 1, : part.shape[1]] = part


def part_halves(grid, place, keep, send):
    rows = grid.shape[0] // 4
    core = place & 1
    for far in range(2):
        here = slice(far * rows, (far + 1) * rows)
        keep[here, :] = take_rows(grid, 2 * far + core, rows)
        send[here, :] = take_rows(grid, 2 * far + 1 - core, rows)


def hidden_back_kernel(
    info, c_hi, c_lo, wd_hi, wd_lo, slope, wu_hi, wu_lo, d_hi, d_lo, keep, send, bias_sum, grid
):
    @pl.when(pl.program_id(0) == 0)
    def _():
        bias_sum[...] = jnp.zeros_like(bias_sum)

    d_pre = dot3(get(wd_hi, wd_lo), get(c_hi, c_lo), NN) * slope[...]
    bias_sum[...] += fold(d_pre)
    parts = split(d_pre)
    d_hi[...], d_lo[...] = parts
    grid[...] = dot3(get(wu_hi, wu_lo), parts, NN)
    part_halves(grid, info[0], keep, send)


def down_kernel(info, wd_hi, wd_lo, act_hi, act_lo, keep, send, grid):
    grid[...] = dot3(get(wd_hi, wd_lo), get(act_hi, act_lo), NN)
    part_halves(grid, info[0], keep, send)


def inner_back_kernel(
    info, half, other, n_hi, n_lo, stats, cols, c0, c1, c2, c3, w_out, f_query, f_numer, quotient,
    b_hi, b_lo, dq_hi, dq_lo, dp_hi, dp_lo, inner_own, sum_gain, sum_bias, sum_out, sum_query,
    c_all, d_all, normal, wo_hi, wo_lo,
):
    step = pl.program_id(0)
    place = info[0]
    core = place & 1
    chans = c0.shape[0]
    place_rows(c_all, place, (c0, c1, c2, c3))
    for far in range(2):
        here = slice(far * chans, (far + 1) * chans)
        d_all[pl.ds(pl.multiple_of((2 * far + core) * chans, chans), chans), :] = half[here, :]
        d_all[pl.ds(pl.multiple_of((2 * far + 1 - core) * chans, chans), chans), :] = other[here, :]
    live = live_row(info[1], step * WIDE, WIDE)
    scaled = d_all[...] * cols[:, 3:4]
    unit = (n_hi[...].astype(F32) + n_lo[...].astype(F32) - cols[:, 4:5]) * (1.0 / cols[:, 3:4])
    normal[...] = unit
    mean_one = jnp.mean(scaled, axis=0, keepdims=True)
    mean_two = jnp.mean(scaled * unit, axis=0, keepdims=True)
    d_inner = c_all[...] + stats[0:1, :] * (scaled - mean_one - unit * mean_two)
    c_all[...] = d_inner
    own = take_rows(c_all, place, chans)
    inner_own[...] = own
    d_own = take_rows(d_all, place, chans)

    @pl.when(step == 0)
    def _():
        put(wo_hi, wo_lo, w_out[...])
        for total in (sum_gain, sum_bias, sum_out, sum_query):
            total[...] = jnp.zeros_like(total)

    sum_gain[...] += fold(d_own * take_rows(normal, place, chans))
    sum_bias[...] += fold(d_own)
    sum_out[...] += fold(own * live)
    branch = split(d_inner * live)
    b_hi[...], b_lo[...] = branch
    d_mixed = dot3(get(wo_hi, wo_lo), branch, NN)
    d_query = d_mixed * f_query[...]
    sum_query[...] += fold(d_query)
    put(dq_hi, dq_lo, d_query)
    d_numer = d_mixed * f_numer[...]
    put(dp_hi, dp_lo, jnp.concatenate([d_numer, -d_numer * quotient[...]], axis=0))


def mix_back_kernel(
    d_hi, d_lo, before_hi, before_lo, here_hi, here_lo, band_hi, band_lo, bias,
    kv_hi, kv_lo, d_bias, sum_value,
    carry, later, ahead,
):
    step = pl.program_id(0)
    block = pl.num_programs(0) - 1 - step
    window = TB
    chans = d_hi.shape[0] // 2

    @pl.when(step == 0)
    def _():
        for total in (carry, later, ahead, sum_value):
            total[...] = jnp.zeros_like(total)

    d_pair = get(d_hi, d_lo)
    d_wide = d_pair[0].astype(F32) + d_pair[1].astype(F32)
    into = dot3(d_pair, get(band_hi, band_lo), NN)
    back = into[:, window:] + carry[...] + later[:, 0:1]
    carry[...] = into[:, :window]
    later[...] = later[...] + ahead[...]
    ahead[...] = jnp.broadcast_to(jnp.sum(d_wide, axis=1, keepdims=True), ahead.shape)
    turned = split(d_wide.T)
    right = dot3(turned, get(here_hi, here_lo), NN)
    left = dot3(turned, get(before_hi, before_lo), NN)
    left = jnp.where(block == 0, 0.0, left)
    wide = jnp.concatenate([reverse_lanes(right), reverse_lanes(left)], axis=1)
    placed = pltpu.roll(wide, window + 1, 1, stride=1, stride_axis=0)
    d_bias[...] = placed[:, :window] * jnp.exp(bias[...])
    pair = here_hi[...].astype(F32) + here_lo[...].astype(F32)
    d_value = pair[chans:] * back[:chans]
    d_key = pair[:chans] * back[:chans] + pair[chans:] * back[chans:]
    sum_value[...] += fold(d_value)
    put(kv_hi, kv_lo, jnp.concatenate([d_key, d_value], axis=0))


def project_back_kernel(
    info, dq_hi, dq_lo, kv_hi, kv_lo, w_hi, w_lo, x0, x1, x2, x3, stats, cols, d_pair, keep, send,
    x_all, grid,
):
    place_rows(x_all, info[0], (x0, x1, x2, x3))
    d_all = (
        jnp.concatenate([dq_hi[...], kv_hi[...]], axis=0),
        jnp.concatenate([dq_lo[...], kv_lo[...]], axis=0),
    )
    terms = dot3(get(w_hi, w_lo), d_all, NN)
    grid[...] = terms
    part_halves(grid, info[0], keep, send)
    scaled = terms * cols[:, 0:1]
    unit = (x_all[...] - stats[0:1, :]) * stats[1:2, :]
    at = grid.shape[0] // 2
    sums = (jnp.sum(scaled, axis=0, keepdims=True), jnp.sum(scaled * unit, axis=0, keepdims=True))
    sums = jnp.concatenate([*sums, jnp.zeros((6, grid.shape[1]), F32)], axis=0)
    rows, window = d_pair.shape[0] // 8, d_pair.shape[1]
    for out, core in ((keep, info[4]), (send, 1 - info[4])):
        out[at : at + 8, :] = sums
        for block in range(grid.shape[1] // window):
            start = 4 * rows * core + rows * (grid.shape[1] // window * pl.program_id(0) + block)
            lanes = slice(block * window, (block + 1) * window)
            out[at + 8 :, lanes] = d_pair[pl.ds(pl.multiple_of(start, rows), rows), :]


def core_halves_kernel(info, keep, come, mine_a, send_a, mine_b, send_b):
    rows = mine_a.shape[0] - 8 - (keep.shape[1] // 16)
    chans = rows + mine_b.shape[0]
    at = 2 * chans
    for out_a, out_b, far in ((mine_a, mine_b, info[5]), (send_a, send_b, 1 - info[5])):
        here = pl.ds(pl.multiple_of(far * chans, 8), rows)
        below = pl.ds(pl.multiple_of(far * chans + rows, 8), chans - rows)
        out_a[:rows, :] = keep[here, :] + come[here, :]
        out_b[...] = keep[below, :] + come[below, :]
        out_a[rows : rows + 8, :] = keep[at : at + 8, :] + come[at : at + 8, :]
        half = keep[at + 8 :, :] + come[at + 8 :, :]
        wide = half.shape[1] // 2
        part = jnp.where(far == 0, half[:, :wide], half[:, wide:])
        tall = part.shape[0] // 2
        out_a[rows + 8 :, :wide] = part[:tall]
        out_a[rows + 8 :, wide:] = part[tall:]


def chip_sum_kernel(info, mine, come, pair, sums):
    rows = mine.shape[0] - pair.shape[0] - 8
    sums[...] = mine[rows : rows + 8, :] + come[rows : rows + 8, :]
    pair[...] = mine[rows + 8 :, :] + come[rows + 8 :, :]


def pair_small_kernel(info, pair, come, small, out):
    rows = pair.shape[0]
    out[:rows, :] = pair[...] + come[...]
    out[rows:, :] = small[...]


def pair_small_sum_kernel(info, held, come, pair, small):
    rows = pair.shape[0]
    pair[...] = held[:rows, :] + come[:rows, :]
    small[...] = held[rows:, :] + come[rows:, :]


def pair_chips_kernel(info, own, other, half):
    tall, wide = own.shape[0], own.shape[1] // 2
    for low, lanes in ((True, slice(0, wide)), (False, slice(wide, 2 * wide))):
        near = info[5] == (0 if low else 1)
        for top in range(2):
            here = slice(top * wide, (top + 1) * wide)
            half[top * tall : (top + 1) * tall, lanes] = jnp.where(near, own[:, here], other[:, here])


def pair_cores_kernel(info, own, other, d_pair):
    rows, window = own.shape[0], d_pair.shape[1]
    for half, core in ((own, info[4]), (other, 1 - info[4])):
        for block in range(4):
            start = 4 * rows * core + rows * block
            d_pair[pl.ds(pl.multiple_of(start, rows), rows), :] = half[:, block * window : (block + 1) * window]


def input_back_kernel(model, mine_a, come_a, mine_b, come_b, inner_own, x_own, stats, sums, gain, d_in, sum_gain, sum_bias):
    rows = inner_own.shape[0] - mine_b.shape[0]
    d_normed = jnp.concatenate([mine_a[:rows, :] + come_a[:rows, :], mine_b[...] + come_b[...]], axis=0)
    unit = (x_own[...] - stats[0:1, :]) * stats[1:2, :]

    @pl.when(pl.program_id(0) == 0)
    def _():
        for total in (sum_gain, sum_bias):
            total[...] = jnp.zeros_like(total)

    sum_gain[...] += fold(d_normed * unit)
    sum_bias[...] += fold(d_normed)
    d_in[...] = inner_own[...] + stats[1:2, :] * (
        d_normed * gain[...] - sums[0:1, :] / model - unit * (sums[1:2, :] / model)
    )


def swap(block, bit):
    return lax.ppermute(block, "mp", [(i, i ^ bit) for i in range(4)])


def gather_parts(own):
    far = swap(own, 2)
    near = swap(own, 1)
    return own, near, far, swap(far, 1)


def in_order(parts, place):
    stacked = jnp.stack(parts)
    return jnp.concatenate(
        [lax.dynamic_index_in_dim(stacked, place ^ i, 0, keepdims=False) for i in range(4)], axis=0
    )


def after(value, *earlier):
    return lax.optimization_barrier((value, earlier))[0]


def trade(block, flip):
    size = lax.axis_size("dp")
    return lax.ppermute(block, "dp", [(i, i ^ flip) for i in range(size)])


def glue(kernel, scalars, ins, outs, name, steps=1):
    def columns(shape):
        return pl.BlockSpec((shape[0], shape[1] // steps), lambda i: (0, i))

    return call(
        kernel, steps,
        [scalars, *[(x, columns(x.shape)) for x in ins]],
        [(shaped(shape), columns(shape)) for shape in outs],
        name=name,
        pin=False,
        pin_out=PIN_GLUE,
    )


def add_trade(block, flip, *gate):
    if lax.axis_size("dp") != 8:
        return jnp.zeros_like(block)
    return trade(after(block, *gate), flip)


def settle(sums, arrived, *gates):
    comes = [s.come for s in sums]
    comes, arrived, _ = lax.optimization_barrier((comes, arrived, gates))
    for s, come in zip(sums, comes):
        s.come = come
        if s.stage < 4:
            s.take()
    return arrived


class Sum:
    FLIPS = ((1, 2), (2, 1), (4,), (2, 1), (1, 2))

    def __init__(self, scalars, blocks, merged):
        self.merged = merged
        self.come = []
        self.scalars = scalars
        self.direct = lax.axis_size("dp") != 8
        self.stage = 0
        if self.direct:
            self.total = lax.psum(blocks, "dp")
            if merged:
                self.total = [jnp.concatenate(self.total, axis=0)]
            self.out = self.total
        else:
            self.mine, self.out = blocks[0::2], blocks[1::2]

    def send(self, *gate):
        if not self.direct:
            pairs = zip(self.out, self.FLIPS[self.stage])
            self.come = [trade(after(block, *gate), flip) for block, flip in pairs]

    def finish(self, *gate):
        if not self.direct:
            self.mine = after(self.mine, *gate)
            self.take()
        return self.total

    def take(self):
        if self.direct:
            return
        ins = [x for pair in zip(self.mine, self.come) for x in pair]
        rows, width = self.mine[0].shape
        name = f"sum_stage_{self.stage}"
        if self.stage == 0:
            half = (rows // 2, width)
            got = glue(partial(halve_kernel, (3, 2)), self.scalars, ins, [half] * 4, name, 2)
            self.mine, self.out = got[0::2], got[1::2]
        elif self.stage == 1:
            self.mine = self.out = glue(pack_kernel, self.scalars, ins, [(2 * rows, width)], name)
        elif self.stage == 2:
            self.mine = self.out = glue(unpack_kernel, self.scalars, ins, [(rows // 2, width)] * 2, name)
        elif self.stage == 3:
            kernel = partial(join_kernel, (3, 2), False)
            self.mine = self.out = glue(kernel, self.scalars, ins, [(2 * rows, width)] * 2, name)
        else:
            shapes = [(4 * rows, width)] if self.merged else [(rows, width)] * 4
            kernel = partial(join_kernel, (2, 3), True) if self.merged else projection_done_kernel
            self.out = self.total = glue(kernel, self.scalars, ins, shapes, name, 2)
        self.stage += 1


def body(
    inputs,
    lengths,
    ln1_gain,
    ln1_bias,
    w_query,
    w_key,
    w_value,
    query_bias,
    value_bias,
    pair_bias,
    w_out,
    out_bias,
    ln2_gain,
    ln2_bias,
    w_up,
    up_bias,
    w_down,
    down_bias,
    cotangent,
):
    seq_rows, span, chans = inputs.shape
    window = pair_bias.shape[1]
    model = 4 * chans
    units = w_up.shape[1]
    steps = span // WIDE
    blocks = span // TB
    assert seq_rows == 1 and window == TB
    place = lax.axis_index("mp")
    row = lax.axis_index("dp")
    halving = lax.axis_size("dp") == 8
    bits = [row % 2, (row // 2) % 2] if halving else [jnp.int32(0)] * 2
    info = jnp.stack([place.astype(jnp.int32), lengths[0], *bits, place % 2, place // 2])

    x_own = inputs[0].T
    x_far = swap(x_own, 2)
    x_near = swap(x_own, 1)
    vectors = jnp.stack([ln1_gain, ln1_bias, out_bias, ln2_gain, ln2_bias, query_bias, value_bias])
    vectors = jnp.pad(vectors, ((0, 1), (0, 256 - chans)))
    v_far = swap(vectors, 2)
    v_near = swap(vectors, 1)

    band = call(
        band_kernel, blocks,
        [(pair_bias, pl.BlockSpec((TB, window), lambda i: (i, 0)))],
        [(shaped((span, 2 * window), BF16), pl.BlockSpec((TB, 2 * window), lambda i: (i, 0)))] * 2,
        name="band",
    )
    wide_qkv, tall_qkv = (3 * chans, model), (model, 3 * chans)
    up_dims, down_dims = (model, units), (units, model)

    def prepare(kernel, ins, dims, name):
        return call(
            kernel, 1, [(w, whole(w.shape)) for w in ins], [(shaped(d, BF16), whole(d)) for d in dims for _ in range(2)], name=name
        )

    wq_hi, wq_lo, wqt_hi, wqt_lo = prepare(
        qkv_weights_kernel, [w_query.T, w_key.T, w_value.T], [wide_qkv, tall_qkv], "qkv_weights"
    )
    wu_hi, wu_lo, wut_hi, wut_lo = prepare(weights_kernel, [w_up], [up_dims, down_dims], "up_weights")
    up_column, gain_column = up_bias[:, None], ln1_gain[:, None]
    v_far, x_far, up_column, gain_column = lax.optimization_barrier(
        (v_far, x_far, up_column, gain_column, band, wq_hi, wu_hi)
    )[:4]
    x_parts = (x_own, x_near, x_far, swap(x_far, 1))
    v_parts = (vectors, v_near, v_far, swap(v_far, 1))
    wo_own = after(w_out, x_far, v_far)
    wo_far = swap(wo_own, 2)
    wo_near = swap(w_out, 1)

    thin = (shaped((chans, span)), across(chans))
    tall_half = (shaped((model, span), BF16), across(model))
    hid_half = (shaped((units, span), BF16), across(units))
    pair_half = (shaped((2 * chans, span), BF16), across(2 * chans))
    thin_half = (shaped((chans, span), BF16), across(chans))
    rows8 = (shaped((8, span)), across(8))
    x_ins = [(x, across(chans)) for x in x_parts]
    scalars = (info, SCALARS)

    cols_out = (shaped((model, 8)), whole((model, 8)))
    cols, mixed, quotient, f_query, f_numer, pair_hi, pair_lo, n1_hi, n1_lo, stats_one = call(
        attend_kernel, steps,
        [scalars, *x_ins, *[(v, whole((8, 256))) for v in v_parts], (wq_hi, whole(wide_qkv)), (wq_lo, whole(wide_qkv))]
        + [(b, pl.BlockSpec((WIDE, 2 * window), lambda i: (i, 0))) for b in band],
        [cols_out, thin, thin, thin, thin, pair_half, pair_half, tall_half, tall_half, rows8],
        [
            pltpu.VMEM((model, WIDE), F32),
            pltpu.VMEM((2 * chans, 128), F32),
            pltpu.VMEM((2 * chans, TB), BF16),
            pltpu.VMEM((2 * chans, TB), BF16),
        ],
        name="attend",
        pin=PIN_ATT,
    )

    cols_in = (cols, whole((model, 8)))
    mixed_far = swap(mixed, 2)
    mixed_near = swap(mixed, 1)
    wo_parts = (w_out, wo_near, wo_far, swap(wo_far, 1))
    wot_hi, wot_lo = prepare(out_weights_kernel, wo_parts, [(model, model)], "out_weights")
    wd_hi, wd_lo, wdt_hi, wdt_lo = prepare(weights_kernel, [w_down], [down_dims, up_dims], "down_weights")
    mixed_far = after(mixed_far, wot_hi, wd_hi)
    mixed_parts = (mixed, mixed_near, mixed_far, swap(mixed_far, 1))
    cot_own = cotangent[0].T
    cot_far = swap(after(cot_own, mixed_far), 2)
    cot_near = swap(cot_own, 1)
    lanes_own = (shaped((chans, 128)), whole((chans, 128)))

    act_hi, act_lo, slope, n2_hi, n2_lo, inner_own, stats_two = call(
        hidden_kernel, steps,
        [scalars, *[(p, across(chans)) for p in mixed_parts], *x_ins, cols_in]
        + [(wot_hi, whole((model, model))), (wot_lo, whole((model, model)))]
        + [(wut_hi, whole(down_dims)), (wut_lo, whole(down_dims)), (up_column, whole((units, 1)))],
        [hid_half, hid_half, (shaped((units, span)), across(units)), tall_half, tall_half, thin, rows8],
        [pltpu.VMEM((model, WIDE), F32)],
        name="hidden",
        pin=PIN_HIN,
        pin_out=PIN_HID,
    )

    cot_far = after(cot_far, act_hi)
    cot_parts = (cot_own, cot_near, cot_far, swap(cot_far, 1))
    cot_ins = [(c, across(chans)) for c in cot_parts]
    def outer(a_hi, a_lo, b_hi, b_lo, name, steps=2):
        rows, inner_len = a_hi.shape
        deep = b_hi.shape[0]
        left = whole((rows, inner_len))
        right = pl.BlockSpec((deep // steps, inner_len), lambda i: (i, 0))
        part = (shaped((rows // 4, deep)), across(rows // 4, deep // steps))
        grads = call(
            outer_kernel, steps,
            [scalars, (a_hi, left), (a_lo, left), (b_hi, right), (b_lo, right)],
            [part] * 4,
            [pltpu.VMEM((rows, inner_len), BF16)] * 2,
            name=name,
            pin=PIN_UG,
            pin_out=PIN_GO,
        )
        return Sum(scalars, grads, True)

    whole_half = (shaped((model, span), BF16), whole((model, span)))
    block = (shaped((units // 4, model)), whole((units // 4, model)))
    *grads, c_hi, c_lo, s_down = call(
        down_grad_kernel, 1,
        [scalars, (act_hi, whole((units, span))), (act_lo, whole((units, span))), *[(c, whole((chans, span))) for c in cot_parts]],
        [block] * 4 + [whole_half, whole_half, lanes_own],
        [pltpu.VMEM((units, span), BF16)] * 2 + [pltpu.VMEM((model, span), F32)],
        name="down_grad",
        pin=PIN_DG,
        pin_out=PIN_GO,
    )
    g_down = Sum(scalars, grads, True)
    g_down.send()
    c_hi, c_lo = after((c_hi, c_lo), g_down.out)
    half_out = (shaped((2 * chans, span)), across(2 * chans))
    half_shape = (2 * chans, span)
    dpre_hi, dpre_lo, keep, send, s_up = call(
        hidden_back_kernel, steps,
        [scalars, (c_hi, across(model)), (c_lo, across(model)), (wd_hi, whole(down_dims)), (wd_lo, whole(down_dims))]
        + [(slope, across(units)), (wu_hi, whole(up_dims)), (wu_lo, whole(up_dims))],
        [hid_half, hid_half, half_out, half_out, (shaped((units, 128)), whole((units, 128)))],
        [pltpu.VMEM((model, WIDE), F32)],
        name="hidden_back",
        pin=PIN_HB,
        pin_out=PIN_MID,
    )
    send = settle([g_down], send, keep)
    half = glue(add_kernel, scalars, [keep, swap(after(send, g_down.out), 1)], [half_shape], "core_sum", 2)[0]
    half_far = swap(half, 2)
    g_down.send(half)
    g_up = outer(after(n2_hi, half), n2_lo, dpre_hi, dpre_lo, "up_grad")
    settle([g_down], [], g_up.out)
    g_down.send()
    g_up.send(g_down.out)
    keep_down, send_down = call(
        down_kernel, steps,
        [scalars, (wdt_hi, whole(up_dims)), (wdt_lo, whole(up_dims)), (after(act_hi, g_down.out), across(units)), (act_lo, across(units))],
        [half_out, half_out],
        [pltpu.VMEM((model, WIDE), F32)],
        name="down",
        pin=False,
        pin_out=PIN_MID,
    )
    half_far, send_down = settle([g_down, g_up], (half_far, send_down), keep_down)
    half = glue(add_kernel, scalars, [half, half_far], [half_shape], "chip_sum", 2)[0]
    other, g_down.out, g_up.out = lax.optimization_barrier((swap(half, 1), g_down.out, g_up.out))
    own_shape = (chans, span)
    g_down.send(other)
    g_up.send(other)
    core_down = swap(after(send_down, other), 1)

    b_hi, b_lo, dq_hi, dq_lo, dp_hi, dp_lo, d_inner_own, s_gain2, s_bias2, s_out, s_query = call(
        inner_back_kernel, steps,
        [scalars, (half, across(2 * chans)), (other, across(2 * chans)), (n2_hi, across(model)), (n2_lo, across(model)), (stats_two, across(8)), cols_in]
        + cot_ins
        + [(w_out, whole((chans, model)))]
        + [(f_query, across(chans)), (f_numer, across(chans)), (quotient, across(chans))],
        [tall_half, tall_half, thin_half, thin_half, pair_half, pair_half, thin, lanes_own, lanes_own, lanes_own, lanes_own],
        [pltpu.VMEM((model, WIDE), F32)] * 3 + [pltpu.VMEM((chans, model), BF16)] * 2,
        name="inner_back",
        pin=PIN_IB,
        pin_out=PIN_MID,
    )
    dp_hi, core_down = settle([g_down, g_up], (dp_hi, core_down), b_hi)
    mine_down, send_down = glue(
        partial(halve_kernel, (5,)), scalars, [keep_down, core_down], [own_shape] * 2, "down_halves", 2
    )
    g_down.send()
    g_up.send()
    come_down = swap(after(send_down, g_down.out, g_up.out), 2)
    dp_hi = after(dp_hi, g_down.out, g_up.out)
    thin_all, tall_all = whole((chans, span)), whole((model, span))

    def back_at(i):
        return blocks - 1 - i

    pair_spec = pl.BlockSpec((2 * chans, TB), lambda i: (0, back_at(i)))
    prev_spec = pl.BlockSpec((2 * chans, TB), lambda i: (0, jnp.maximum(back_at(i) - 1, 0)))
    band_spec = pl.BlockSpec((TB, 2 * window), lambda i: (back_at(i), 0))
    row_spec = pl.BlockSpec((TB, window), lambda i: (back_at(i), 0))
    kv_hi, kv_lo, d_pair, s_value = call(
        mix_back_kernel, blocks,
        [(dp_hi, pair_spec), (dp_lo, pair_spec), (pair_hi, prev_spec), (pair_lo, prev_spec), (pair_hi, pair_spec), (pair_lo, pair_spec)]
        + [(band[0], band_spec), (band[1], band_spec), (pair_bias, row_spec)],
        [(shaped((2 * chans, span), BF16), pair_spec)] * 2 + [(shaped((span, window)), row_spec), lanes_own],
        [pltpu.VMEM((2 * chans, TB), F32), pltpu.VMEM((2 * chans, 128), F32), pltpu.VMEM((2 * chans, 128), F32)],
        name="mix_back",
        pin=PIN_MB,
        pin_out=PIN_MID,
    )
    slab = pl.BlockSpec((model // 2, span), lambda i: (i, 0))
    grads = call(
        projection_grads_kernel, 2,
        [scalars, (mixed, thin_all), (b_hi, slab), (b_lo, slab), (dq_hi, thin_all), (dq_lo, thin_all)]
        + [(kv_hi, whole((2 * chans, span))), (kv_lo, whole((2 * chans, span))), (n1_hi, slab), (n1_lo, slab)],
        [(shaped((chans, model)), across(chans, model // 2))] * 4,
        name="projection_grads", pin=PIN_PG, pin_out=PIN_GO,
    )
    g_mix = Sum(scalars, grads, False)
    dq_hi, kv_hi = after((dq_hi, kv_hi), grads)
    payload_rows = 2 * chans + 8 + span // 8
    payload = (shaped((payload_rows, span)), across(payload_rows))
    keep, send = call(
        project_back_kernel, steps,
        [scalars, (dq_hi, across(chans)), (dq_lo, across(chans)), (kv_hi, across(2 * chans)), (kv_lo, across(2 * chans))]
        + [(wqt_hi, whole(tall_qkv)), (wqt_lo, whole(tall_qkv)), *x_ins, (stats_one, across(8)), cols_in, (d_pair, whole((span, window)))],
        [payload, payload],
        [pltpu.VMEM((model, WIDE), F32)] * 2,
        name="project_back",
        pin=PIN_PB,
        pin_out=PIN_MID,
    )
    send, come_down = settle([g_down, g_up], (send, come_down), keep, grads)
    g_up.send(send)
    come = settle([g_up], swap(after(send, g_up.out), 1))
    first_rows = FIRST_ROWS
    rest_shape = (chans - first_rows, span)
    mine, send, mine_rest, send_rest = glue(
        core_halves_kernel, scalars, [keep, come], [(first_rows + 8 + span // 16, span)] * 2 + [rest_shape] * 2, "core_halves"
    )
    send = after(send, send_rest)
    g_mix.send(send)
    come, g_up.out = settle([g_mix], (swap(send, 2), g_up.out))
    quarter = (span // 16, span)
    pair_sum, sums = glue(chip_sum_kernel, scalars, [mine, come], [quarter, (8, span)], "chip_sums")
    come, sums, pair_sum = after((come, sums, pair_sum), g_mix.out)
    come, sums, pair_sum = lax.optimization_barrier((come, sums, pair_sum))
    g_mix.send(pair_sum)
    come_rest, pair_come = settle([g_mix], (swap(after(send_rest, pair_sum), 2), add_trade(pair_sum, 4)))
    pair_sum = glue(add_kernel, scalars, [pair_sum, pair_come], [quarter], "pair_far")[0]
    pair_sum, come_rest = after((pair_sum, come_rest), g_mix.out)
    g_mix.send(pair_sum)
    g_up.send(pair_sum)
    d_inputs, s_gain1, s_bias1 = call(
        partial(input_back_kernel, float(model)), steps,
        [(x, across(x.shape[0])) for x in (mine, come, mine_rest, come_rest, d_inner_own, x_own, stats_one, sums)]
        + [(gain_column, whole((chans, 1)))],
        [thin, lanes_own, lanes_own],
        name="input_back",
        pin=False,
        pin_out=PIN_MID,
    )
    lanes = (s_gain1, s_bias1, s_query, s_value, s_out, s_gain2, s_bias2, s_down, s_up)
    count = sum(x.shape[0] for x in lanes)
    small = call(
        lane_sums_kernel, 1, [(x, whole(x.shape)) for x in lanes], [(shaped((8, span)), whole((8, span)))],
        name="lane_sums", pin=False,
    )[0]
    sum_down = g_down.finish(pair_sum)[0]
    live = (jnp.arange(span, dtype=jnp.int32) < lengths[0]).astype(F32)[None, :]
    result = inner_own + live * (mine_down + after(come_down, pair_sum) + down_bias[:, None])
    pair_come, small, sum_down, result = settle([g_mix, g_up], (add_trade(pair_sum, 1), small, sum_down, result))
    packed = (span // 16 + 8, span)
    packed_sum = glue(pair_small_kernel, scalars, [pair_sum, pair_come, small], [packed], "pair_x")[0]
    packed_sum = after(packed_sum, g_mix.out)
    g_mix.send(packed_sum)
    come = settle([g_mix], add_trade(packed_sum, 2))
    pair_sum, small = glue(pair_small_sum_kernel, scalars, [packed_sum, come], [quarter, (8, span)], "pair_z")
    small, pair_sum = after((small, pair_sum), g_mix.out)
    g_mix.send(small, pair_sum)
    sum_up = g_up.finish(small)[0]
    small_come, pair_come, sum_up = settle([g_mix], (add_trade(small, 4), swap(pair_sum, 2), sum_up))
    pair_half = glue(pair_chips_kernel, scalars, [pair_sum, pair_come], [(span // 8, span)], "pair_chips")[0]
    small = glue(add_kernel, scalars, [small, small_come], [(8, span)], "small_far")[0]
    small, pair_half = lax.optimization_barrier((small, pair_half))
    pair_come = swap(pair_half, 1)
    small = (small + add_trade(small, 1)).reshape(-1)[:count]
    d_w_out, d_w_query, d_w_key, d_w_value = g_mix.finish(pair_half)
    d_pair = glue(pair_cores_kernel, scalars, [pair_half, pair_come], [(span, window)], "pair_cores")[0]
    if not halving:
        d_pair = lax.psum(d_pair, "dp")
        small = lax.psum(small, "dp")
    vecs = [small[i * chans : (i + 1) * chans] for i in range(8)]
    return (
        result.T[None],
        d_inputs.T[None],
        vecs[0],
        vecs[1],
        d_w_query.T,
        d_w_key.T,
        d_w_value.T,
        vecs[2],
        vecs[3],
        d_pair,
        d_w_out,
        vecs[4],
        vecs[5],
        vecs[6],
        sum_up,
        small[8 * chans :],
        sum_down,
        vecs[7],
    )


def solution(mesh):
    rows = P("dp", None, "mp")
    vec = P("mp")
    out_dim = P(None, "mp")
    in_dim = P("mp", None)
    return jax.shard_map(
        body,
        mesh=mesh,
        in_specs=(
            rows, P("dp"), vec, vec, out_dim, out_dim, out_dim, vec, vec, P(), in_dim, vec, vec, vec,
            out_dim, vec, in_dim, vec, rows,
        ),
        out_specs=(
            rows, rows, vec, vec, out_dim, out_dim, out_dim, vec, vec, P(), in_dim, vec, vec, vec,
            out_dim, vec, in_dim, vec,
        ),
        check_vma=False,
    )
```
